256 devices in a mesh: blk: 64 (over x, y_lo, z), rep: 4 (over y_hi, core).
Axes of the slice: x: 4, y: 4 (y_hi: 2, y_lo: 2; y = y_hi * 2 + y_lo), z: 8, core: 2. Of those that a mesh axis runs over, the one named last changes fastest.
Arguments:
- node_feats: bfloat16 [131072, 128], P(('blk', 'rep')), may hold values from -6 to 6
- adj_tiles: bfloat16 [1024, 4, 4, 128, 128], P('blk', 'rep'), as said below
- col_index: int32 [1024, 4, 4], P('blk', 'rep'), may hold values from 0 to 255, as said below
- w_in: bfloat16 [128, 512], replicated, may hold values from -0.5 to 0.5
- b_in: float32 [512], replicated, may hold values from -3 to 3
- w_out: bfloat16 [512, 128], replicated, may hold values from -0.25 to 0.25
- b_out: float32 [128], replicated, may hold values from -3 to 3
- cot_out: bfloat16 [131072, 128], P(('blk', 'rep')), may hold values from -6 to 6
Outputs:
- out_feats: bfloat16 [131072, 128], P(('blk', 'rep'))
- grad_feats: bfloat16 [131072, 128], P(('blk', 'rep'))
The draws below stay inside these ranges and needn't reach their ends.
Inputs may be any that keep to these rules, and one draw needn't show every extreme that they name: The matrix A described by adj_tiles and col_index is symmetric (A equals its transpose). `col_index`: column block numbers within a quarter.
All inputs are finite; a program needn't handle non-finite values.
Results may differ from the reference program's by a relative error of at most 0.0045.
Values may be sent and summed in bfloat16 or wider, within the bound.
A program may use at most 128 MiB of HBM per device.

```python
import jax
import jax.numpy as jnp
from jax import lax

WIDTH = 128
MLP_UNITS = 512
BLOCK = 128
KQ = 4
ROWS_DEV = 2048
NODES = 131072
NBLOCKS = 1024
N_BLK = 64


def pairing(key):
    half = KQ // 2
    quarter_blocks = NODES // (4 * BLOCK)
    per_shard = ROWS_DEV // (4 * BLOCK)
    keys = jax.random.split(jax.random.fold_in(key, 11), half * 16)
    perms = jax.vmap(lambda one_key: jax.random.permutation(one_key, quarter_blocks))(keys)
    perms = perms.reshape(half, 4, 4, quarter_blocks).astype(jnp.int32)
    inverse = jnp.argsort(perms, axis=-1, stable=True).astype(jnp.int32)
    rows = jnp.arange(NBLOCKS, dtype=jnp.int32)
    own_quarter = rows // per_shard % 4
    position = rows // (4 * per_shard) * per_shard + rows % per_shard
    quarters = jnp.arange(4, dtype=jnp.int32)
    forward = perms[:, own_quarter[:, None], quarters[None, :], position[:, None]]
    backward = inverse[:, quarters[None, :], own_quarter[:, None], position[:, None]]
    forward = jnp.transpose(forward, (1, 2, 0))
    backward = jnp.transpose(backward, (1, 2, 0))
    source = backward // per_shard * 4 * per_shard + quarters[None, :, None] * per_shard + backward % per_shard
    columns = jnp.concatenate([forward, backward], axis=-1).astype(jnp.int32)
    return (columns, source.astype(jnp.int32), own_quarter)


def draw_col_index(key, part):
    columns, source, own_quarter = pairing(key)
    return columns


def draw_adj_tiles(key, part):
    columns, source, own_quarter = pairing(key)
    half = KQ // 2
    scale = (BLOCK * 4 * KQ) ** (-0.5)
    shape = (NBLOCKS, 4, half, BLOCK, BLOCK)
    base = jax.random.normal(jax.random.fold_in(key, 12), shape, jnp.float32) * scale
    slots = jnp.arange(half, dtype=jnp.int32)
    mirrored = base[source, own_quarter[:, None, None], slots[None, None, :]]
    mirrored = jnp.swapaxes(mirrored, -1, -2)
    return jnp.concatenate([base, mirrored], axis=2).astype(jnp.bfloat16)


def level_of(key, shape, cuts, low, top_value):
    factor_of = 1.0
    for axis_at, blocks in cuts:
        heights = jax.random.uniform(jax.random.fold_in(jax.random.fold_in(key, 6), axis_at), (blocks,), jnp.float32, low / len(cuts), top_value / len(cuts))
        factor_of = factor_of * jnp.repeat(jnp.exp(heights), shape[axis_at] // blocks).reshape((-1,) + (1,) * (len(shape) - 1 - axis_at))
    return factor_of


def normal_values(own_key, shape, deviation, most, cuts=(), kind=jnp.bfloat16):
    factor_of = level_of(own_key, shape, cuts, -0.22, 0.18) if cuts else 1.0
    array = jax.random.normal(own_key, shape, jnp.float32) * deviation * factor_of
    return jnp.minimum(jnp.maximum(array, -most), most).astype(kind)


def setup_inputs(seed: int = 0) -> dict:
    arg_keys = jax.random.split(jax.random.key(seed), 9)
    return {
        "node_feats": normal_values(arg_keys[0], (NODES, WIDTH), 1.0, 6.0, ((0, 256),)),
        "adj_tiles": draw_adj_tiles(jax.random.fold_in(arg_keys[8], 71), 0),
        "col_index": draw_col_index(jax.random.fold_in(arg_keys[8], 71), 0),
        "w_in": normal_values(arg_keys[3], (WIDTH, MLP_UNITS), WIDTH ** -0.5, 0.5),
        "b_in": normal_values(arg_keys[4], (MLP_UNITS,), 0.5, 3.0, (), jnp.float32),
        "w_out": normal_values(arg_keys[5], (MLP_UNITS, WIDTH), MLP_UNITS ** -0.5, 0.25),
        "b_out": normal_values(arg_keys[6], (WIDTH,), 0.5, 3.0, (), jnp.float32),
        "cot_out": normal_values(arg_keys[7], (NODES, WIDTH), 1.0, 6.0, ((0, 256),)),
    }


def quarter_panel(feats, quarter):
    return feats.reshape(N_BLK, 4, ROWS_DEV // 4, WIDTH)[:, quarter].reshape(-1, BLOCK, WIDTH)


def aggregate(feats, adj_tiles, col_index):
    def one_quarter(quarter):
        grouped = quarter_panel(feats, quarter)
        picked = grouped[col_index[:, quarter, :]].astype(jnp.float32)
        tiles_here = adj_tiles[:, quarter].astype(jnp.float32)
        return jnp.einsum("gkij,gkjh->gih", tiles_here, picked)

    parts = lax.map(one_quarter, jnp.arange(4, dtype=jnp.int32))
    return jnp.sum(parts, axis=0).reshape(NODES, WIDTH)


def adjoint(grads, adj_tiles, col_index):
    blocks = grads.reshape(NBLOCKS, BLOCK, WIDTH).astype(jnp.float32)

    def one_quarter(quarter):
        tiles_here = adj_tiles[:, quarter].astype(jnp.float32)
        contrib = jnp.einsum("gkij,gih->gkjh", tiles_here, blocks)
        return jax.ops.segment_sum(contrib.reshape(-1, BLOCK, WIDTH), col_index[:, quarter, :].reshape(-1), num_segments=NODES // (4 * BLOCK))

    parts = lax.map(one_quarter, jnp.arange(4, dtype=jnp.int32))
    parts = parts.reshape(4, N_BLK, ROWS_DEV // 4, WIDTH)
    return jnp.transpose(parts, (1, 0, 2, 3)).reshape(NODES, WIDTH)


def reference(node_feats, adj_tiles, col_index, w_in, b_in, w_out, b_out, cot_out):
    agg = aggregate(node_feats, adj_tiles, col_index)
    agg_b = agg.astype(jnp.bfloat16)
    pre = jnp.dot(agg_b, w_in, preferred_element_type=jnp.float32) + b_in
    hidden = jax.nn.silu(pre).astype(jnp.bfloat16)
    projected = jnp.dot(hidden, w_out, preferred_element_type=jnp.float32) + b_out
    out_feats = (node_feats.astype(jnp.float32) + projected).astype(jnp.bfloat16)
    g_hidden = jnp.dot(cot_out, w_out.T, preferred_element_type=jnp.float32)
    sigma = jax.nn.sigmoid(pre)
    g_pre = (g_hidden * sigma * (1.0 + pre * (1.0 - sigma))).astype(jnp.bfloat16)
    g_agg = jnp.dot(g_pre, w_in.T, preferred_element_type=jnp.float32).astype(jnp.bfloat16)
    back_rows = adjoint(g_agg, adj_tiles, col_index)
    grad_feats = (cot_out.astype(jnp.float32) + back_rows).astype(jnp.bfloat16)
    return (out_feats, grad_feats)
```

```python
import jax
import jax.numpy as jnp
from jax import lax
from jax.sharding import Mesh
from jax.sharding import PartitionSpec as P

BLOCK = 128
NAMES = ("x", "ylo", "z", "yhi", "core")
BLK = ("x", "ylo", "z")
REP = ("yhi", "core")


def gather_blk(rows):
    part = lax.all_gather(rows, "ylo", axis=0, tiled=False)
    part = lax.all_gather(part, "x", axis=0, tiled=False)
    part = lax.all_gather(part, "z", axis=0, tiled=False)
    return part.reshape(-1, BLOCK, rows.shape[1])


def staged_index(col, per_owner):
    nz = lax.axis_size("z")
    nylo = lax.axis_size("ylo")
    nx = lax.axis_size("x")
    owner = col // per_owner
    sub = col % per_owner
    z = owner % nz
    ylo = (owner // nz) % nylo
    x = owner // (nz * nylo)
    return ((z * nx + x) * nylo + ylo) * per_owner + sub


def tile_products(grouped, adj_tiles, index):
    picked = grouped[index]
    summed = jnp.einsum(
        "rkij,rkjh->rih", adj_tiles[:, 0], picked, preferred_element_type=jnp.float32
    )
    return summed.reshape(-1, grouped.shape[2])


def local(node_feats, adj_tiles, col_index, w_in, b_in, w_out, b_out, cot_out):
    per_owner = node_feats.shape[0] // BLOCK
    index = staged_index(col_index[:, 0, :], per_owner)
    panels = gather_blk(node_feats)
    partial_sum = tile_products(panels, adj_tiles, index)
    agg = lax.psum_scatter(partial_sum, REP, scatter_dimension=0, tiled=True)
    agg_b = agg.astype(jnp.bfloat16)
    pre = jnp.dot(agg_b, w_in, preferred_element_type=jnp.float32) + b_in
    hidden = jax.nn.silu(pre).astype(jnp.bfloat16)
    projected = jnp.dot(hidden, w_out, preferred_element_type=jnp.float32) + b_out
    out_feats = (node_feats.astype(jnp.float32) + projected).astype(jnp.bfloat16)
    g_hidden = jnp.einsum("nh,fh->nf", cot_out, w_out, preferred_element_type=jnp.float32)
    sigma = jax.nn.sigmoid(pre)
    g_pre = (g_hidden * sigma * (1.0 + pre * (1.0 - sigma))).astype(jnp.bfloat16)
    g_agg = jnp.einsum("nf,hf->nh", g_pre, w_in, preferred_element_type=jnp.float32).astype(
        jnp.bfloat16
    )
    g_panels = gather_blk(g_agg)
    back_partial = tile_products(g_panels, adj_tiles, index)
    back_rows = lax.psum_scatter(back_partial, REP, scatter_dimension=0, tiled=True)
    grad_feats = (cot_out.astype(jnp.float32) + back_rows).astype(jnp.bfloat16)
    return (out_feats, grad_feats)


def solution(mesh):
    nblk = mesh.shape["blk"]
    nrep = mesh.shape["rep"]
    fine = Mesh(mesh.devices.reshape(nblk // 16, 2, 8, nrep // 2, 2), NAMES)
    rows = P(BLK + REP, None)
    placed = (
        rows,
        P(BLK, REP, None, None, None),
        P(BLK, REP, None),
        P(),
        P(),
        P(),
        P(),
        rows,
    )
    return jax.shard_map(
        local,
        mesh=fine,
        in_specs=placed,
        out_specs=(rows, rows),
        check_vma=False,
    )
```

```python
import functools

import jax
import jax.numpy as jnp
from jax import lax
from jax.experimental import pallas as pl
from jax.experimental.pallas import tpu as pltpu
from jax.sharding import Mesh
from jax.sharding import PartitionSpec as P

BLOCK = 128
NAMES = ("x", "ylo", "z", "yhi", "core")
BLK = ("x", "ylo", "z")
REP = ("yhi", "core")


def group_place(axes):
    sizes = [lax.axis_size(a) for a in axes]
    me = 0
    for a, n in zip(axes, sizes):
        me = me * n + lax.axis_index(a)
    return me, sizes


def peer_id(axes, sizes, p):
    coords = {}
    for a, n in reversed(list(zip(axes, sizes))):
        coords[a] = p % n
        p = p // n
    return coords


def exchange_kernel(axes, gather, src_ref, out_ref, send_sem, recv_sem, local_sem):
    me, sizes = group_place(axes)
    n = out_ref.shape[0]
    barrier = pltpu.get_barrier_semaphore()
    for d in range(1, n):
        p = lax.rem(me + d, n)
        pl.semaphore_signal(barrier, 1, device_id=peer_id(axes, sizes, p))
    pl.semaphore_wait(barrier, n - 1)
    copies = []
    for d in range(1, n):
        p = lax.rem(me + d, n)
        copy = pltpu.make_async_remote_copy(
            src_ref=src_ref if gather else src_ref.at[p],
            dst_ref=out_ref.at[me],
            send_sem=send_sem.at[d],
            recv_sem=recv_sem.at[d],
            device_id=peer_id(axes, sizes, p),
        )
        copy.start()
        copies.append(copy)
    own = pltpu.make_async_copy(src_ref if gather else src_ref.at[me], out_ref.at[me], local_sem)
    own.start()
    for copy in copies:
        copy.wait()
    own.wait()


def group_exchange(src, axes, gather, cid):
    n = 1
    for a in axes:
        n *= lax.axis_size(a)
    block = src.shape if gather else src.shape[1:]
    return pl.pallas_call(
        functools.partial(exchange_kernel, axes, gather),
        out_shape=jax.ShapeDtypeStruct((n, *block), src.dtype),
        in_specs=[pl.BlockSpec(memory_space=pl.ANY)],
        out_specs=pl.BlockSpec(memory_space=pl.ANY),
        scratch_shapes=[
            pltpu.SemaphoreType.DMA((n,)),
            pltpu.SemaphoreType.DMA((n,)),
            pltpu.SemaphoreType.DMA,
        ],
        compiler_params=pltpu.CompilerParams(collective_id=cid, has_side_effects=True),
    )(src)


def gather_blk(rows, cid):
    part = group_exchange(rows, ("x", "ylo"), True, cid)
    part = lax.all_gather(part, "z", axis=0, tiled=False)
    return part.reshape(-1, BLOCK, rows.shape[1])


def reduce_rep(partial, cid):
    nrep = lax.axis_size("yhi") * lax.axis_size("core")
    pieces = partial.reshape(nrep, -1, partial.shape[1])
    return jnp.sum(group_exchange(pieces, REP, False, cid), axis=0)


def staged_index(col, per_owner):
    nz = lax.axis_size("z")
    nxy = lax.axis_size("x") * lax.axis_size("ylo")
    owner = col // per_owner
    sub = col % per_owner
    return ((owner % nz) * nxy + owner // nz) * per_owner + sub


def tile_products(grouped, adj_tiles, index):
    picked = grouped[index]
    summed = jnp.einsum(
        "rkij,rkjh->rih", adj_tiles[:, 0], picked, preferred_element_type=jnp.float32
    )
    return summed.reshape(-1, grouped.shape[2])


def local(node_feats, adj_tiles, col_index, w_in, b_in, w_out, b_out, cot_out):
    per_owner = node_feats.shape[0] // BLOCK
    index = staged_index(col_index[:, 0, :], per_owner)
    panels = gather_blk(node_feats, 0)
    partial_sum = tile_products(panels, adj_tiles, index)
    agg = reduce_rep(partial_sum, 2)
    agg_b = agg.astype(jnp.bfloat16)
    pre = jnp.dot(agg_b, w_in, preferred_element_type=jnp.float32) + b_in
    hidden = jax.nn.silu(pre).astype(jnp.bfloat16)
    projected = jnp.dot(hidden, w_out, preferred_element_type=jnp.float32) + b_out
    out_feats = (node_feats.astype(jnp.float32) + projected).astype(jnp.bfloat16)
    g_hidden = jnp.einsum("nh,fh->nf", cot_out, w_out, preferred_element_type=jnp.float32)
    sigma = jax.nn.sigmoid(pre)
    g_pre = (g_hidden * sigma * (1.0 + pre * (1.0 - sigma))).astype(jnp.bfloat16)
    g_agg = jnp.einsum("nf,hf->nh", g_pre, w_in, preferred_element_type=jnp.float32).astype(
        jnp.bfloat16
    )
    g_panels = gather_blk(g_agg, 1)
    back_partial = tile_products(g_panels, adj_tiles, index)
    back_rows = reduce_rep(back_partial, 3)
    grad_feats = (cot_out.astype(jnp.float32) + back_rows).astype(jnp.bfloat16)
    return (out_feats, grad_feats)


def solution(mesh):
    nblk = mesh.shape["blk"]
    nrep = mesh.shape["rep"]
    fine = Mesh(mesh.devices.reshape(nblk // 16, 2, 8, nrep // 2, 2), NAMES)
    rows = P(BLK + REP, None)
    placed = (
        rows,
        P(BLK, REP, None, None, None),
        P(BLK, REP, None),
        P(),
        P(),
        P(),
        P(),
        rows,
    )
    return jax.shard_map(
        local,
        mesh=fine,
        in_specs=placed,
        out_specs=(rows, rows),
        check_vma=False,
    )
```

```python
import functools

import jax
import jax.numpy as jnp
from jax import lax
from jax.experimental import pallas as pl
from jax.experimental.pallas import tpu as pltpu
from jax.sharding import Mesh
from jax.sharding import PartitionSpec as P

BLOCK = 128
NAMES = ("x", "ylo", "z", "yhi", "core")
BLK = ("x", "ylo", "z")
REP = ("yhi", "core")


def group_place(axes):
    sizes = [lax.axis_size(a) for a in axes]
    me = 0
    for a, n in zip(axes, sizes):
        me = me * n + lax.axis_index(a)
    return me, sizes


def peer_id(axes, sizes, p):
    coords = {}
    for a, n in reversed(list(zip(axes, sizes))):
        coords[a] = p % n
        p = p // n
    return coords


def exchange_kernel(axes, gather, src_ref, out_ref, send_sem, recv_sem, local_sem):
    me, sizes = group_place(axes)
    n = out_ref.shape[0]
    barrier = pltpu.get_barrier_semaphore()
    for d in range(1, n):
        p = lax.rem(me + d, n)
        pl.semaphore_signal(barrier, 1, device_id=peer_id(axes, sizes, p))
    pl.semaphore_wait(barrier, n - 1)
    copies = []
    for d in range(1, n):
        p = lax.rem(me + d, n)
        copy = pltpu.make_async_remote_copy(
            src_ref=src_ref if gather else src_ref.at[p],
            dst_ref=out_ref.at[me],
            send_sem=send_sem.at[d],
            recv_sem=recv_sem.at[d],
            device_id=peer_id(axes, sizes, p),
        )
        copy.start()
        copies.append(copy)
    own = pltpu.make_async_copy(src_ref if gather else src_ref.at[me], out_ref.at[me], local_sem)
    own.start()
    for copy in copies:
        copy.wait()
    own.wait()


def group_exchange(src, axes, gather, cid):
    n = 1
    for a in axes:
        n *= lax.axis_size(a)
    block = src.shape if gather else src.shape[1:]
    return pl.pallas_call(
        functools.partial(exchange_kernel, axes, gather),
        out_shape=jax.ShapeDtypeStruct((n, *block), src.dtype),
        in_specs=[pl.BlockSpec(memory_space=pl.ANY)],
        out_specs=pl.BlockSpec(memory_space=pl.ANY),
        scratch_shapes=[
            pltpu.SemaphoreType.DMA((n,)),
            pltpu.SemaphoreType.DMA((n,)),
            pltpu.SemaphoreType.DMA,
        ],
        compiler_params=pltpu.CompilerParams(collective_id=cid, has_side_effects=True),
    )(src)


def gather_blk(rows, cid):
    half = rows.shape[0] // 2
    first = group_exchange(rows[:half], ("x", "ylo"), True, cid)
    first = lax.all_gather(first, "z", axis=0, tiled=False)
    second = lax.all_gather(rows[half:], "z", axis=0, tiled=False)
    second = group_exchange(second, ("x", "ylo"), True, cid + 4)
    width = rows.shape[1]
    return first.reshape(-1, BLOCK, width), second.reshape(-1, BLOCK, width)


def reduce_rep(partial, cid):
    nrep = lax.axis_size("yhi") * lax.axis_size("core")
    pieces = partial.reshape(nrep, -1, partial.shape[1])
    return jnp.sum(group_exchange(pieces, REP, False, cid), axis=0)


def staged_index(col, per_owner):
    nz = lax.axis_size("z")
    nxy = lax.axis_size("x") * lax.axis_size("ylo")
    half = per_owner // 2
    owner = col // per_owner
    sub = col % per_owner
    z = owner % nz
    xy = owner // nz
    in_first = sub < half
    first = (z * nxy + xy) * half + jnp.where(in_first, sub, 0)
    second = (xy * nz + z) * half + jnp.where(in_first, 0, sub - half)
    return in_first, first, second


def tile_products(panels, adj_tiles, index):
    in_first, first, second = index
    picked = jnp.where(in_first[..., None, None], panels[0][first], panels[1][second])
    summed = jnp.einsum(
        "rkij,rkjh->rih", adj_tiles[:, 0], picked, preferred_element_type=jnp.float32
    )
    return summed.reshape(-1, panels[0].shape[2])


def local(node_feats, adj_tiles, col_index, w_in, b_in, w_out, b_out, cot_out):
    per_owner = node_feats.shape[0] // BLOCK
    index = staged_index(col_index[:, 0, :], per_owner)
    panels = gather_blk(node_feats, 0)
    partial_sum = tile_products(panels, adj_tiles, index)
    agg = reduce_rep(partial_sum, 8)
    agg_b = agg.astype(jnp.bfloat16)
    pre = jnp.dot(agg_b, w_in, preferred_element_type=jnp.float32) + b_in
    hidden = jax.nn.silu(pre).astype(jnp.bfloat16)
    projected = jnp.dot(hidden, w_out, preferred_element_type=jnp.float32) + b_out
    out_feats = (node_feats.astype(jnp.float32) + projected).astype(jnp.bfloat16)
    g_hidden = jnp.einsum("nh,fh->nf", cot_out, w_out, preferred_element_type=jnp.float32)
    sigma = jax.nn.sigmoid(pre)
    g_pre = (g_hidden * sigma * (1.0 + pre * (1.0 - sigma))).astype(jnp.bfloat16)
    g_agg = jnp.einsum("nf,hf->nh", g_pre, w_in, preferred_element_type=jnp.float32).astype(
        jnp.bfloat16
    )
    g_panels = gather_blk(g_agg, 1)
    back_partial = tile_products(g_panels, adj_tiles, index)
    back_rows = reduce_rep(back_partial, 9)
    grad_feats = (cot_out.astype(jnp.float32) + back_rows).astype(jnp.bfloat16)
    return (out_feats, grad_feats)


def solution(mesh):
    nblk = mesh.shape["blk"]
    nrep = mesh.shape["rep"]
    fine = Mesh(mesh.devices.reshape(nblk // 16, 2, 8, nrep // 2, 2), NAMES)
    rows = P(BLK + REP, None)
    placed = (
        rows,
        P(BLK, REP, None, None, None),
        P(BLK, REP, None),
        P(),
        P(),
        P(),
        P(),
        rows,
    )
    return jax.shard_map(
        local,
        mesh=fine,
        in_specs=placed,
        out_specs=(rows, rows),
        check_vma=False,
    )
```

```python
import functools

import jax
import jax.numpy as jnp
from jax import lax
from jax.experimental import pallas as pl
from jax.experimental.pallas import tpu as pltpu
from jax.sharding import Mesh
from jax.sharding import PartitionSpec as P

BLOCK = 128
NAMES = ("x", "ylo", "z", "yhi", "core")
BLK = ("x", "ylo", "z")
REP = ("yhi", "core")


def group_place(axes):
    sizes = [lax.axis_size(a) for a in axes]
    me = 0
    for a, n in zip(axes, sizes):
        me = me * n + lax.axis_index(a)
    return me, sizes


def peer_id(axes, sizes, p):
    coords = {}
    for a, n in reversed(list(zip(axes, sizes))):
        coords[a] = p % n
        p = p // n
    return coords


def exchange_kernel(jobs, *refs):
    count = len(jobs)
    src_refs, out_refs = refs[:count], refs[count : 2 * count]
    send_sem, recv_sem, local_sem = refs[2 * count :]
    places = [group_place(axes) for axes, _ in jobs]
    barrier = pltpu.get_barrier_semaphore()
    total = 0
    for (axes, _), (me, sizes), out_ref in zip(jobs, places, out_refs):
        n = out_ref.shape[0]
        total += n - 1
        for d in range(1, n):
            p = lax.rem(me + d, n)
            pl.semaphore_signal(barrier, 1, device_id=peer_id(axes, sizes, p))
    pl.semaphore_wait(barrier, total)
    copies = []
    for j, ((axes, gather), (me, sizes)) in enumerate(zip(jobs, places)):
        src_ref, out_ref = src_refs[j], out_refs[j]
        n = out_ref.shape[0]
        for d in range(1, n):
            p = lax.rem(me + d, n)
            copy = pltpu.make_async_remote_copy(
                src_ref=src_ref if gather else src_ref.at[p],
                dst_ref=out_ref.at[me],
                send_sem=send_sem.at[j, d],
                recv_sem=recv_sem.at[j, d],
                device_id=peer_id(axes, sizes, p),
            )
            copy.start()
            copies.append(copy)
        own = pltpu.make_async_copy(
            src_ref if gather else src_ref.at[me], out_ref.at[me], local_sem.at[j]
        )
        own.start()
        copies.append(own)
    for copy in copies:
        copy.wait()


def group_exchange(srcs, jobs, cid):
    shapes = []
    most = 1
    for src, (axes, gather) in zip(srcs, jobs):
        n = 1
        for a in axes:
            n *= lax.axis_size(a)
        most = max(most, n)
        block = src.shape if gather else src.shape[1:]
        shapes.append(jax.ShapeDtypeStruct((n, *block), src.dtype))
    count = len(jobs)
    return pl.pallas_call(
        functools.partial(exchange_kernel, tuple(jobs)),
        out_shape=tuple(shapes),
        in_specs=[pl.BlockSpec(memory_space=pl.ANY)] * count,
        out_specs=tuple([pl.BlockSpec(memory_space=pl.ANY)] * count),
        scratch_shapes=[
            pltpu.SemaphoreType.DMA((count, most)),
            pltpu.SemaphoreType.DMA((count, most)),
            pltpu.SemaphoreType.DMA((count,)),
        ],
        compiler_params=pltpu.CompilerParams(collective_id=cid, has_side_effects=True),
    )(*srcs)


def gather_blk(rows, cid):
    half = rows.shape[0] // 2
    xy = (("x", "ylo"), True)
    first, second = group_exchange((rows[:half], rows[half:]), (xy, (("z",), True)), cid)
    first = lax.all_gather(first, "z", axis=0, tiled=False)
    (second,) = group_exchange((second,), (xy,), cid + 4)
    width = rows.shape[1]
    return first.reshape(-1, BLOCK, width), second.reshape(-1, BLOCK, width)


def reduce_rep(partial, cid):
    nrep = lax.axis_size("yhi") * lax.axis_size("core")
    pieces = partial.reshape(nrep, -1, partial.shape[1])
    (pieces,) = group_exchange((pieces,), ((REP, False),), cid)
    return jnp.sum(pieces, axis=0)


def staged_index(col, per_owner):
    nz = lax.axis_size("z")
    nxy = lax.axis_size("x") * lax.axis_size("ylo")
    half = per_owner // 2
    owner = col // per_owner
    sub = col % per_owner
    z = owner % nz
    xy = owner // nz
    in_first = sub < half
    first = (z * nxy + xy) * half + jnp.where(in_first, sub, 0)
    second = (xy * nz + z) * half + jnp.where(in_first, 0, sub - half)
    return in_first, first, second


def tile_products(panels, adj_tiles, index):
    in_first, first, second = index
    picked = jnp.where(in_first[..., None, None], panels[0][first], panels[1][second])
    summed = jnp.einsum(
        "rkij,rkjh->rih", adj_tiles[:, 0], picked, preferred_element_type=jnp.float32
    )
    return summed.reshape(-1, panels[0].shape[2])


def local(node_feats, adj_tiles, col_index, w_in, b_in, w_out, b_out, cot_out):
    per_owner = node_feats.shape[0] // BLOCK
    index = staged_index(col_index[:, 0, :], per_owner)
    panels = gather_blk(node_feats, 0)
    partial_sum = tile_products(panels, adj_tiles, index)
    agg = reduce_rep(partial_sum, 8)
    agg_b = agg.astype(jnp.bfloat16)
    pre = jnp.dot(agg_b, w_in, preferred_element_type=jnp.float32) + b_in
    hidden = jax.nn.silu(pre).astype(jnp.bfloat16)
    projected = jnp.dot(hidden, w_out, preferred_element_type=jnp.float32) + b_out
    out_feats = (node_feats.astype(jnp.float32) + projected).astype(jnp.bfloat16)
    g_hidden = jnp.einsum("nh,fh->nf", cot_out, w_out, preferred_element_type=jnp.float32)
    sigma = jax.nn.sigmoid(pre)
    g_pre = (g_hidden * sigma * (1.0 + pre * (1.0 - sigma))).astype(jnp.bfloat16)
    g_agg = jnp.einsum("nf,hf->nh", g_pre, w_in, preferred_element_type=jnp.float32).astype(
        jnp.bfloat16
    )
    g_panels = gather_blk(g_agg, 1)
    back_partial = tile_products(g_panels, adj_tiles, index)
    back_rows = reduce_rep(back_partial, 9)
    grad_feats = (cot_out.astype(jnp.float32) + back_rows).astype(jnp.bfloat16)
    return (out_feats, grad_feats)


def solution(mesh):
    nblk = mesh.shape["blk"]
    nrep = mesh.shape["rep"]
    fine = Mesh(mesh.devices.reshape(nblk // 16, 2, 8, nrep // 2, 2), NAMES)
    rows = P(BLK + REP, None)
    placed = (
        rows,
        P(BLK, REP, None, None, None),
        P(BLK, REP, None),
        P(),
        P(),
        P(),
        P(),
        rows,
    )
    return jax.shard_map(
        local,
        mesh=fine,
        in_specs=placed,
        out_specs=(rows, rows),
        check_vma=False,
    )
```

```python
import functools

import jax
import jax.numpy as jnp
from jax import lax
from jax.experimental import pallas as pl
from jax.experimental.pallas import tpu as pltpu
from jax.sharding import Mesh
from jax.sharding import PartitionSpec as P

BLOCK = 128
NAMES = ("x", "ylo", "z", "yhi", "core")
BLK = ("x", "ylo", "z")
REP = ("yhi", "core")


def group_place(axes):
    sizes = [lax.axis_size(a) for a in axes]
    me = 0
    for a, n in zip(axes, sizes):
        me = me * n + lax.axis_index(a)
    return me, sizes


def peer_id(axes, sizes, p):
    coords = {}
    for a, n in reversed(list(zip(axes, sizes))):
        coords[a] = p % n
        p = p // n
    return coords


def exchange_kernel(jobs, *refs):
    count = len(jobs)
    src_refs, out_refs = refs[:count], refs[count : 2 * count]
    send_sem, recv_sem, local_sem = refs[2 * count :]
    places = [group_place(axes) for axes, _ in jobs]
    barrier = pltpu.get_barrier_semaphore()
    total = 0
    for (axes, _), (me, sizes), out_ref in zip(jobs, places, out_refs):
        n = out_ref.shape[0]
        total += n - 1
        for d in range(1, n):
            p = lax.rem(me + d, n)
            pl.semaphore_signal(barrier, 1, device_id=peer_id(axes, sizes, p))
    pl.semaphore_wait(barrier, total)
    copies = []
    for j, ((axes, gather), (me, sizes)) in enumerate(zip(jobs, places)):
        src_ref, out_ref = src_refs[j], out_refs[j]
        n = out_ref.shape[0]
        for d in range(1, n):
            p = lax.rem(me + d, n)
            copy = pltpu.make_async_remote_copy(
                src_ref=src_ref if gather else src_ref.at[p],
                dst_ref=out_ref.at[me],
                send_sem=send_sem.at[j, d],
                recv_sem=recv_sem.at[j, d],
                device_id=peer_id(axes, sizes, p),
            )
            copy.start()
            copies.append(copy)
        own = pltpu.make_async_copy(
            src_ref if gather else src_ref.at[me], out_ref.at[me], local_sem.at[j]
        )
        own.start()
        copies.append(own)
    for copy in copies:
        copy.wait()


def group_exchange(srcs, jobs, cid):
    shapes = []
    most = 1
    for src, (axes, gather) in zip(srcs, jobs):
        n = 1
        for a in axes:
            n *= lax.axis_size(a)
        most = max(most, n)
        block = src.shape if gather else src.shape[1:]
        shapes.append(jax.ShapeDtypeStruct((n, *block), src.dtype))
    count = len(jobs)
    return pl.pallas_call(
        functools.partial(exchange_kernel, tuple(jobs)),
        out_shape=tuple(shapes),
        in_specs=[pl.BlockSpec(memory_space=pl.ANY)] * count,
        out_specs=tuple([pl.BlockSpec(memory_space=pl.ANY)] * count),
        scratch_shapes=[
            pltpu.SemaphoreType.DMA((count, most)),
            pltpu.SemaphoreType.DMA((count, most)),
            pltpu.SemaphoreType.DMA((count,)),
        ],
        compiler_params=pltpu.CompilerParams(collective_id=cid, has_side_effects=True),
    )(*srcs)


def push_products_kernel(axes, flag_ref, first_ref, hi_ref, lo_ref, src_ref, panel_ref, adj_ref,
                         out_ref, landed, send_sem, recv_sem, local_sem):
    me, sizes = group_place(axes)
    n = landed.shape[0]
    rows, kq = adj_ref.shape[0], adj_ref.shape[1]
    barrier = pltpu.get_barrier_semaphore()
    for d in range(1, n):
        p = lax.rem(me + d, n)
        pl.semaphore_signal(barrier, 1, device_id=peer_id(axes, sizes, p))
    pl.semaphore_wait(barrier, n - 1)
    copies = []
    for d in range(1, n):
        p = lax.rem(me + d, n)
        copy = pltpu.make_async_remote_copy(
            src_ref=src_ref,
            dst_ref=landed.at[me],
            send_sem=send_sem.at[d],
            recv_sem=recv_sem.at[d],
            device_id=peer_id(axes, sizes, p),
        )
        copy.start()
        copies.append(copy)
    own = pltpu.make_async_copy(src_ref, landed.at[me], local_sem)
    own.start()

    def first_half(g, carry):
        acc = jnp.zeros(out_ref.shape[1:], jnp.float32)
        for k in range(kq):
            block = panel_ref[first_ref[g, k]]
            block = jnp.where(flag_ref[g, k] != 0, block, jnp.zeros_like(block))
            acc = acc + jnp.dot(adj_ref[g, k], block, preferred_element_type=jnp.float32)
        out_ref[g] = acc
        return carry

    def second_half(g, carry):
        acc = out_ref[g]
        for k in range(kq):
            block = landed[hi_ref[g, k], lo_ref[g, k]]
            block = jnp.where(flag_ref[g, k] != 0, jnp.zeros_like(block), block)
            acc = acc + jnp.dot(adj_ref[g, k], block, preferred_element_type=jnp.float32)
        out_ref[g] = acc
        return carry

    lax.fori_loop(0, rows, first_half, 0)
    for copy in copies:
        copy.wait()
    own.wait()
    lax.fori_loop(0, rows, second_half, 0)


def push_products(index, src, panel, adj, axes, cid):
    n = 1
    for a in axes:
        n *= lax.axis_size(a)
    rows = adj.shape[0]
    smem = pl.BlockSpec(memory_space=pltpu.SMEM)
    vmem = pl.BlockSpec(memory_space=pltpu.VMEM)
    return pl.pallas_call(
        functools.partial(push_products_kernel, axes),
        out_shape=jax.ShapeDtypeStruct((rows, BLOCK, panel.shape[2]), jnp.float32),
        in_specs=[smem] * 4 + [pl.BlockSpec(memory_space=pl.ANY), vmem, vmem],
        out_specs=vmem,
        scratch_shapes=[
            pltpu.VMEM((n, *src.shape), src.dtype),
            pltpu.SemaphoreType.DMA((n,)),
            pltpu.SemaphoreType.DMA((n,)),
            pltpu.SemaphoreType.DMA,
        ],
        compiler_params=pltpu.CompilerParams(collective_id=cid, has_side_effects=True),
    )(*index, src, panel, adj)


def aggregate(rows, adj, index, cid):
    half = rows.shape[0] // 2
    width = rows.shape[1]
    xy = (("x", "ylo"), True)
    first, second = group_exchange((rows[:half], rows[half:]), (xy, (("z",), True)), cid)
    first = lax.all_gather(first, "z", axis=0, tiled=False).reshape(-1, BLOCK, width)
    second = second.reshape(-1, BLOCK, width)
    summed = push_products(index, second, first, adj, ("x", "ylo"), cid + 4)
    return summed.reshape(-1, width)


def reduce_rep(partial, cid):
    nrep = lax.axis_size("yhi") * lax.axis_size("core")
    pieces = partial.reshape(nrep, -1, partial.shape[1])
    (pieces,) = group_exchange((pieces,), ((REP, False),), cid)
    return jnp.sum(pieces, axis=0)


def staged_index(col, per_owner):
    nz = lax.axis_size("z")
    nxy = lax.axis_size("x") * lax.axis_size("ylo")
    half = per_owner // 2
    owner = col // per_owner
    sub = col % per_owner
    z = owner % nz
    xy = owner // nz
    in_first = sub < half
    first = (z * nxy + xy) * half + jnp.where(in_first, sub, 0)
    lo = z * half + jnp.where(in_first, 0, sub - half)
    return in_first.astype(jnp.int32), first, xy, lo


def local(node_feats, adj_tiles, col_index, w_in, b_in, w_out, b_out, cot_out):
    per_owner = node_feats.shape[0] // BLOCK
    index = staged_index(col_index[:, 0, :], per_owner)
    adj = adj_tiles[:, 0]
    partial_sum = aggregate(node_feats, adj, index, 0)
    agg = reduce_rep(partial_sum, 8)
    agg_b = agg.astype(jnp.bfloat16)
    pre = jnp.dot(agg_b, w_in, preferred_element_type=jnp.float32) + b_in
    hidden = jax.nn.silu(pre).astype(jnp.bfloat16)
    projected = jnp.dot(hidden, w_out, preferred_element_type=jnp.float32) + b_out
    out_feats = (node_feats.astype(jnp.float32) + projected).astype(jnp.bfloat16)
    g_hidden = jnp.einsum("nh,fh->nf", cot_out, w_out, preferred_element_type=jnp.float32)
    sigma = jax.nn.sigmoid(pre)
    g_pre = (g_hidden * sigma * (1.0 + pre * (1.0 - sigma))).astype(jnp.bfloat16)
    g_agg = jnp.einsum("nf,hf->nh", g_pre, w_in, preferred_element_type=jnp.float32).astype(
        jnp.bfloat16
    )
    back_partial = aggregate(g_agg, adj, index, 1)
    back_rows = reduce_rep(back_partial, 9)
    grad_feats = (cot_out.astype(jnp.float32) + back_rows).astype(jnp.bfloat16)
    return (out_feats, grad_feats)


def solution(mesh):
    nblk = mesh.shape["blk"]
    nrep = mesh.shape["rep"]
    fine = Mesh(mesh.devices.reshape(nblk // 16, 2, 8, nrep // 2, 2), NAMES)
    rows = P(BLK + REP, None)
    placed = (
        rows,
        P(BLK, REP, None, None, None),
        P(BLK, REP, None),
        P(),
        P(),
        P(),
        P(),
        rows,
    )
    return jax.shard_map(
        local,
        mesh=fine,
        in_specs=placed,
        out_specs=(rows, rows),
        check_vma=False,
    )
```

```python
import functools

import jax
import jax.numpy as jnp
from jax import lax
from jax.experimental import pallas as pl
from jax.experimental.pallas import tpu as pltpu
from jax.sharding import Mesh
from jax.sharding import PartitionSpec as P

BLOCK = 128
NAMES = ("x", "ylo", "z", "yhi", "core")
BLK = ("x", "ylo", "z")
REP = ("yhi", "core")


def group_place(axes):
    sizes = [lax.axis_size(a) for a in axes]
    me = 0
    for a, n in zip(axes, sizes):
        me = me * n + lax.axis_index(a)
    return me, sizes


def peer_id(axes, sizes, p):
    coords = {}
    for a, n in reversed(list(zip(axes, sizes))):
        coords[a] = p % n
        p = p // n
    return coords


def exchange_kernel(jobs, *refs):
    count = len(jobs)
    src_refs, out_refs = refs[:count], refs[count : 2 * count]
    send_sem, recv_sem, local_sem = refs[2 * count :]
    places = [group_place(axes) for axes, _ in jobs]
    barrier = pltpu.get_barrier_semaphore()
    total = 0
    for (axes, _), (me, sizes), out_ref in zip(jobs, places, out_refs):
        n = out_ref.shape[0]
        total += n - 1
        for d in range(1, n):
            p = lax.rem(me + d, n)
            pl.semaphore_signal(barrier, 1, device_id=peer_id(axes, sizes, p))
    pl.semaphore_wait(barrier, total)
    copies = []
    for j, ((axes, gather), (me, sizes)) in enumerate(zip(jobs, places)):
        src_ref, out_ref = src_refs[j], out_refs[j]
        n = out_ref.shape[0]
        for d in range(1, n):
            p = lax.rem(me + d, n)
            copy = pltpu.make_async_remote_copy(
                src_ref=src_ref if gather else src_ref.at[p],
                dst_ref=out_ref.at[me],
                send_sem=send_sem.at[j, d],
                recv_sem=recv_sem.at[j, d],
                device_id=peer_id(axes, sizes, p),
            )
            copy.start()
            copies.append(copy)
        own = pltpu.make_async_copy(
            src_ref if gather else src_ref.at[me], out_ref.at[me], local_sem.at[j]
        )
        own.start()
        copies.append(own)
    for copy in copies:
        copy.wait()


def group_exchange(srcs, jobs, cid):
    shapes = []
    most = 1
    for src, (axes, gather) in zip(srcs, jobs):
        n = 1
        for a in axes:
            n *= lax.axis_size(a)
        most = max(most, n)
        block = src.shape if gather else src.shape[1:]
        shapes.append(jax.ShapeDtypeStruct((n, *block), src.dtype))
    count = len(jobs)
    return pl.pallas_call(
        functools.partial(exchange_kernel, tuple(jobs)),
        out_shape=tuple(shapes),
        in_specs=[pl.BlockSpec(memory_space=pl.ANY)] * count,
        out_specs=tuple([pl.BlockSpec(memory_space=pl.ANY)] * count),
        scratch_shapes=[
            pltpu.SemaphoreType.DMA((count, most)),
            pltpu.SemaphoreType.DMA((count, most)),
            pltpu.SemaphoreType.DMA((count,)),
        ],
        compiler_params=pltpu.CompilerParams(collective_id=cid, has_side_effects=True),
    )(*srcs)


def gather_blk(rows, cid):
    half = rows.shape[0] // 2
    xy = (("x", "ylo"), True)
    first, second = group_exchange((rows[:half], rows[half:]), (xy, (("z",), True)), cid)
    first = lax.all_gather(first, "z", axis=0, tiled=False)
    (second,) = group_exchange((second,), (xy,), cid + 4)
    width = rows.shape[1]
    return first.reshape(-1, BLOCK, width), second.reshape(-1, BLOCK, width)


def reduce_rep(partial, cid):
    nrep = lax.axis_size("yhi") * lax.axis_size("core")
    pieces = partial.reshape(nrep, -1, partial.shape[1])
    (pieces,) = group_exchange((pieces,), ((REP, False),), cid)
    return jnp.sum(pieces, axis=0)


def staged_index(col, per_owner):
    nz = lax.axis_size("z")
    nxy = lax.axis_size("x") * lax.axis_size("ylo")
    half = per_owner // 2
    owner = col // per_owner
    sub = col % per_owner
    z = owner % nz
    xy = owner // nz
    in_first = sub < half
    first = (z * nxy + xy) * half + jnp.where(in_first, sub, 0)
    second = (xy * nz + z) * half + jnp.where(in_first, 0, sub - half)
    return in_first.astype(jnp.int32), first, second


def products_kernel(flag_ref, first_ref, second_ref, *refs):
    kq = len(refs) // 2 - 1
    firsts, seconds = refs[:kq], refs[kq : 2 * kq]
    adj_ref, out_ref = refs[2 * kq :]
    g = pl.program_id(0)
    acc = jnp.zeros(out_ref.shape[1:], jnp.float32)
    for k in range(kq):
        block = jnp.where(flag_ref[g, k] != 0, firsts[k][0], seconds[k][0])
        acc = acc + jnp.dot(adj_ref[0, k], block, preferred_element_type=jnp.float32)
    out_ref[0] = acc


def tile_products(panels, adj_tiles, index):
    flag, first, second = index
    rows, kq = flag.shape
    width = panels[0].shape[2]
    tile = (1, BLOCK, width)

    def pick(table, k):
        return pl.BlockSpec(tile, lambda g, f, a, b: (table(f, a, b)[g, k], 0, 0))

    specs = [pick(lambda f, a, b: a, k) for k in range(kq)]
    specs += [pick(lambda f, a, b: b, k) for k in range(kq)]
    specs.append(pl.BlockSpec((1, kq, BLOCK, BLOCK), lambda g, f, a, b: (g, 0, 0, 0)))
    summed = pl.pallas_call(
        products_kernel,
        out_shape=jax.ShapeDtypeStruct((rows, BLOCK, width), jnp.float32),
        grid_spec=pltpu.PrefetchScalarGridSpec(
            num_scalar_prefetch=3,
            grid=(rows,),
            in_specs=specs,
            out_specs=pl.BlockSpec(tile, lambda g, f, a, b: (g, 0, 0)),
        ),
    )(flag, first, second, *([panels[0]] * kq), *([panels[1]] * kq), adj_tiles[:, 0])
    return summed.reshape(-1, width)


def local(node_feats, adj_tiles, col_index, w_in, b_in, w_out, b_out, cot_out):
    per_owner = node_feats.shape[0] // BLOCK
    index = staged_index(col_index[:, 0, :], per_owner)
    panels = gather_blk(node_feats, 0)
    partial_sum = tile_products(panels, adj_tiles, index)
    agg = reduce_rep(partial_sum, 8)
    agg_b = agg.astype(jnp.bfloat16)
    pre = jnp.dot(agg_b, w_in, preferred_element_type=jnp.float32) + b_in
    hidden = jax.nn.silu(pre).astype(jnp.bfloat16)
    projected = jnp.dot(hidden, w_out, preferred_element_type=jnp.float32) + b_out
    out_feats = (node_feats.astype(jnp.float32) + projected).astype(jnp.bfloat16)
    g_hidden = jnp.einsum("nh,fh->nf", cot_out, w_out, preferred_element_type=jnp.float32)
    sigma = jax.nn.sigmoid(pre)
    g_pre = (g_hidden * sigma * (1.0 + pre * (1.0 - sigma))).astype(jnp.bfloat16)
    g_agg = jnp.einsum("nf,hf->nh", g_pre, w_in, preferred_element_type=jnp.float32).astype(
        jnp.bfloat16
    )
    g_panels = gather_blk(g_agg, 1)
    back_partial = tile_products(g_panels, adj_tiles, index)
    back_rows = reduce_rep(back_partial, 9)
    grad_feats = (cot_out.astype(jnp.float32) + back_rows).astype(jnp.bfloat16)
    return (out_feats, grad_feats)


def solution(mesh):
    nblk = mesh.shape["blk"]
    nrep = mesh.shape["rep"]
    fine = Mesh(mesh.devices.reshape(nblk // 16, 2, 8, nrep // 2, 2), NAMES)
    rows = P(BLK + REP, None)
    placed = (
        rows,
        P(BLK, REP, None, None, None),
        P(BLK, REP, None),
        P(),
        P(),
        P(),
        P(),
        rows,
    )
    return jax.shard_map(
        local,
        mesh=fine,
        in_specs=placed,
        out_specs=(rows, rows),
        check_vma=False,
    )
```

```python
import functools

import jax
import jax.numpy as jnp
from jax import lax
from jax.experimental import pallas as pl
from jax.experimental.pallas import tpu as pltpu
from jax.sharding import Mesh
from jax.sharding import PartitionSpec as P

BLOCK = 128
NAMES = ("x", "ylo", "z", "yhi", "core")
BLK = ("x", "ylo", "z")
REP = ("yhi", "core")


def group_place(axes):
    sizes = [lax.axis_size(a) for a in axes]
    me = 0
    for a, n in zip(axes, sizes):
        me = me * n + lax.axis_index(a)
    return me, sizes


def peer_id(axes, sizes, p):
    coords = {}
    for a, n in reversed(list(zip(axes, sizes))):
        coords[a] = p % n
        p = p // n
    return coords


def exchange_kernel(jobs, *refs):
    count = len(jobs)
    src_refs, out_refs = refs[:count], refs[count : 2 * count]
    send_sem, recv_sem, local_sem = refs[2 * count :]
    places = [group_place(axes) for axes, _ in jobs]
    barrier = pltpu.get_barrier_semaphore()
    total = 0
    for (axes, _), (me, sizes), out_ref in zip(jobs, places, out_refs):
        n = out_ref.shape[0]
        total += n - 1
        for d in range(1, n):
            p = lax.rem(me + d, n)
            pl.semaphore_signal(barrier, 1, device_id=peer_id(axes, sizes, p))
    pl.semaphore_wait(barrier, total)
    copies = []
    for j, ((axes, gather), (me, sizes)) in enumerate(zip(jobs, places)):
        src_ref, out_ref = src_refs[j], out_refs[j]
        n = out_ref.shape[0]
        for d in range(1, n):
            p = lax.rem(me + d, n)
            copy = pltpu.make_async_remote_copy(
                src_ref=src_ref if gather else src_ref.at[p],
                dst_ref=out_ref.at[me],
                send_sem=send_sem.at[j, d],
                recv_sem=recv_sem.at[j, d],
                device_id=peer_id(axes, sizes, p),
            )
            copy.start()
            copies.append(copy)
        own = pltpu.make_async_copy(
            src_ref if gather else src_ref.at[me], out_ref.at[me], local_sem.at[j]
        )
        own.start()
        copies.append(own)
    for copy in copies:
        copy.wait()


def group_exchange(srcs, jobs, cid):
    shapes = []
    most = 1
    for src, (axes, gather) in zip(srcs, jobs):
        n = 1
        for a in axes:
            n *= lax.axis_size(a)
        most = max(most, n)
        block = src.shape if gather else src.shape[1:]
        shapes.append(jax.ShapeDtypeStruct((n, *block), src.dtype))
    count = len(jobs)
    return pl.pallas_call(
        functools.partial(exchange_kernel, tuple(jobs)),
        out_shape=tuple(shapes),
        in_specs=[pl.BlockSpec(memory_space=pl.ANY)] * count,
        out_specs=tuple([pl.BlockSpec(memory_space=pl.ANY)] * count),
        scratch_shapes=[
            pltpu.SemaphoreType.DMA((count, most)),
            pltpu.SemaphoreType.DMA((count, most)),
            pltpu.SemaphoreType.DMA((count,)),
        ],
        compiler_params=pltpu.CompilerParams(collective_id=cid, has_side_effects=True),
    )(*srcs)


def tree_kernel(src_ref, out_ref, send_sem, recv_sem, local_sem):
    nx, ny = lax.axis_size("x"), lax.axis_size("ylo")
    x, y = lax.axis_index("x"), lax.axis_index("ylo")
    right, left, other = lax.rem(x + 1, nx), lax.rem(x + nx - 1, nx), ny - 1 - y
    to_right, to_left, to_other = {"x": right}, {"x": left}, {"ylo": other}
    barrier = pltpu.get_barrier_semaphore()
    for peer in (to_right, to_left, to_other):
        pl.semaphore_signal(barrier, 1, device_id=peer)
    pl.semaphore_wait(barrier, 3)

    def send(kind, src, slot, peer):
        copy = pltpu.make_async_remote_copy(
            src_ref=src,
            dst_ref=out_ref.at[slot],
            send_sem=send_sem.at[kind],
            recv_sem=recv_sem.at[kind],
            device_id=peer,
        )
        copy.start()
        return copy

    me = x * ny + y
    own = pltpu.make_async_copy(src_ref, out_ref.at[me], local_sem)
    own.start()
    first_right = send(0, src_ref, me, to_right)
    first_left = send(1, src_ref, me, to_left)
    first_other = send(2, src_ref, me, to_other)
    first_right.wait_recv()
    from_left = left * ny + y
    second_right = send(3, out_ref.at[from_left], from_left, to_right)
    first_other.wait_recv()
    from_other = x * ny + other
    other_right = send(4, out_ref.at[from_other], from_other, to_right)
    other_left = send(5, out_ref.at[from_other], from_other, to_left)
    other_right.wait_recv()
    from_left_other = left * ny + other
    third_right = send(6, out_ref.at[from_left_other], from_left_other, to_right)
    for copy in (first_left, second_right, other_left, third_right):
        copy.wait_recv()
    for copy in (first_right, first_left, first_other, second_right, other_right, other_left, third_right):
        copy.wait_send()
    own.wait()


def tree_gather(src, cid):
    n = lax.axis_size("x") * lax.axis_size("ylo")
    return pl.pallas_call(
        tree_kernel,
        out_shape=jax.ShapeDtypeStruct((n, *src.shape), src.dtype),
        in_specs=[pl.BlockSpec(memory_space=pl.ANY)],
        out_specs=pl.BlockSpec(memory_space=pl.ANY),
        scratch_shapes=[
            pltpu.SemaphoreType.DMA((7,)),
            pltpu.SemaphoreType.DMA((7,)),
            pltpu.SemaphoreType.DMA,
        ],
        compiler_params=pltpu.CompilerParams(collective_id=cid, has_side_effects=True),
    )(src)


def gather_blk(rows, cid):
    half = rows.shape[0] // 2
    xy = (("x", "ylo"), True)
    first, second = group_exchange((rows[:half], rows[half:]), (xy, (("z",), True)), cid)
    first = lax.all_gather(first, "z", axis=0, tiled=False)
    second = tree_gather(second, cid + 4)
    width = rows.shape[1]
    return first.reshape(-1, BLOCK, width), second.reshape(-1, BLOCK, width)


def reduce_rep(partial, cid):
    nrep = lax.axis_size("yhi") * lax.axis_size("core")
    pieces = partial.reshape(nrep, -1, partial.shape[1])
    (pieces,) = group_exchange((pieces,), ((REP, False),), cid)
    return jnp.sum(pieces, axis=0)


def staged_index(col, per_owner):
    nz = lax.axis_size("z")
    nxy = lax.axis_size("x") * lax.axis_size("ylo")
    half = per_owner // 2
    owner = col // per_owner
    sub = col % per_owner
    z = owner % nz
    xy = owner // nz
    in_first = sub < half
    first = (z * nxy + xy) * half + jnp.where(in_first, sub, 0)
    second = (xy * nz + z) * half + jnp.where(in_first, 0, sub - half)
    return in_first.astype(jnp.int32), first, second


def products_kernel(flag_ref, first_ref, second_ref, *refs):
    kq = len(refs) // 2 - 1
    firsts, seconds = refs[:kq], refs[kq : 2 * kq]
    adj_ref, out_ref = refs[2 * kq :]
    g = pl.program_id(0)
    acc = jnp.zeros(out_ref.shape[1:], jnp.float32)
    for k in range(kq):
        block = jnp.where(flag_ref[g, k] != 0, firsts[k][0], seconds[k][0])
        acc = acc + jnp.dot(adj_ref[0, k], block, preferred_element_type=jnp.float32)
    out_ref[0] = acc


def tile_products(panels, adj_tiles, index):
    flag, first, second = index
    rows, kq = flag.shape
    width = panels[0].shape[2]
    tile = (1, BLOCK, width)

    def pick(table, k):
        return pl.BlockSpec(tile, lambda g, f, a, b: (table(f, a, b)[g, k], 0, 0))

    specs = [pick(lambda f, a, b: a, k) for k in range(kq)]
    specs += [pick(lambda f, a, b: b, k) for k in range(kq)]
    specs.append(pl.BlockSpec((1, kq, BLOCK, BLOCK), lambda g, f, a, b: (g, 0, 0, 0)))
    summed = pl.pallas_call(
        products_kernel,
        out_shape=jax.ShapeDtypeStruct((rows, BLOCK, width), jnp.float32),
        grid_spec=pltpu.PrefetchScalarGridSpec(
            num_scalar_prefetch=3,
            grid=(rows,),
            in_specs=specs,
            out_specs=pl.BlockSpec(tile, lambda g, f, a, b: (g, 0, 0)),
        ),
    )(flag, first, second, *([panels[0]] * kq), *([panels[1]] * kq), adj_tiles[:, 0])
    return summed.reshape(-1, width)


def local(node_feats, adj_tiles, col_index, w_in, b_in, w_out, b_out, cot_out):
    per_owner = node_feats.shape[0] // BLOCK
    index = staged_index(col_index[:, 0, :], per_owner)
    panels = gather_blk(node_feats, 0)
    partial_sum = tile_products(panels, adj_tiles, index)
    agg = reduce_rep(partial_sum, 8)
    agg_b = agg.astype(jnp.bfloat16)
    pre = jnp.dot(agg_b, w_in, preferred_element_type=jnp.float32) + b_in
    hidden = jax.nn.silu(pre).astype(jnp.bfloat16)
    projected = jnp.dot(hidden, w_out, preferred_element_type=jnp.float32) + b_out
    out_feats = (node_feats.astype(jnp.float32) + projected).astype(jnp.bfloat16)
    g_hidden = jnp.einsum("nh,fh->nf", cot_out, w_out, preferred_element_type=jnp.float32)
    sigma = jax.nn.sigmoid(pre)
    g_pre = (g_hidden * sigma * (1.0 + pre * (1.0 - sigma))).astype(jnp.bfloat16)
    g_agg = jnp.einsum("nf,hf->nh", g_pre, w_in, preferred_element_type=jnp.float32).astype(
        jnp.bfloat16
    )
    g_panels = gather_blk(g_agg, 1)
    back_partial = tile_products(g_panels, adj_tiles, index)
    back_rows = reduce_rep(back_partial, 9)
    grad_feats = (cot_out.astype(jnp.float32) + back_rows).astype(jnp.bfloat16)
    return (out_feats, grad_feats)


def solution(mesh):
    nblk = mesh.shape["blk"]
    nrep = mesh.shape["rep"]
    fine = Mesh(mesh.devices.reshape(nblk // 16, 2, 8, nrep // 2, 2), NAMES)
    rows = P(BLK + REP, None)
    placed = (
        rows,
        P(BLK, REP, None, None, None),
        P(BLK, REP, None),
        P(),
        P(),
        P(),
        P(),
        rows,
    )
    return jax.shard_map(
        local,
        mesh=fine,
        in_specs=placed,
        out_specs=(rows, rows),
        check_vma=False,
    )
```

```python
import functools

import jax
import jax.numpy as jnp
from jax import lax
from jax.experimental import pallas as pl
from jax.experimental.pallas import tpu as pltpu
from jax.sharding import Mesh
from jax.sharding import PartitionSpec as P

BLOCK = 128
NAMES = ("x", "ylo", "z", "yhi", "core")
BLK = ("x", "ylo", "z")
REP = ("yhi", "core")


def group_place(axes):
    sizes = [lax.axis_size(a) for a in axes]
    me = 0
    for a, n in zip(axes, sizes):
        me = me * n + lax.axis_index(a)
    return me, sizes


def peer_id(axes, sizes, p):
    coords = {}
    for a, n in reversed(list(zip(axes, sizes))):
        coords[a] = p % n
        p = p // n
    return coords


def exchange_kernel(jobs, *refs):
    count = len(jobs)
    src_refs, out_refs = refs[:count], refs[count : 2 * count]
    send_sem, recv_sem, local_sem = refs[2 * count :]
    places = [group_place(axes) for axes, _ in jobs]
    barrier = pltpu.get_barrier_semaphore()
    total = 0
    for (axes, _), (me, sizes), out_ref in zip(jobs, places, out_refs):
        n = out_ref.shape[0]
        total += n - 1
        for d in range(1, n):
            p = lax.rem(me + d, n)
            pl.semaphore_signal(barrier, 1, device_id=peer_id(axes, sizes, p))
    pl.semaphore_wait(barrier, total)
    copies = []
    for j, ((axes, gather), (me, sizes)) in enumerate(zip(jobs, places)):
        src_ref, out_ref = src_refs[j], out_refs[j]
        n = out_ref.shape[0]
        for d in range(1, n):
            p = lax.rem(me + d, n)
            copy = pltpu.make_async_remote_copy(
                src_ref=src_ref if gather else src_ref.at[p],
                dst_ref=out_ref.at[me],
                send_sem=send_sem.at[j, d],
                recv_sem=recv_sem.at[j, d],
                device_id=peer_id(axes, sizes, p),
            )
            copy.start()
            copies.append(copy)
        own = pltpu.make_async_copy(
            src_ref if gather else src_ref.at[me], out_ref.at[me], local_sem.at[j]
        )
        own.start()
        copies.append(own)
    for copy in copies:
        copy.wait()


def group_exchange(srcs, jobs, cid):
    shapes = []
    most = 1
    for src, (axes, gather) in zip(srcs, jobs):
        n = 1
        for a in axes:
            n *= lax.axis_size(a)
        most = max(most, n)
        block = src.shape if gather else src.shape[1:]
        shapes.append(jax.ShapeDtypeStruct((n, *block), src.dtype))
    count = len(jobs)
    return pl.pallas_call(
        functools.partial(exchange_kernel, tuple(jobs)),
        out_shape=tuple(shapes),
        in_specs=[pl.BlockSpec(memory_space=pl.ANY)] * count,
        out_specs=tuple([pl.BlockSpec(memory_space=pl.ANY)] * count),
        scratch_shapes=[
            pltpu.SemaphoreType.DMA((count, most)),
            pltpu.SemaphoreType.DMA((count, most)),
            pltpu.SemaphoreType.DMA((count,)),
        ],
        compiler_params=pltpu.CompilerParams(collective_id=cid, has_side_effects=True),
    )(*srcs)


def tree_kernel(src_ref, out_ref, send_sem, recv_sem, local_sem):
    nx, ny = lax.axis_size("x"), lax.axis_size("ylo")
    x, y = lax.axis_index("x"), lax.axis_index("ylo")
    right, left, other = lax.rem(x + 1, nx), lax.rem(x + nx - 1, nx), ny - 1 - y
    to_right, to_left, to_other = {"x": right}, {"x": left}, {"ylo": other}
    barrier = pltpu.get_barrier_semaphore()
    for peer in (to_right, to_left, to_other):
        pl.semaphore_signal(barrier, 1, device_id=peer)
    pl.semaphore_wait(barrier, 3)

    def send(kind, src, slot, peer):
        copy = pltpu.make_async_remote_copy(
            src_ref=src,
            dst_ref=out_ref.at[slot],
            send_sem=send_sem.at[kind],
            recv_sem=recv_sem.at[kind],
            device_id=peer,
        )
        copy.start()
        return copy

    me = x * ny + y
    own = pltpu.make_async_copy(src_ref, out_ref.at[me], local_sem)
    own.start()
    first_right = send(0, src_ref, me, to_right)
    first_left = send(1, src_ref, me, to_left)
    first_other = send(2, src_ref, me, to_other)
    first_right.wait_recv()
    from_left = left * ny + y
    second_right = send(3, out_ref.at[from_left], from_left, to_right)
    first_other.wait_recv()
    from_other = x * ny + other
    other_right = send(4, out_ref.at[from_other], from_other, to_right)
    other_left = send(5, out_ref.at[from_other], from_other, to_left)
    other_right.wait_recv()
    from_left_other = left * ny + other
    third_right = send(6, out_ref.at[from_left_other], from_left_other, to_right)
    for copy in (first_left, second_right, other_left, third_right):
        copy.wait_recv()
    for copy in (first_right, first_left, first_other, second_right, other_right, other_left, third_right):
        copy.wait_send()
    own.wait()


def tree_gather(src, cid):
    n = lax.axis_size("x") * lax.axis_size("ylo")
    return pl.pallas_call(
        tree_kernel,
        out_shape=jax.ShapeDtypeStruct((n, *src.shape), src.dtype),
        in_specs=[pl.BlockSpec(memory_space=pl.ANY)],
        out_specs=pl.BlockSpec(memory_space=pl.ANY),
        scratch_shapes=[
            pltpu.SemaphoreType.DMA((7,)),
            pltpu.SemaphoreType.DMA((7,)),
            pltpu.SemaphoreType.DMA,
        ],
        compiler_params=pltpu.CompilerParams(collective_id=cid, has_side_effects=True),
    )(src)


def gather_blk(rows, cid):
    half = rows.shape[0] // 2
    xy = (("x", "ylo"), True)
    first, second = group_exchange((rows[:half], rows[half:]), (xy, (("z",), True)), cid)
    first = lax.all_gather(first, "z", axis=0, tiled=False)
    second = tree_gather(second, cid + 4)
    width = rows.shape[1]
    return first.reshape(-1, BLOCK, width), second.reshape(-1, BLOCK, width)


def reduce_rep(partial, cid):
    ncore = lax.axis_size("core")
    nyhi = lax.axis_size("yhi")
    pieces = partial.reshape(ncore, nyhi, -1, partial.shape[1])
    (pieces,) = group_exchange((pieces,), ((("core",), False),), cid)
    pieces = jnp.sum(pieces, axis=0)
    (pieces,) = group_exchange((pieces,), ((("yhi",), False),), cid + 2)
    return jnp.sum(pieces, axis=0)


def staged_index(col, per_owner):
    nz = lax.axis_size("z")
    nxy = lax.axis_size("x") * lax.axis_size("ylo")
    half = per_owner // 2
    owner = col // per_owner
    sub = col % per_owner
    z = owner % nz
    xy = owner // nz
    in_first = sub < half
    first = (z * nxy + xy) * half + jnp.where(in_first, sub, 0)
    second = (xy * nz + z) * half + jnp.where(in_first, 0, sub - half)
    return in_first.astype(jnp.int32), first, second


def products_kernel(flag_ref, first_ref, second_ref, *refs):
    adj_ref, out_ref = refs[-2:]
    rows, kq = adj_ref.shape[0], adj_ref.shape[1]
    firsts, seconds = refs[: rows * kq], refs[rows * kq : 2 * rows * kq]
    base = pl.program_id(0) * rows
    for r in range(rows):
        acc = jnp.zeros(out_ref.shape[1:], jnp.float32)
        for k in range(kq):
            at = r * kq + k
            block = jnp.where(flag_ref[base + r, k] != 0, firsts[at][0], seconds[at][0])
            acc = acc + jnp.dot(adj_ref[r, k], block, preferred_element_type=jnp.float32)
        out_ref[r] = acc


def tile_products(panels, adj_tiles, index, per_piece):
    flag, first, second = index
    rows, kq = flag.shape
    width = panels[0].shape[2]
    tile = (1, BLOCK, width)
    ncore = lax.axis_size("core")
    nyhi = lax.axis_size("yhi")

    def pick(table, r, k):
        return pl.BlockSpec(tile, lambda g, f, a, b: (table(f, a, b)[g * per_piece + r, k], 0, 0))

    specs = [pick(lambda f, a, b: a, r, k) for r in range(per_piece) for k in range(kq)]
    specs += [pick(lambda f, a, b: b, r, k) for r in range(per_piece) for k in range(kq)]
    specs.append(pl.BlockSpec((per_piece, kq, BLOCK, BLOCK), lambda g, f, a, b: (g, 0, 0, 0)))
    out_spec = pl.BlockSpec(
        (per_piece, BLOCK, width), lambda g, f, a, b: ((g % ncore) * nyhi + g // ncore, 0, 0)
    )
    summed = pl.pallas_call(
        products_kernel,
        out_shape=jax.ShapeDtypeStruct((rows, BLOCK, width), jnp.float32),
        grid_spec=pltpu.PrefetchScalarGridSpec(
            num_scalar_prefetch=3,
            grid=(rows // per_piece,),
            in_specs=specs,
            out_specs=out_spec,
        ),
    )(flag, first, second, *([panels[0]] * (per_piece * kq)), *([panels[1]] * (per_piece * kq)), adj_tiles[:, 0])
    return summed.reshape(-1, width)


def local(node_feats, adj_tiles, col_index, w_in, b_in, w_out, b_out, cot_out):
    per_owner = node_feats.shape[0] // BLOCK
    index = staged_index(col_index[:, 0, :], per_owner)
    per_piece = per_owner
    panels = gather_blk(node_feats, 0)
    partial_sum = tile_products(panels, adj_tiles, index, per_piece)
    agg = reduce_rep(partial_sum, 8)
    agg_b = agg.astype(jnp.bfloat16)
    pre = jnp.dot(agg_b, w_in, preferred_element_type=jnp.float32) + b_in
    hidden = jax.nn.silu(pre).astype(jnp.bfloat16)
    projected = jnp.dot(hidden, w_out, preferred_element_type=jnp.float32) + b_out
    out_feats = (node_feats.astype(jnp.float32) + projected).astype(jnp.bfloat16)
    g_hidden = jnp.einsum("nh,fh->nf", cot_out, w_out, preferred_element_type=jnp.float32)
    sigma = jax.nn.sigmoid(pre)
    g_pre = (g_hidden * sigma * (1.0 + pre * (1.0 - sigma))).astype(jnp.bfloat16)
    g_agg = jnp.einsum("nf,hf->nh", g_pre, w_in, preferred_element_type=jnp.float32).astype(
        jnp.bfloat16
    )
    g_panels = gather_blk(g_agg, 1)
    back_partial = tile_products(g_panels, adj_tiles, index, per_piece)
    back_rows = reduce_rep(back_partial, 9)
    grad_feats = (cot_out.astype(jnp.float32) + back_rows).astype(jnp.bfloat16)
    return (out_feats, grad_feats)


def solution(mesh):
    nblk = mesh.shape["blk"]
    nrep = mesh.shape["rep"]
    fine = Mesh(mesh.devices.reshape(nblk // 16, 2, 8, nrep // 2, 2), NAMES)
    rows = P(BLK + REP, None)
    placed = (
        rows,
        P(BLK, REP, None, None, None),
        P(BLK, REP, None),
        P(),
        P(),
        P(),
        P(),
        rows,
    )
    return jax.shard_map(
        local,
        mesh=fine,
        in_specs=placed,
        out_specs=(rows, rows),
        check_vma=False,
    )
```

```python
import functools

import jax
import jax.numpy as jnp
from jax import lax
from jax.experimental import pallas as pl
from jax.experimental.pallas import tpu as pltpu
from jax.sharding import Mesh
from jax.sharding import PartitionSpec as P

BLOCK = 128
NAMES = ("x", "ylo", "z", "yhi", "core")
BLK = ("x", "ylo", "z")
REP = ("yhi", "core")


def group_place(axes):
    sizes = [lax.axis_size(a) for a in axes]
    me = 0
    for a, n in zip(axes, sizes):
        me = me * n + lax.axis_index(a)
    return me, sizes


def peer_id(axes, sizes, p):
    coords = {}
    for a, n in reversed(list(zip(axes, sizes))):
        coords[a] = p % n
        p = p // n
    return coords


def exchange_kernel(jobs, *refs):
    count = len(jobs)
    src_refs, out_refs = refs[:count], refs[count : 2 * count]
    send_sem, recv_sem, local_sem = refs[2 * count :]
    places = [group_place(axes) for axes, _ in jobs]
    barrier = pltpu.get_barrier_semaphore()
    total = 0
    for (axes, _), (me, sizes), out_ref in zip(jobs, places, out_refs):
        n = out_ref.shape[0]
        total += n - 1
        for d in range(1, n):
            p = lax.rem(me + d, n)
            pl.semaphore_signal(barrier, 1, device_id=peer_id(axes, sizes, p))
    pl.semaphore_wait(barrier, total)
    copies = []
    for j, ((axes, gather), (me, sizes)) in enumerate(zip(jobs, places)):
        src_ref, out_ref = src_refs[j], out_refs[j]
        n = out_ref.shape[0]
        for d in range(1, n):
            p = lax.rem(me + d, n)
            copy = pltpu.make_async_remote_copy(
                src_ref=src_ref if gather else src_ref.at[p],
                dst_ref=out_ref.at[me],
                send_sem=send_sem.at[j, d],
                recv_sem=recv_sem.at[j, d],
                device_id=peer_id(axes, sizes, p),
            )
            copy.start()
            copies.append(copy)
        own = pltpu.make_async_copy(
            src_ref if gather else src_ref.at[me], out_ref.at[me], local_sem.at[j]
        )
        own.start()
        copies.append(own)
    for copy in copies:
        copy.wait()


def group_exchange(srcs, jobs, cid):
    shapes = []
    most = 1
    for src, (axes, gather) in zip(srcs, jobs):
        n = 1
        for a in axes:
            n *= lax.axis_size(a)
        most = max(most, n)
        block = src.shape if gather else src.shape[1:]
        shapes.append(jax.ShapeDtypeStruct((n, *block), src.dtype))
    count = len(jobs)
    return pl.pallas_call(
        functools.partial(exchange_kernel, tuple(jobs)),
        out_shape=tuple(shapes),
        in_specs=[pl.BlockSpec(memory_space=pl.ANY)] * count,
        out_specs=tuple([pl.BlockSpec(memory_space=pl.ANY)] * count),
        scratch_shapes=[
            pltpu.SemaphoreType.DMA((count, most)),
            pltpu.SemaphoreType.DMA((count, most)),
            pltpu.SemaphoreType.DMA((count,)),
        ],
        compiler_params=pltpu.CompilerParams(collective_id=cid, has_side_effects=True),
    )(*srcs)


def tree_kernel(src_ref, out_ref, send_sem, recv_sem, local_sem):
    nx, ny = lax.axis_size("x"), lax.axis_size("ylo")
    x, y = lax.axis_index("x"), lax.axis_index("ylo")
    right, left, other = lax.rem(x + 1, nx), lax.rem(x + nx - 1, nx), ny - 1 - y
    to_right, to_left, to_other = {"x": right}, {"x": left}, {"ylo": other}
    barrier = pltpu.get_barrier_semaphore()
    for peer in (to_right, to_left, to_other):
        pl.semaphore_signal(barrier, 1, device_id=peer)
    pl.semaphore_wait(barrier, 3)

    def send(kind, src, slot, peer):
        copy = pltpu.make_async_remote_copy(
            src_ref=src,
            dst_ref=out_ref.at[slot],
            send_sem=send_sem.at[kind],
            recv_sem=recv_sem.at[kind],
            device_id=peer,
        )
        copy.start()
        return copy

    me = x * ny + y
    own = pltpu.make_async_copy(src_ref, out_ref.at[me], local_sem)
    own.start()
    first_right = send(0, src_ref, me, to_right)
    first_left = send(1, src_ref, me, to_left)
    first_other = send(2, src_ref, me, to_other)
    first_right.wait_recv()
    from_left = left * ny + y
    second_right = send(3, out_ref.at[from_left], from_left, to_right)
    first_other.wait_recv()
    from_other = x * ny + other
    other_right = send(4, out_ref.at[from_other], from_other, to_right)
    other_left = send(5, out_ref.at[from_other], from_other, to_left)
    other_right.wait_recv()
    from_left_other = left * ny + other
    third_right = send(6, out_ref.at[from_left_other], from_left_other, to_right)
    for copy in (first_left, second_right, other_left, third_right):
        copy.wait_recv()
    for copy in (first_right, first_left, first_other, second_right, other_right, other_left, third_right):
        copy.wait_send()
    own.wait()


def tree_gather(src, cid):
    n = lax.axis_size("x") * lax.axis_size("ylo")
    return pl.pallas_call(
        tree_kernel,
        out_shape=jax.ShapeDtypeStruct((n, *src.shape), src.dtype),
        in_specs=[pl.BlockSpec(memory_space=pl.ANY)],
        out_specs=pl.BlockSpec(memory_space=pl.ANY),
        scratch_shapes=[
            pltpu.SemaphoreType.DMA((7,)),
            pltpu.SemaphoreType.DMA((7,)),
            pltpu.SemaphoreType.DMA,
        ],
        compiler_params=pltpu.CompilerParams(collective_id=cid, has_side_effects=True),
    )(src)


def gather_blk(rows, cid):
    half = rows.shape[0] // 2
    xy = (("x", "ylo"), True)
    first, second = group_exchange((rows[:half], rows[half:]), (xy, (("z",), True)), cid)
    first = lax.all_gather(first, "z", axis=0, tiled=False)
    second = tree_gather(second, cid + 4)
    width = rows.shape[1]
    return first.reshape(-1, BLOCK, width), second.reshape(-1, BLOCK, width)


def reduce_rep(partial, cid):
    nrep = lax.axis_size("yhi") * lax.axis_size("core")
    pieces = partial.reshape(nrep, -1, partial.shape[1])
    (pieces,) = group_exchange((pieces,), ((REP, False),), cid)
    return jnp.sum(pieces, axis=0)


def staged_index(col, per_owner):
    nz = lax.axis_size("z")
    nxy = lax.axis_size("x") * lax.axis_size("ylo")
    half = per_owner // 2
    owner = col // per_owner
    sub = col % per_owner
    z = owner % nz
    xy = owner // nz
    in_first = sub < half
    first = (z * nxy + xy) * half + jnp.where(in_first, sub, 0)
    second = (xy * nz + z) * half + jnp.where(in_first, 0, sub - half)
    return in_first.astype(jnp.int32), first, second


def products_kernel(flag_ref, first_ref, second_ref, *refs):
    adj_ref, out_ref = refs[-2:]
    rows, kq = adj_ref.shape[0], adj_ref.shape[1]
    firsts, seconds = refs[: rows * kq], refs[rows * kq : 2 * rows * kq]
    base = pl.program_id(0) * rows
    for r in range(rows):
        acc = jnp.zeros(out_ref.shape[1:], jnp.float32)
        for k in range(kq):
            at = r * kq + k
            block = jnp.where(flag_ref[base + r, k] != 0, firsts[at][0], seconds[at][0])
            acc = acc + jnp.dot(adj_ref[r, k], block, preferred_element_type=jnp.float32)
        out_ref[r] = acc


def tile_products(panels, adj_tiles, index, per_piece):
    flag, first, second = index
    rows, kq = flag.shape
    width = panels[0].shape[2]
    tile = (1, BLOCK, width)

    def pick(table, r, k):
        return pl.BlockSpec(tile, lambda g, f, a, b: (table(f, a, b)[g * per_piece + r, k], 0, 0))

    specs = [pick(lambda f, a, b: a, r, k) for r in range(per_piece) for k in range(kq)]
    specs += [pick(lambda f, a, b: b, r, k) for r in range(per_piece) for k in range(kq)]
    specs.append(pl.BlockSpec((per_piece, kq, BLOCK, BLOCK), lambda g, f, a, b: (g, 0, 0, 0)))
    out_spec = pl.BlockSpec((per_piece, BLOCK, width), lambda g, f, a, b: (g, 0, 0))
    summed = pl.pallas_call(
        products_kernel,
        out_shape=jax.ShapeDtypeStruct((rows, BLOCK, width), jnp.float32),
        grid_spec=pltpu.PrefetchScalarGridSpec(
            num_scalar_prefetch=3,
            grid=(rows // per_piece,),
            in_specs=specs,
            out_specs=out_spec,
        ),
    )(flag, first, second, *([panels[0]] * (per_piece * kq)), *([panels[1]] * (per_piece * kq)), adj_tiles[:, 0])
    return summed.reshape(-1, width)


def local(node_feats, adj_tiles, col_index, w_in, b_in, w_out, b_out, cot_out):
    per_owner = node_feats.shape[0] // BLOCK
    index = staged_index(col_index[:, 0, :], per_owner)
    per_piece = per_owner
    panels = gather_blk(node_feats, 0)
    partial_sum = tile_products(panels, adj_tiles, index, per_piece)
    agg = reduce_rep(partial_sum, 8)
    agg_b = agg.astype(jnp.bfloat16)
    pre = jnp.dot(agg_b, w_in, preferred_element_type=jnp.float32) + b_in
    hidden = jax.nn.silu(pre).astype(jnp.bfloat16)
    projected = jnp.dot(hidden, w_out, preferred_element_type=jnp.float32) + b_out
    out_feats = (node_feats.astype(jnp.float32) + projected).astype(jnp.bfloat16)
    g_hidden = jnp.einsum("nh,fh->nf", cot_out, w_out, preferred_element_type=jnp.float32)
    sigma = jax.nn.sigmoid(pre)
    g_pre = (g_hidden * sigma * (1.0 + pre * (1.0 - sigma))).astype(jnp.bfloat16)
    g_agg = jnp.einsum("nf,hf->nh", g_pre, w_in, preferred_element_type=jnp.float32).astype(
        jnp.bfloat16
    )
    g_panels = gather_blk(g_agg, 1)
    back_partial = tile_products(g_panels, adj_tiles, index, per_piece)
    back_rows = reduce_rep(back_partial, 9)
    grad_feats = (cot_out.astype(jnp.float32) + back_rows).astype(jnp.bfloat16)
    return (out_feats, grad_feats)


def solution(mesh):
    nblk = mesh.shape["blk"]
    nrep = mesh.shape["rep"]
    fine = Mesh(mesh.devices.reshape(nblk // 16, 2, 8, nrep // 2, 2), NAMES)
    rows = P(BLK + REP, None)
    placed = (
        rows,
        P(BLK, REP, None, None, None),
        P(BLK, REP, None),
        P(),
        P(),
        P(),
        P(),
        rows,
    )
    return jax.shard_map(
        local,
        mesh=fine,
        in_specs=placed,
        out_specs=(rows, rows),
        check_vma=False,
    )
```

```python
import functools

import jax
import jax.numpy as jnp
from jax import lax
from jax.experimental import pallas as pl
from jax.experimental.pallas import tpu as pltpu
from jax.sharding import Mesh
from jax.sharding import PartitionSpec as P

BLOCK = 128
NAMES = ("x", "ylo", "z", "yhi", "core")
BLK = ("x", "ylo", "z")
REP = ("yhi", "core")


def group_place(axes):
    sizes = [lax.axis_size(a) for a in axes]
    me = 0
    for a, n in zip(axes, sizes):
        me = me * n + lax.axis_index(a)
    return me, sizes


def peer_id(axes, sizes, p):
    coords = {}
    for a, n in reversed(list(zip(axes, sizes))):
        coords[a] = p % n
        p = p // n
    return coords


def exchange_kernel(jobs, *refs):
    count = len(jobs)
    src_refs, out_refs = refs[:count], refs[count : 2 * count]
    send_sem, recv_sem, local_sem = refs[2 * count :]
    places = [group_place(axes) for axes, _ in jobs]
    barrier = pltpu.get_barrier_semaphore()
    total = 0
    for (axes, _), (me, sizes), out_ref in zip(jobs, places, out_refs):
        n = out_ref.shape[0]
        total += n - 1
        for d in range(1, n):
            p = lax.rem(me + d, n)
            pl.semaphore_signal(barrier, 1, device_id=peer_id(axes, sizes, p))
    pl.semaphore_wait(barrier, total)
    copies = []
    for j, ((axes, gather), (me, sizes)) in enumerate(zip(jobs, places)):
        src_ref, out_ref = src_refs[j], out_refs[j]
        n = out_ref.shape[0]
        for d in range(1, n):
            p = lax.rem(me + d, n)
            copy = pltpu.make_async_remote_copy(
                src_ref=src_ref if gather else src_ref.at[p],
                dst_ref=out_ref.at[me],
                send_sem=send_sem.at[j, d],
                recv_sem=recv_sem.at[j, d],
                device_id=peer_id(axes, sizes, p),
            )
            copy.start()
            copies.append(copy)
        own = pltpu.make_async_copy(
            src_ref if gather else src_ref.at[me], out_ref.at[me], local_sem.at[j]
        )
        own.start()
        copies.append(own)
    for copy in copies:
        copy.wait()


def group_exchange(srcs, jobs, cid):
    shapes = []
    most = 1
    for src, (axes, gather) in zip(srcs, jobs):
        n = 1
        for a in axes:
            n *= lax.axis_size(a)
        most = max(most, n)
        block = src.shape if gather else src.shape[1:]
        shapes.append(jax.ShapeDtypeStruct((n, *block), src.dtype))
    count = len(jobs)
    return pl.pallas_call(
        functools.partial(exchange_kernel, tuple(jobs)),
        out_shape=tuple(shapes),
        in_specs=[pl.BlockSpec(memory_space=pl.ANY)] * count,
        out_specs=tuple([pl.BlockSpec(memory_space=pl.ANY)] * count),
        scratch_shapes=[
            pltpu.SemaphoreType.DMA((count, most)),
            pltpu.SemaphoreType.DMA((count, most)),
            pltpu.SemaphoreType.DMA((count,)),
        ],
        compiler_params=pltpu.CompilerParams(collective_id=cid, has_side_effects=True),
    )(*srcs)


def stage_two_kernel(ring_src, tree_src, ring_out, tree_out, send_sem, recv_sem, local_sem):
    nx, ny, nz = lax.axis_size("x"), lax.axis_size("ylo"), lax.axis_size("z")
    x, y, z = lax.axis_index("x"), lax.axis_index("ylo"), lax.axis_index("z")
    right, left, other = lax.rem(x + 1, nx), lax.rem(x + nx - 1, nx), ny - 1 - y
    to_right, to_left, to_other = {"x": right}, {"x": left}, {"ylo": other}
    up, down = {"z": lax.rem(z + 1, nz)}, {"z": lax.rem(z + nz - 1, nz)}
    barrier = pltpu.get_barrier_semaphore()
    for peer in (to_right, to_left, to_other, up, down):
        pl.semaphore_signal(barrier, 1, device_id=peer)
    pl.semaphore_wait(barrier, 5)

    def send(kind, src, dst, peer):
        copy = pltpu.make_async_remote_copy(
            src_ref=src, dst_ref=dst, send_sem=send_sem.at[kind], recv_sem=recv_sem.at[kind], device_id=peer
        )
        copy.start()
        return copy

    me = x * ny + y
    own_tree = pltpu.make_async_copy(tree_src, tree_out.at[me], local_sem.at[0])
    own_tree.start()
    own_ring = pltpu.make_async_copy(ring_src, ring_out.at[z], local_sem.at[1])
    own_ring.start()
    sent = []
    first_right = send(0, tree_src, tree_out.at[me], to_right)
    first_left = send(1, tree_src, tree_out.at[me], to_left)
    first_other = send(2, tree_src, tree_out.at[me], to_other)
    steps = nz // 2
    split = ring_src.shape[0] // 2
    ups = [send(7, ring_src, ring_out.at[z], up)]
    downs = [send(7 + steps, ring_src, ring_out.at[z], down)]

    def ring_step(s):
        below = lax.rem(z + nz - (s - 1), nz)
        above = lax.rem(z + s - 1, nz)
        ups[-1].wait_recv()
        downs[-1].wait_recv()
        if s < steps:
            ups.append(send(7 + s - 1, ring_out.at[below], ring_out.at[below], up))
            downs.append(send(7 + steps + s - 1, ring_out.at[above], ring_out.at[above], down))
        else:
            ups.append(send(7 + s - 1, ring_out.at[below, :split], ring_out.at[below, :split], up))
            downs.append(send(7 + steps + s - 1, ring_out.at[above, split:], ring_out.at[above, split:], down))

    first_right.wait_recv()
    from_left = left * ny + y
    second_right = send(3, tree_out.at[from_left], tree_out.at[from_left], to_right)
    ring_step(2)
    first_other.wait_recv()
    from_other = x * ny + other
    other_right = send(4, tree_out.at[from_other], tree_out.at[from_other], to_right)
    other_left = send(5, tree_out.at[from_other], tree_out.at[from_other], to_left)
    ring_step(3)
    other_right.wait_recv()
    from_left_other = left * ny + other
    third_right = send(6, tree_out.at[from_left_other], tree_out.at[from_left_other], to_right)
    for s in range(4, steps + 1):
        ring_step(s)
    for copy in (first_left, second_right, other_left, third_right, ups[-1], downs[-1]):
        copy.wait_recv()
    tree = [first_right, first_left, first_other, second_right, other_right, other_left, third_right]
    for copy in tree + ups + downs:
        copy.wait_send()
    own_tree.wait()
    own_ring.wait()


def stage_two(ring_src, tree_src, cid):
    nz = lax.axis_size("z")
    nxy = lax.axis_size("x") * lax.axis_size("ylo")
    return pl.pallas_call(
        stage_two_kernel,
        out_shape=(
            jax.ShapeDtypeStruct((nz, *ring_src.shape), ring_src.dtype),
            jax.ShapeDtypeStruct((nxy, *tree_src.shape), tree_src.dtype),
        ),
        in_specs=[pl.BlockSpec(memory_space=pl.ANY)] * 2,
        out_specs=(pl.BlockSpec(memory_space=pl.ANY), pl.BlockSpec(memory_space=pl.ANY)),
        scratch_shapes=[
            pltpu.SemaphoreType.DMA((7 + nz,)),
            pltpu.SemaphoreType.DMA((7 + nz,)),
            pltpu.SemaphoreType.DMA((2,)),
        ],
        compiler_params=pltpu.CompilerParams(collective_id=cid, has_side_effects=True),
    )(ring_src, tree_src)


def gather_blk(rows, cid):
    half = rows.shape[0] // 2
    xy = (("x", "ylo"), True)
    first, second = group_exchange((rows[:half], rows[half:]), (xy, (("z",), True)), cid)
    first, second = stage_two(first, second, cid + 4)
    width = rows.shape[1]
    return first.reshape(-1, BLOCK, width), second.reshape(-1, BLOCK, width)


def reduce_rep(partial, cid):
    nrep = lax.axis_size("yhi") * lax.axis_size("core")
    pieces = partial.reshape(nrep, -1, partial.shape[1])
    (pieces,) = group_exchange((pieces,), ((REP, False),), cid)
    return jnp.sum(pieces, axis=0)


def staged_index(col, per_owner):
    nz = lax.axis_size("z")
    nxy = lax.axis_size("x") * lax.axis_size("ylo")
    half = per_owner // 2
    owner = col // per_owner
    sub = col % per_owner
    z = owner % nz
    xy = owner // nz
    in_first = sub < half
    first = (z * nxy + xy) * half + jnp.where(in_first, sub, 0)
    second = (xy * nz + z) * half + jnp.where(in_first, 0, sub - half)
    return in_first.astype(jnp.int32), first, second


def products_kernel(flag_ref, first_ref, second_ref, *refs):
    adj_ref, out_ref = refs[-2:]
    rows, kq = adj_ref.shape[0], adj_ref.shape[1]
    firsts, seconds = refs[: rows * kq], refs[rows * kq : 2 * rows * kq]
    base = pl.program_id(0) * rows
    for r in range(rows):
        acc = jnp.zeros(out_ref.shape[1:], jnp.float32)
        for k in range(kq):
            at = r * kq + k
            block = jnp.where(flag_ref[base + r, k] != 0, firsts[at][0], seconds[at][0])
            acc = acc + jnp.dot(adj_ref[r, k], block, preferred_element_type=jnp.float32)
        out_ref[r] = acc


def tile_products(panels, adj_tiles, index, per_piece):
    flag, first, second = index
    rows, kq = flag.shape
    width = panels[0].shape[2]
    tile = (1, BLOCK, width)

    def pick(table, r, k):
        return pl.BlockSpec(tile, lambda g, f, a, b: (table(f, a, b)[g * per_piece + r, k], 0, 0))

    specs = [pick(lambda f, a, b: a, r, k) for r in range(per_piece) for k in range(kq)]
    specs += [pick(lambda f, a, b: b, r, k) for r in range(per_piece) for k in range(kq)]
    specs.append(pl.BlockSpec((per_piece, kq, BLOCK, BLOCK), lambda g, f, a, b: (g, 0, 0, 0)))
    out_spec = pl.BlockSpec((per_piece, BLOCK, width), lambda g, f, a, b: (g, 0, 0))
    summed = pl.pallas_call(
        products_kernel,
        out_shape=jax.ShapeDtypeStruct((rows, BLOCK, width), jnp.float32),
        grid_spec=pltpu.PrefetchScalarGridSpec(
            num_scalar_prefetch=3,
            grid=(rows // per_piece,),
            in_specs=specs,
            out_specs=out_spec,
        ),
    )(flag, first, second, *([panels[0]] * (per_piece * kq)), *([panels[1]] * (per_piece * kq)), adj_tiles[:, 0])
    return summed.reshape(-1, width)


def local(node_feats, adj_tiles, col_index, w_in, b_in, w_out, b_out, cot_out):
    per_owner = node_feats.shape[0] // BLOCK
    index = staged_index(col_index[:, 0, :], per_owner)
    per_piece = per_owner
    panels = gather_blk(node_feats, 0)
    partial_sum = tile_products(panels, adj_tiles, index, per_piece)
    agg = reduce_rep(partial_sum, 8)
    agg_b = agg.astype(jnp.bfloat16)
    pre = jnp.dot(agg_b, w_in, preferred_element_type=jnp.float32) + b_in
    hidden = jax.nn.silu(pre).astype(jnp.bfloat16)
    projected = jnp.dot(hidden, w_out, preferred_element_type=jnp.float32) + b_out
    out_feats = (node_feats.astype(jnp.float32) + projected).astype(jnp.bfloat16)
    g_hidden = jnp.einsum("nh,fh->nf", cot_out, w_out, preferred_element_type=jnp.float32)
    sigma = jax.nn.sigmoid(pre)
    g_pre = (g_hidden * sigma * (1.0 + pre * (1.0 - sigma))).astype(jnp.bfloat16)
    g_agg = jnp.einsum("nf,hf->nh", g_pre, w_in, preferred_element_type=jnp.float32).astype(
        jnp.bfloat16
    )
    g_panels = gather_blk(g_agg, 1)
    back_partial = tile_products(g_panels, adj_tiles, index, per_piece)
    back_rows = reduce_rep(back_partial, 9)
    grad_feats = (cot_out.astype(jnp.float32) + back_rows).astype(jnp.bfloat16)
    return (out_feats, grad_feats)


def solution(mesh):
    nblk = mesh.shape["blk"]
    nrep = mesh.shape["rep"]
    fine = Mesh(mesh.devices.reshape(nblk // 16, 2, 8, nrep // 2, 2), NAMES)
    rows = P(BLK + REP, None)
    placed = (
        rows,
        P(BLK, REP, None, None, None),
        P(BLK, REP, None),
        P(),
        P(),
        P(),
        P(),
        rows,
    )
    return jax.shard_map(
        local,
        mesh=fine,
        in_specs=placed,
        out_specs=(rows, rows),
        check_vma=False,
    )
```

```python
import functools

import jax
import jax.numpy as jnp
from jax import lax
from jax.experimental import pallas as pl
from jax.experimental.pallas import tpu as pltpu
from jax.sharding import Mesh
from jax.sharding import PartitionSpec as P

BLOCK = 128
NAMES = ("x", "ylo", "z", "yhi", "core")
BLK = ("x", "ylo", "z")
REP = ("yhi", "core")


def group_place(axes):
    sizes = [lax.axis_size(a) for a in axes]
    me = 0
    for a, n in zip(axes, sizes):
        me = me * n + lax.axis_index(a)
    return me, sizes


def peer_id(axes, sizes, p):
    coords = {}
    for a, n in reversed(list(zip(axes, sizes))):
        coords[a] = p % n
        p = p // n
    return coords


def exchange_kernel(jobs, *refs):
    count = len(jobs)
    src_refs, out_refs = refs[:count], refs[count : 2 * count]
    send_sem, recv_sem, local_sem = refs[2 * count :]
    places = [group_place(axes) for axes, _ in jobs]
    barrier = pltpu.get_barrier_semaphore()
    total = 0
    for (axes, _), (me, sizes), out_ref in zip(jobs, places, out_refs):
        n = out_ref.shape[0]
        total += n - 1
        for d in range(1, n):
            p = lax.rem(me + d, n)
            pl.semaphore_signal(barrier, 1, device_id=peer_id(axes, sizes, p))
    pl.semaphore_wait(barrier, total)
    copies = []
    for j, ((axes, gather), (me, sizes)) in enumerate(zip(jobs, places)):
        src_ref, out_ref = src_refs[j], out_refs[j]
        n = out_ref.shape[0]
        for d in range(1, n):
            p = lax.rem(me + d, n)
            copy = pltpu.make_async_remote_copy(
                src_ref=src_ref if gather else src_ref.at[p],
                dst_ref=out_ref.at[me],
                send_sem=send_sem.at[j, d],
                recv_sem=recv_sem.at[j, d],
                device_id=peer_id(axes, sizes, p),
            )
            copy.start()
            copies.append(copy)
        own = pltpu.make_async_copy(
            src_ref if gather else src_ref.at[me], out_ref.at[me], local_sem.at[j]
        )
        own.start()
        copies.append(own)
    for copy in copies:
        copy.wait()


def group_exchange(srcs, jobs, cid):
    shapes = []
    most = 1
    for src, (axes, gather) in zip(srcs, jobs):
        n = 1
        for a in axes:
            n *= lax.axis_size(a)
        most = max(most, n)
        block = src.shape if gather else src.shape[1:]
        shapes.append(jax.ShapeDtypeStruct((n, *block), src.dtype))
    count = len(jobs)
    return pl.pallas_call(
        functools.partial(exchange_kernel, tuple(jobs)),
        out_shape=tuple(shapes),
        in_specs=[pl.BlockSpec(memory_space=pl.ANY)] * count,
        out_specs=tuple([pl.BlockSpec(memory_space=pl.ANY)] * count),
        scratch_shapes=[
            pltpu.SemaphoreType.DMA((count, most)),
            pltpu.SemaphoreType.DMA((count, most)),
            pltpu.SemaphoreType.DMA((count,)),
        ],
        compiler_params=pltpu.CompilerParams(collective_id=cid, has_side_effects=True),
    )(*srcs)


def stage_two_kernel(ring_src, tree_src, ring_out, tree_out, send_sem, recv_sem, local_sem):
    nx, ny, nz = lax.axis_size("x"), lax.axis_size("ylo"), lax.axis_size("z")
    x, y, z = lax.axis_index("x"), lax.axis_index("ylo"), lax.axis_index("z")
    right, left, other = lax.rem(x + 1, nx), lax.rem(x + nx - 1, nx), ny - 1 - y
    to_right, to_left, to_other = {"x": right}, {"x": left}, {"ylo": other}
    up, down = {"z": lax.rem(z + 1, nz)}, {"z": lax.rem(z + nz - 1, nz)}
    barrier = pltpu.get_barrier_semaphore()
    for peer in (to_right, to_left, to_other, up, down):
        pl.semaphore_signal(barrier, 1, device_id=peer)
    pl.semaphore_wait(barrier, 5)

    def send(kind, src, dst, peer):
        copy = pltpu.make_async_remote_copy(
            src_ref=src, dst_ref=dst, send_sem=send_sem.at[kind], recv_sem=recv_sem.at[kind], device_id=peer
        )
        copy.start()
        return copy

    me = x * ny + y
    own_tree = pltpu.make_async_copy(tree_src, tree_out.at[me], local_sem.at[0])
    own_tree.start()
    own_ring = pltpu.make_async_copy(ring_src, ring_out.at[z], local_sem.at[1])
    own_ring.start()
    sent = []
    first_right = send(0, tree_src, tree_out.at[me], to_right)
    first_left = send(1, tree_src, tree_out.at[me], to_left)
    first_other = send(2, tree_src, tree_out.at[me], to_other)
    steps = nz // 2
    split = ring_src.shape[0] // 2
    ups = [send(7, ring_src, ring_out.at[z], up)]
    downs = [send(7 + steps, ring_src, ring_out.at[z], down)]

    def ring_step(s):
        below = lax.rem(z + nz - (s - 1), nz)
        above = lax.rem(z + s - 1, nz)
        ups[-1].wait_recv()
        downs[-1].wait_recv()
        if s < steps:
            ups.append(send(7 + s - 1, ring_out.at[below], ring_out.at[below], up))
            downs.append(send(7 + steps + s - 1, ring_out.at[above], ring_out.at[above], down))
        else:
            ups.append(send(7 + s - 1, ring_out.at[below, :split], ring_out.at[below, :split], up))
            downs.append(send(7 + steps + s - 1, ring_out.at[above, split:], ring_out.at[above, split:], down))

    first_right.wait_recv()
    from_left = left * ny + y
    second_right = send(3, tree_out.at[from_left], tree_out.at[from_left], to_right)
    ring_step(2)
    first_other.wait_recv()
    from_other = x * ny + other
    other_right = send(4, tree_out.at[from_other], tree_out.at[from_other], to_right)
    other_left = send(5, tree_out.at[from_other], tree_out.at[from_other], to_left)
    ring_step(3)
    other_right.wait_recv()
    from_left_other = left * ny + other
    third_right = send(6, tree_out.at[from_left_other], tree_out.at[from_left_other], to_right)
    for s in range(4, steps + 1):
        ring_step(s)
    for copy in (first_left, second_right, other_left, third_right, ups[-1], downs[-1]):
        copy.wait_recv()
    tree = [first_right, first_left, first_other, second_right, other_right, other_left, third_right]
    for copy in tree + ups + downs:
        copy.wait_send()
    own_tree.wait()
    own_ring.wait()


def stage_two(ring_src, tree_src, cid):
    nz = lax.axis_size("z")
    nxy = lax.axis_size("x") * lax.axis_size("ylo")
    return pl.pallas_call(
        stage_two_kernel,
        out_shape=(
            jax.ShapeDtypeStruct((nz, *ring_src.shape), ring_src.dtype),
            jax.ShapeDtypeStruct((nxy, *tree_src.shape), tree_src.dtype),
        ),
        in_specs=[pl.BlockSpec(memory_space=pl.ANY)] * 2,
        out_specs=(pl.BlockSpec(memory_space=pl.ANY), pl.BlockSpec(memory_space=pl.ANY)),
        scratch_shapes=[
            pltpu.SemaphoreType.DMA((7 + nz,)),
            pltpu.SemaphoreType.DMA((7 + nz,)),
            pltpu.SemaphoreType.DMA((2,)),
        ],
        compiler_params=pltpu.CompilerParams(collective_id=cid, has_side_effects=True),
    )(ring_src, tree_src)


def gather_blk(rows, cid):
    half = rows.shape[0] // 2
    second, first = stage_two(rows[half:], rows[:half], cid)
    first, second = stage_two(first, second, cid + 4)
    width = rows.shape[1]
    return first.reshape(-1, BLOCK, width), second.reshape(-1, BLOCK, width)


def reduce_rep(partial, cid):
    nrep = lax.axis_size("yhi") * lax.axis_size("core")
    pieces = partial.reshape(nrep, -1, partial.shape[1])
    (pieces,) = group_exchange((pieces,), ((REP, False),), cid)
    return jnp.sum(pieces, axis=0)


def staged_index(col, per_owner):
    nz = lax.axis_size("z")
    nxy = lax.axis_size("x") * lax.axis_size("ylo")
    half = per_owner // 2
    owner = col // per_owner
    sub = col % per_owner
    z = owner % nz
    xy = owner // nz
    in_first = sub < half
    first = (z * nxy + xy) * half + jnp.where(in_first, sub, 0)
    second = (xy * nz + z) * half + jnp.where(in_first, 0, sub - half)
    return in_first.astype(jnp.int32), first, second


def products_kernel(flag_ref, first_ref, second_ref, *refs):
    adj_ref, out_ref = refs[-2:]
    rows, kq = adj_ref.shape[0], adj_ref.shape[1]
    firsts, seconds = refs[: rows * kq], refs[rows * kq : 2 * rows * kq]
    base = pl.program_id(0) * rows
    for r in range(rows):
        acc = jnp.zeros(out_ref.shape[1:], jnp.float32)
        for k in range(kq):
            at = r * kq + k
            block = jnp.where(flag_ref[base + r, k] != 0, firsts[at][0], seconds[at][0])
            acc = acc + jnp.dot(adj_ref[r, k], block, preferred_element_type=jnp.float32)
        out_ref[r] = acc


def tile_products(panels, adj_tiles, index, per_piece):
    flag, first, second = index
    rows, kq = flag.shape
    width = panels[0].shape[2]
    tile = (1, BLOCK, width)

    def pick(table, r, k):
        return pl.BlockSpec(tile, lambda g, f, a, b: (table(f, a, b)[g * per_piece + r, k], 0, 0))

    specs = [pick(lambda f, a, b: a, r, k) for r in range(per_piece) for k in range(kq)]
    specs += [pick(lambda f, a, b: b, r, k) for r in range(per_piece) for k in range(kq)]
    specs.append(pl.BlockSpec((per_piece, kq, BLOCK, BLOCK), lambda g, f, a, b: (g, 0, 0, 0)))
    out_spec = pl.BlockSpec((per_piece, BLOCK, width), lambda g, f, a, b: (g, 0, 0))
    summed = pl.pallas_call(
        products_kernel,
        out_shape=jax.ShapeDtypeStruct((rows, BLOCK, width), jnp.float32),
        grid_spec=pltpu.PrefetchScalarGridSpec(
            num_scalar_prefetch=3,
            grid=(rows // per_piece,),
            in_specs=specs,
            out_specs=out_spec,
        ),
    )(flag, first, second, *([panels[0]] * (per_piece * kq)), *([panels[1]] * (per_piece * kq)), adj_tiles[:, 0])
    return summed.reshape(-1, width)


def local(node_feats, adj_tiles, col_index, w_in, b_in, w_out, b_out, cot_out):
    per_owner = node_feats.shape[0] // BLOCK
    index = staged_index(col_index[:, 0, :], per_owner)
    per_piece = per_owner
    panels = gather_blk(node_feats, 0)
    partial_sum = tile_products(panels, adj_tiles, index, per_piece)
    agg = reduce_rep(partial_sum, 8)
    agg_b = agg.astype(jnp.bfloat16)
    pre = jnp.dot(agg_b, w_in, preferred_element_type=jnp.float32) + b_in
    hidden = jax.nn.silu(pre).astype(jnp.bfloat16)
    projected = jnp.dot(hidden, w_out, preferred_element_type=jnp.float32) + b_out
    out_feats = (node_feats.astype(jnp.float32) + projected).astype(jnp.bfloat16)
    g_hidden = jnp.einsum("nh,fh->nf", cot_out, w_out, preferred_element_type=jnp.float32)
    sigma = jax.nn.sigmoid(pre)
    g_pre = (g_hidden * sigma * (1.0 + pre * (1.0 - sigma))).astype(jnp.bfloat16)
    g_agg = jnp.einsum("nf,hf->nh", g_pre, w_in, preferred_element_type=jnp.float32).astype(
        jnp.bfloat16
    )
    g_panels = gather_blk(g_agg, 1)
    back_partial = tile_products(g_panels, adj_tiles, index, per_piece)
    back_rows = reduce_rep(back_partial, 9)
    grad_feats = (cot_out.astype(jnp.float32) + back_rows).astype(jnp.bfloat16)
    return (out_feats, grad_feats)


def solution(mesh):
    nblk = mesh.shape["blk"]
    nrep = mesh.shape["rep"]
    fine = Mesh(mesh.devices.reshape(nblk // 16, 2, 8, nrep // 2, 2), NAMES)
    rows = P(BLK + REP, None)
    placed = (
        rows,
        P(BLK, REP, None, None, None),
        P(BLK, REP, None),
        P(),
        P(),
        P(),
        P(),
        rows,
    )
    return jax.shard_map(
        local,
        mesh=fine,
        in_specs=placed,
        out_specs=(rows, rows),
        check_vma=False,
    )
```

```python
import functools

import jax
import jax.numpy as jnp
from jax import lax
from jax.experimental import pallas as pl
from jax.experimental.pallas import tpu as pltpu
from jax.sharding import Mesh
from jax.sharding import PartitionSpec as P

BLOCK = 128
NAMES = ("x", "ylo", "z", "yhi", "core")
BLK = ("x", "ylo", "z")
REP = ("yhi", "core")


def group_place(axes):
    sizes = [lax.axis_size(a) for a in axes]
    me = 0
    for a, n in zip(axes, sizes):
        me = me * n + lax.axis_index(a)
    return me, sizes


def peer_id(axes, sizes, p):
    coords = {}
    for a, n in reversed(list(zip(axes, sizes))):
        coords[a] = p % n
        p = p // n
    return coords


def exchange_kernel(jobs, *refs):
    count = len(jobs)
    src_refs, out_refs = refs[:count], refs[count : 2 * count]
    send_sem, recv_sem, local_sem = refs[2 * count :]
    places = [group_place(axes) for axes, _ in jobs]
    barrier = pltpu.get_barrier_semaphore()
    total = 0
    for (axes, _), (me, sizes), out_ref in zip(jobs, places, out_refs):
        n = out_ref.shape[0]
        total += n - 1
        for d in range(1, n):
            p = lax.rem(me + d, n)
            pl.semaphore_signal(barrier, 1, device_id=peer_id(axes, sizes, p))
    pl.semaphore_wait(barrier, total)
    copies = []
    for j, ((axes, gather), (me, sizes)) in enumerate(zip(jobs, places)):
        src_ref, out_ref = src_refs[j], out_refs[j]
        n = out_ref.shape[0]
        for d in range(1, n):
            p = lax.rem(me + d, n)
            copy = pltpu.make_async_remote_copy(
                src_ref=src_ref if gather else src_ref.at[p],
                dst_ref=out_ref.at[me],
                send_sem=send_sem.at[j, d],
                recv_sem=recv_sem.at[j, d],
                device_id=peer_id(axes, sizes, p),
            )
            copy.start()
            copies.append(copy)
        own = pltpu.make_async_copy(
            src_ref if gather else src_ref.at[me], out_ref.at[me], local_sem.at[j]
        )
        own.start()
        copies.append(own)
    for copy in copies:
        copy.wait()


def group_exchange(srcs, jobs, cid):
    shapes = []
    most = 1
    for src, (axes, gather) in zip(srcs, jobs):
        n = 1
        for a in axes:
            n *= lax.axis_size(a)
        most = max(most, n)
        block = src.shape if gather else src.shape[1:]
        shapes.append(jax.ShapeDtypeStruct((n, *block), src.dtype))
    count = len(jobs)
    return pl.pallas_call(
        functools.partial(exchange_kernel, tuple(jobs)),
        out_shape=tuple(shapes),
        in_specs=[pl.BlockSpec(memory_space=pl.ANY)] * count,
        out_specs=tuple([pl.BlockSpec(memory_space=pl.ANY)] * count),
        scratch_shapes=[
            pltpu.SemaphoreType.DMA((count, most)),
            pltpu.SemaphoreType.DMA((count, most)),
            pltpu.SemaphoreType.DMA((count,)),
        ],
        compiler_params=pltpu.CompilerParams(collective_id=cid, has_side_effects=True),
    )(*srcs)


def stage_two_kernel(halves, *refs):
    if halves:
        rows_ref = refs[0]
        half = rows_ref.shape[0] // 2
        ring_src, tree_src = rows_ref.at[pl.ds(half, half)], rows_ref.at[pl.ds(0, half)]
        refs = refs[1:]
    else:
        ring_src, tree_src = refs[:2]
        refs = refs[2:]
    ring_out, tree_out, send_sem, recv_sem, local_sem = refs
    stage_two_body(ring_src, tree_src, ring_out, tree_out, send_sem, recv_sem, local_sem)


def stage_two_body(ring_src, tree_src, ring_out, tree_out, send_sem, recv_sem, local_sem):
    nx, ny, nz = lax.axis_size("x"), lax.axis_size("ylo"), lax.axis_size("z")
    x, y, z = lax.axis_index("x"), lax.axis_index("ylo"), lax.axis_index("z")
    right, left, other = lax.rem(x + 1, nx), lax.rem(x + nx - 1, nx), ny - 1 - y
    to_right, to_left, to_other = {"x": right}, {"x": left}, {"ylo": other}
    up, down = {"z": lax.rem(z + 1, nz)}, {"z": lax.rem(z + nz - 1, nz)}
    barrier = pltpu.get_barrier_semaphore()
    for peer in (to_right, to_left, to_other, up, down):
        pl.semaphore_signal(barrier, 1, device_id=peer)
    pl.semaphore_wait(barrier, 5)

    def send(kind, src, dst, peer):
        copy = pltpu.make_async_remote_copy(
            src_ref=src, dst_ref=dst, send_sem=send_sem.at[kind], recv_sem=recv_sem.at[kind], device_id=peer
        )
        copy.start()
        return copy

    me = x * ny + y
    own_tree = pltpu.make_async_copy(tree_src, tree_out.at[me], local_sem.at[0])
    own_tree.start()
    own_ring = pltpu.make_async_copy(ring_src, ring_out.at[z], local_sem.at[1])
    own_ring.start()
    sent = []
    first_right = send(0, tree_src, tree_out.at[me], to_right)
    first_left = send(1, tree_src, tree_out.at[me], to_left)
    first_other = send(2, tree_src, tree_out.at[me], to_other)
    steps = nz // 2
    split = ring_src.shape[0] // 2
    ups = [send(7, ring_src, ring_out.at[z], up)]
    downs = [send(7 + steps, ring_src, ring_out.at[z], down)]

    def ring_step(s):
        below = lax.rem(z + nz - (s - 1), nz)
        above = lax.rem(z + s - 1, nz)
        ups[-1].wait_recv()
        downs[-1].wait_recv()
        if s < steps:
            ups.append(send(7 + s - 1, ring_out.at[below], ring_out.at[below], up))
            downs.append(send(7 + steps + s - 1, ring_out.at[above], ring_out.at[above], down))
        else:
            ups.append(send(7 + s - 1, ring_out.at[below, :split], ring_out.at[below, :split], up))
            downs.append(send(7 + steps + s - 1, ring_out.at[above, split:], ring_out.at[above, split:], down))

    first_right.wait_recv()
    from_left = left * ny + y
    second_right = send(3, tree_out.at[from_left], tree_out.at[from_left], to_right)
    ring_step(2)
    first_other.wait_recv()
    from_other = x * ny + other
    other_right = send(4, tree_out.at[from_other], tree_out.at[from_other], to_right)
    other_left = send(5, tree_out.at[from_other], tree_out.at[from_other], to_left)
    ring_step(3)
    other_right.wait_recv()
    from_left_other = left * ny + other
    third_right = send(6, tree_out.at[from_left_other], tree_out.at[from_left_other], to_right)
    for s in range(4, steps + 1):
        ring_step(s)
    for copy in (first_left, second_right, other_left, third_right, ups[-1], downs[-1]):
        copy.wait_recv()
    tree = [first_right, first_left, first_other, second_right, other_right, other_left, third_right]
    for copy in tree + ups + downs:
        copy.wait_send()
    own_tree.wait()
    own_ring.wait()


def stage_two(srcs, cid):
    nz = lax.axis_size("z")
    nxy = lax.axis_size("x") * lax.axis_size("ylo")
    if len(srcs) == 1:
        half = srcs[0].shape[0] // 2
        ring_shape = tree_shape = (half, *srcs[0].shape[1:])
    else:
        ring_shape, tree_shape = srcs[0].shape, srcs[1].shape
    dtype = srcs[0].dtype
    return pl.pallas_call(
        functools.partial(stage_two_kernel, len(srcs) == 1),
        out_shape=(
            jax.ShapeDtypeStruct((nz, *ring_shape), dtype),
            jax.ShapeDtypeStruct((nxy, *tree_shape), dtype),
        ),
        in_specs=[pl.BlockSpec(memory_space=pl.ANY)] * len(srcs),
        out_specs=(pl.BlockSpec(memory_space=pl.ANY), pl.BlockSpec(memory_space=pl.ANY)),
        scratch_shapes=[
            pltpu.SemaphoreType.DMA((7 + nz,)),
            pltpu.SemaphoreType.DMA((7 + nz,)),
            pltpu.SemaphoreType.DMA((2,)),
        ],
        compiler_params=pltpu.CompilerParams(collective_id=cid, has_side_effects=True),
    )(*srcs)


def gather_blk(rows, cid):
    second, first = stage_two((rows,), cid)
    first, second = stage_two((first, second), cid + 4)
    width = rows.shape[1]
    return first.reshape(-1, BLOCK, width), second.reshape(-1, BLOCK, width)


def reduce_kernel(src_ref, out_ref, landed, send_sem, recv_sem, local_sem):
    me, sizes = group_place(REP)
    n = landed.shape[0]
    barrier = pltpu.get_barrier_semaphore()
    for d in range(1, n):
        pl.semaphore_signal(barrier, 1, device_id=peer_id(REP, sizes, lax.rem(me + d, n)))
    pl.semaphore_wait(barrier, n - 1)
    copies = []
    for d in range(1, n):
        p = lax.rem(me + d, n)
        copy = pltpu.make_async_remote_copy(
            src_ref=src_ref.at[p],
            dst_ref=landed.at[me],
            send_sem=send_sem.at[d],
            recv_sem=recv_sem.at[d],
            device_id=peer_id(REP, sizes, p),
        )
        copy.start()
        copies.append(copy)
    own = pltpu.make_async_copy(src_ref.at[me], landed.at[me], local_sem)
    own.start()
    for copy in copies:
        copy.wait()
    own.wait()
    total = landed[0]
    for slot in range(1, n):
        total = total + landed[slot]
    out_ref[...] = total


def reduce_rep(partial, cid):
    nrep = lax.axis_size("yhi") * lax.axis_size("core")
    pieces = partial.reshape(nrep, -1, partial.shape[1])
    return pl.pallas_call(
        reduce_kernel,
        out_shape=jax.ShapeDtypeStruct(pieces.shape[1:], pieces.dtype),
        in_specs=[pl.BlockSpec(memory_space=pl.ANY)],
        out_specs=pl.BlockSpec(memory_space=pltpu.VMEM),
        scratch_shapes=[
            pltpu.VMEM(pieces.shape, pieces.dtype),
            pltpu.SemaphoreType.DMA((nrep,)),
            pltpu.SemaphoreType.DMA((nrep,)),
            pltpu.SemaphoreType.DMA,
        ],
        compiler_params=pltpu.CompilerParams(collective_id=cid, has_side_effects=True),
    )(pieces)


def block_of(col, per_owner, nz, nxy):
    half = per_owner // 2
    owner = col // per_owner
    sub = col % per_owner
    z = owner % nz
    xy = owner // nz
    in_first = sub < half
    first = (z * nxy + xy) * half + jnp.where(in_first, sub, 0)
    second = (xy * nz + z) * half + jnp.where(in_first, 0, sub - half)
    return in_first, first, second


def products_kernel(layout, col_ref, *refs):
    adj_ref, out_ref = refs[-2:]
    rows, kq = adj_ref.shape[0], adj_ref.shape[1]
    firsts, seconds = refs[: rows * kq], refs[rows * kq : 2 * rows * kq]
    base = pl.program_id(0) * rows
    for r in range(rows):
        acc = jnp.zeros(out_ref.shape[1:], jnp.float32)
        for k in range(kq):
            at = r * kq + k
            in_first = block_of(col_ref[base + r, k], *layout)[0]
            block = jnp.where(in_first, firsts[at][0], seconds[at][0])
            acc = acc + jnp.dot(adj_ref[r, k], block, preferred_element_type=jnp.float32)
        out_ref[r] = acc


def tile_products(panels, adj_tiles, col, per_piece):
    rows, kq = col.shape
    width = panels[0].shape[2]
    tile = (1, BLOCK, width)
    layout = (panels[0].shape[0] * 2 // lax.axis_size(BLK), lax.axis_size("z"),
              lax.axis_size("x") * lax.axis_size("ylo"))

    def pick(which, r, k):
        return pl.BlockSpec(
            tile, lambda g, c: (block_of(c[g * per_piece + r, k], *layout)[which], 0, 0)
        )

    specs = [pick(1, r, k) for r in range(per_piece) for k in range(kq)]
    specs += [pick(2, r, k) for r in range(per_piece) for k in range(kq)]
    specs.append(pl.BlockSpec((per_piece, kq, BLOCK, BLOCK), lambda g, c: (g, 0, 0, 0)))
    summed = pl.pallas_call(
        functools.partial(products_kernel, layout),
        out_shape=jax.ShapeDtypeStruct((rows, BLOCK, width), jnp.float32),
        grid_spec=pltpu.PrefetchScalarGridSpec(
            num_scalar_prefetch=1,
            grid=(rows // per_piece,),
            in_specs=specs,
            out_specs=pl.BlockSpec((per_piece, BLOCK, width), lambda g, c: (g, 0, 0)),
        ),
    )(col, *([panels[0]] * (per_piece * kq)), *([panels[1]] * (per_piece * kq)), adj_tiles[:, 0])
    return summed.reshape(-1, width)


def local(node_feats, adj_tiles, col_index, w_in, b_in, w_out, b_out, cot_out):
    per_piece = node_feats.shape[0] // BLOCK
    index = col_index.reshape(col_index.shape[0], -1)
    panels = gather_blk(node_feats, 0)
    partial_sum = tile_products(panels, adj_tiles, index, per_piece)
    agg = reduce_rep(partial_sum, 8)
    agg_b = agg.astype(jnp.bfloat16)
    pre = jnp.dot(agg_b, w_in, preferred_element_type=jnp.float32) + b_in
    hidden = jax.nn.silu(pre).astype(jnp.bfloat16)
    projected = jnp.dot(hidden, w_out, preferred_element_type=jnp.float32) + b_out
    out_feats = (node_feats.astype(jnp.float32) + projected).astype(jnp.bfloat16)
    g_hidden = jnp.einsum("nh,fh->nf", cot_out, w_out, preferred_element_type=jnp.float32)
    sigma = jax.nn.sigmoid(pre)
    g_pre = (g_hidden * sigma * (1.0 + pre * (1.0 - sigma))).astype(jnp.bfloat16)
    g_agg = jnp.einsum("nf,hf->nh", g_pre, w_in, preferred_element_type=jnp.float32).astype(
        jnp.bfloat16
    )
    g_panels = gather_blk(g_agg, 1)
    back_partial = tile_products(g_panels, adj_tiles, index, per_piece)
    back_rows = reduce_rep(back_partial, 9)
    grad_feats = (cot_out.astype(jnp.float32) + back_rows).astype(jnp.bfloat16)
    return (out_feats, grad_feats)


def solution(mesh):
    nblk = mesh.shape["blk"]
    nrep = mesh.shape["rep"]
    fine = Mesh(mesh.devices.reshape(nblk // 16, 2, 8, nrep // 2, 2), NAMES)
    rows = P(BLK + REP, None)
    placed = (
        rows,
        P(BLK, REP, None, None, None),
        P(BLK, REP, None),
        P(),
        P(),
        P(),
        P(),
        rows,
    )
    return jax.shard_map(
        local,
        mesh=fine,
        in_specs=placed,
        out_specs=(rows, rows),
        check_vma=False,
    )
```

```python
import functools

import jax
import jax.numpy as jnp
from jax import lax
from jax.experimental import pallas as pl
from jax.experimental.pallas import tpu as pltpu
from jax.sharding import Mesh
from jax.sharding import PartitionSpec as P

BLOCK = 128
NAMES = ("x", "ylo", "z", "yhi", "core")
BLK = ("x", "ylo", "z")
REP = ("yhi", "core")


def group_place(axes):
    sizes = [lax.axis_size(a) for a in axes]
    me = 0
    for a, n in zip(axes, sizes):
        me = me * n + lax.axis_index(a)
    return me, sizes


def peer_id(axes, sizes, p):
    coords = {}
    for a, n in reversed(list(zip(axes, sizes))):
        coords[a] = p % n
        p = p // n
    return coords


def exchange_kernel(jobs, *refs):
    count = len(jobs)
    src_refs, out_refs = refs[:count], refs[count : 2 * count]
    send_sem, recv_sem, local_sem = refs[2 * count :]
    places = [group_place(axes) for axes, _ in jobs]
    barrier = pltpu.get_barrier_semaphore()
    total = 0
    for (axes, _), (me, sizes), out_ref in zip(jobs, places, out_refs):
        n = out_ref.shape[0]
        total += n - 1
        for d in range(1, n):
            p = lax.rem(me + d, n)
            pl.semaphore_signal(barrier, 1, device_id=peer_id(axes, sizes, p))
    pl.semaphore_wait(barrier, total)
    copies = []
    for j, ((axes, gather), (me, sizes)) in enumerate(zip(jobs, places)):
        src_ref, out_ref = src_refs[j], out_refs[j]
        n = out_ref.shape[0]
        for d in range(1, n):
            p = lax.rem(me + d, n)
            copy = pltpu.make_async_remote_copy(
                src_ref=src_ref if gather else src_ref.at[p],
                dst_ref=out_ref.at[me],
                send_sem=send_sem.at[j, d],
                recv_sem=recv_sem.at[j, d],
                device_id=peer_id(axes, sizes, p),
            )
            copy.start()
            copies.append(copy)
        own = pltpu.make_async_copy(
            src_ref if gather else src_ref.at[me], out_ref.at[me], local_sem.at[j]
        )
        own.start()
        copies.append(own)
    for copy in copies:
        copy.wait()


def group_exchange(srcs, jobs, cid):
    shapes = []
    most = 1
    for src, (axes, gather) in zip(srcs, jobs):
        n = 1
        for a in axes:
            n *= lax.axis_size(a)
        most = max(most, n)
        block = src.shape if gather else src.shape[1:]
        shapes.append(jax.ShapeDtypeStruct((n, *block), src.dtype))
    count = len(jobs)
    return pl.pallas_call(
        functools.partial(exchange_kernel, tuple(jobs)),
        out_shape=tuple(shapes),
        in_specs=[pl.BlockSpec(memory_space=pl.ANY)] * count,
        out_specs=tuple([pl.BlockSpec(memory_space=pl.ANY)] * count),
        scratch_shapes=[
            pltpu.SemaphoreType.DMA((count, most)),
            pltpu.SemaphoreType.DMA((count, most)),
            pltpu.SemaphoreType.DMA((count,)),
        ],
        compiler_params=pltpu.CompilerParams(collective_id=cid, has_side_effects=True),
    )(*srcs)


def stage_two_kernel(halves, *refs):
    if halves:
        rows_ref = refs[0]
        half = rows_ref.shape[0] // 2
        ring_src, tree_src = rows_ref.at[pl.ds(half, half)], rows_ref.at[pl.ds(0, half)]
        refs = refs[1:]
    else:
        ring_src, tree_src = refs[:2]
        refs = refs[2:]
    ring_out, tree_out, send_sem, recv_sem, local_sem = refs
    stage_two_body(ring_src, tree_src, ring_out, tree_out, send_sem, recv_sem, local_sem)


def stage_two_body(ring_src, tree_src, ring_out, tree_out, send_sem, recv_sem, local_sem):
    nx, ny, nz = lax.axis_size("x"), lax.axis_size("ylo"), lax.axis_size("z")
    x, y, z = lax.axis_index("x"), lax.axis_index("ylo"), lax.axis_index("z")
    right, left, other = lax.rem(x + 1, nx), lax.rem(x + nx - 1, nx), ny - 1 - y
    to_right, to_left, to_other = {"x": right}, {"x": left}, {"ylo": other}
    up, down = {"z": lax.rem(z + 1, nz)}, {"z": lax.rem(z + nz - 1, nz)}
    barrier = pltpu.get_barrier_semaphore()
    for peer in (to_right, to_left, to_other, up, down):
        pl.semaphore_signal(barrier, 1, device_id=peer)
    pl.semaphore_wait(barrier, 5)

    def send(kind, src, dst, peer):
        copy = pltpu.make_async_remote_copy(
            src_ref=src, dst_ref=dst, send_sem=send_sem.at[kind], recv_sem=recv_sem.at[kind], device_id=peer
        )
        copy.start()
        return copy

    me = x * ny + y
    own_tree = pltpu.make_async_copy(tree_src, tree_out.at[me], local_sem.at[0])
    own_tree.start()
    own_ring = pltpu.make_async_copy(ring_src, ring_out.at[z], local_sem.at[1])
    own_ring.start()
    sent = []
    first_right = send(0, tree_src, tree_out.at[me], to_right)
    first_left = send(1, tree_src, tree_out.at[me], to_left)
    first_other = send(2, tree_src, tree_out.at[me], to_other)
    steps = nz // 2
    split = ring_src.shape[0] // 2
    ups = [send(7, ring_src, ring_out.at[z], up)]
    downs = [send(7 + steps, ring_src, ring_out.at[z], down)]

    def ring_step(s):
        below = lax.rem(z + nz - (s - 1), nz)
        above = lax.rem(z + s - 1, nz)
        ups[-1].wait_recv()
        downs[-1].wait_recv()
        if s < steps:
            ups.append(send(7 + s - 1, ring_out.at[below], ring_out.at[below], up))
            downs.append(send(7 + steps + s - 1, ring_out.at[above], ring_out.at[above], down))
        else:
            ups.append(send(7 + s - 1, ring_out.at[below, :split], ring_out.at[below, :split], up))
            downs.append(send(7 + steps + s - 1, ring_out.at[above, split:], ring_out.at[above, split:], down))

    first_right.wait_recv()
    from_left = left * ny + y
    second_right = send(3, tree_out.at[from_left], tree_out.at[from_left], to_right)
    ring_step(2)
    first_other.wait_recv()
    from_other = x * ny + other
    other_right = send(4, tree_out.at[from_other], tree_out.at[from_other], to_right)
    other_left = send(5, tree_out.at[from_other], tree_out.at[from_other], to_left)
    ring_step(3)
    other_right.wait_recv()
    from_left_other = left * ny + other
    third_right = send(6, tree_out.at[from_left_other], tree_out.at[from_left_other], to_right)
    for s in range(4, steps + 1):
        ring_step(s)
    for copy in (first_left, second_right, other_left, third_right, ups[-1], downs[-1]):
        copy.wait_recv()
    tree = [first_right, first_left, first_other, second_right, other_right, other_left, third_right]
    for copy in tree + ups + downs:
        copy.wait_send()
    own_tree.wait()
    own_ring.wait()


def stage_two(srcs, cid):
    nz = lax.axis_size("z")
    nxy = lax.axis_size("x") * lax.axis_size("ylo")
    if len(srcs) == 1:
        half = srcs[0].shape[0] // 2
        ring_shape = tree_shape = (half, *srcs[0].shape[1:])
    else:
        ring_shape, tree_shape = srcs[0].shape, srcs[1].shape
    dtype = srcs[0].dtype
    return pl.pallas_call(
        functools.partial(stage_two_kernel, len(srcs) == 1),
        out_shape=(
            jax.ShapeDtypeStruct((nz, *ring_shape), dtype),
            jax.ShapeDtypeStruct((nxy, *tree_shape), dtype),
        ),
        in_specs=[pl.BlockSpec(memory_space=pl.ANY)] * len(srcs),
        out_specs=(pl.BlockSpec(memory_space=pl.ANY), pl.BlockSpec(memory_space=pl.ANY)),
        scratch_shapes=[
            pltpu.SemaphoreType.DMA((7 + nz,)),
            pltpu.SemaphoreType.DMA((7 + nz,)),
            pltpu.SemaphoreType.DMA((2,)),
        ],
        compiler_params=pltpu.CompilerParams(collective_id=cid, has_side_effects=True),
    )(*srcs)


def gather_blk(rows, cid):
    second, first = stage_two((rows,), cid)
    first, second = stage_two((first, second), cid + 4)
    width = rows.shape[1]
    return first.reshape(-1, BLOCK, width), second.reshape(-1, BLOCK, width)


def reduce_kernel(src_ref, out_ref, landed, send_sem, recv_sem, local_sem):
    me, sizes = group_place(REP)
    n = landed.shape[0]
    barrier = pltpu.get_barrier_semaphore()
    for d in range(1, n):
        pl.semaphore_signal(barrier, 1, device_id=peer_id(REP, sizes, lax.rem(me + d, n)))
    pl.semaphore_wait(barrier, n - 1)
    copies = []
    for d in range(1, n):
        p = lax.rem(me + d, n)
        copy = pltpu.make_async_remote_copy(
            src_ref=src_ref.at[p],
            dst_ref=landed.at[me],
            send_sem=send_sem.at[d],
            recv_sem=recv_sem.at[d],
            device_id=peer_id(REP, sizes, p),
        )
        copy.start()
        copies.append(copy)
    own = pltpu.make_async_copy(src_ref.at[me], landed.at[me], local_sem)
    own.start()
    for copy in copies:
        copy.wait()
    own.wait()
    total = landed[0]
    for slot in range(1, n):
        total = total + landed[slot]
    out_ref[...] = total


def reduce_rep(partial, cid):
    nrep = lax.axis_size("yhi") * lax.axis_size("core")
    pieces = partial.reshape(nrep, -1, partial.shape[1])
    return pl.pallas_call(
        reduce_kernel,
        out_shape=jax.ShapeDtypeStruct(pieces.shape[1:], pieces.dtype),
        in_specs=[pl.BlockSpec(memory_space=pl.ANY)],
        out_specs=pl.BlockSpec(memory_space=pltpu.VMEM),
        scratch_shapes=[
            pltpu.VMEM(pieces.shape, pieces.dtype),
            pltpu.SemaphoreType.DMA((nrep,)),
            pltpu.SemaphoreType.DMA((nrep,)),
            pltpu.SemaphoreType.DMA,
        ],
        compiler_params=pltpu.CompilerParams(collective_id=cid, has_side_effects=True),
    )(pieces)


def staged_index(col, per_owner):
    nz = lax.axis_size("z")
    nxy = lax.axis_size("x") * lax.axis_size("ylo")
    half = per_owner // 2
    owner = col // per_owner
    sub = col % per_owner
    z = owner % nz
    xy = owner // nz
    in_first = sub < half
    first = (z * nxy + xy) * half + jnp.where(in_first, sub, 0)
    second = (xy * nz + z) * half + jnp.where(in_first, 0, sub - half)
    return in_first.astype(jnp.int32), first, second


def products_kernel(flag_ref, first_ref, second_ref, *refs):
    adj_ref, out_ref = refs[-2:]
    rows, kq = adj_ref.shape[0], adj_ref.shape[1]
    firsts, seconds = refs[: rows * kq], refs[rows * kq : 2 * rows * kq]
    base = pl.program_id(0) * rows
    for r in range(rows):
        acc = jnp.zeros(out_ref.shape[1:], jnp.float32)
        for k in range(kq):
            at = r * kq + k
            block = jnp.where(flag_ref[base + r, k] != 0, firsts[at][0], seconds[at][0])
            acc = acc + jnp.dot(adj_ref[r, k], block, preferred_element_type=jnp.float32)
        out_ref[r] = acc


def tile_products(panels, adj_tiles, index, per_piece):
    flag, first, second = index
    rows, kq = flag.shape
    width = panels[0].shape[2]
    tile = (1, BLOCK, width)

    def pick(table, r, k):
        return pl.BlockSpec(tile, lambda g, f, a, b: (table(f, a, b)[g * per_piece + r, k], 0, 0))

    specs = [pick(lambda f, a, b: a, r, k) for r in range(per_piece) for k in range(kq)]
    specs += [pick(lambda f, a, b: b, r, k) for r in range(per_piece) for k in range(kq)]
    specs.append(pl.BlockSpec((per_piece, kq, BLOCK, BLOCK), lambda g, f, a, b: (g, 0, 0, 0)))
    out_spec = pl.BlockSpec((per_piece, BLOCK, width), lambda g, f, a, b: (g, 0, 0))
    summed = pl.pallas_call(
        products_kernel,
        out_shape=jax.ShapeDtypeStruct((rows, BLOCK, width), jnp.float32),
        grid_spec=pltpu.PrefetchScalarGridSpec(
            num_scalar_prefetch=3,
            grid=(rows // per_piece,),
            in_specs=specs,
            out_specs=out_spec,
        ),
    )(flag, first, second, *([panels[0]] * (per_piece * kq)), *([panels[1]] * (per_piece * kq)), adj_tiles[:, 0])
    return summed.reshape(-1, width)


def local(node_feats, adj_tiles, col_index, w_in, b_in, w_out, b_out, cot_out):
    per_piece = node_feats.shape[0] // BLOCK
    index = staged_index(col_index[:, 0, :], per_piece)
    panels = gather_blk(node_feats, 0)
    partial_sum = tile_products(panels, adj_tiles, index, per_piece)
    agg = reduce_rep(partial_sum, 8)
    agg_b = agg.astype(jnp.bfloat16)
    pre = jnp.dot(agg_b, w_in, preferred_element_type=jnp.float32) + b_in
    hidden = jax.nn.silu(pre).astype(jnp.bfloat16)
    projected = jnp.dot(hidden, w_out, preferred_element_type=jnp.float32) + b_out
    out_feats = (node_feats.astype(jnp.float32) + projected).astype(jnp.bfloat16)
    g_hidden = jnp.einsum("nh,fh->nf", cot_out, w_out, preferred_element_type=jnp.float32)
    sigma = jax.nn.sigmoid(pre)
    g_pre = (g_hidden * sigma * (1.0 + pre * (1.0 - sigma))).astype(jnp.bfloat16)
    g_agg = jnp.einsum("nf,hf->nh", g_pre, w_in, preferred_element_type=jnp.float32).astype(
        jnp.bfloat16
    )
    g_panels = gather_blk(g_agg, 1)
    back_partial = tile_products(g_panels, adj_tiles, index, per_piece)
    back_rows = reduce_rep(back_partial, 9)
    grad_feats = (cot_out.astype(jnp.float32) + back_rows).astype(jnp.bfloat16)
    return (out_feats, grad_feats)


def solution(mesh):
    nblk = mesh.shape["blk"]
    nrep = mesh.shape["rep"]
    fine = Mesh(mesh.devices.reshape(nblk // 16, 2, 8, nrep // 2, 2), NAMES)
    rows = P(BLK + REP, None)
    placed = (
        rows,
        P(BLK, REP, None, None, None),
        P(BLK, REP, None),
        P(),
        P(),
        P(),
        P(),
        rows,
    )
    return jax.shard_map(
        local,
        mesh=fine,
        in_specs=placed,
        out_specs=(rows, rows),
        check_vma=False,
    )
```

```python
import functools

import jax
import jax.numpy as jnp
from jax import lax
from jax.experimental import pallas as pl
from jax.experimental.pallas import tpu as pltpu
from jax.sharding import Mesh
from jax.sharding import PartitionSpec as P

BLOCK = 128
NAMES = ("x", "ylo", "z", "yhi", "core")
BLK = ("x", "ylo", "z")
REP = ("yhi", "core")


def group_place(axes):
    sizes = [lax.axis_size(a) for a in axes]
    me = 0
    for a, n in zip(axes, sizes):
        me = me * n + lax.axis_index(a)
    return me, sizes


def peer_id(axes, sizes, p):
    coords = {}
    for a, n in reversed(list(zip(axes, sizes))):
        coords[a] = p % n
        p = p // n
    return coords


def neighbours():
    nx, ny, nz = lax.axis_size("x"), lax.axis_size("ylo"), lax.axis_size("z")
    x, y, z = lax.axis_index("x"), lax.axis_index("ylo"), lax.axis_index("z")
    right, left, other = lax.rem(x + 1, nx), lax.rem(x + nx - 1, nx), ny - 1 - y
    return {"x": right}, {"x": left}, {"ylo": other}, {"z": lax.rem(z + 1, nz)}, {"z": lax.rem(z + nz - 1, nz)}


def gather_phase(phase, ring_src, tree_src, ring_out, tree_out, send_sem, recv_sem, local_sem):
    nx, ny, nz = lax.axis_size("x"), lax.axis_size("ylo"), lax.axis_size("z")
    x, y, z = lax.axis_index("x"), lax.axis_index("ylo"), lax.axis_index("z")
    left, other = lax.rem(x + nx - 1, nx), ny - 1 - y
    to_right, to_left, to_other, up, down = neighbours()

    def send(kind, src, dst, peer):
        copy = pltpu.make_async_remote_copy(
            src_ref=src,
            dst_ref=dst,
            send_sem=send_sem.at[phase, kind],
            recv_sem=recv_sem.at[phase, kind],
            device_id=peer,
        )
        copy.start()
        return copy

    me = x * ny + y
    own_tree = pltpu.make_async_copy(tree_src, tree_out.at[me], local_sem.at[phase, 0])
    own_tree.start()
    own_ring = pltpu.make_async_copy(ring_src, ring_out.at[z], local_sem.at[phase, 1])
    own_ring.start()
    first_right = send(0, tree_src, tree_out.at[me], to_right)
    first_left = send(1, tree_src, tree_out.at[me], to_left)
    first_other = send(2, tree_src, tree_out.at[me], to_other)
    steps = nz // 2
    split = ring_src.shape[0] // 2
    ups = [send(7, ring_src, ring_out.at[z], up)]
    downs = [send(7 + steps, ring_src, ring_out.at[z], down)]

    def ring_step(s):
        below = lax.rem(z + nz - (s - 1), nz)
        above = lax.rem(z + s - 1, nz)
        ups[-1].wait_recv()
        downs[-1].wait_recv()
        if s < steps:
            ups.append(send(7 + s - 1, ring_out.at[below], ring_out.at[below], up))
            downs.append(send(7 + steps + s - 1, ring_out.at[above], ring_out.at[above], down))
        else:
            ups.append(send(7 + s - 1, ring_out.at[below, :split], ring_out.at[below, :split], up))
            downs.append(send(7 + steps + s - 1, ring_out.at[above, split:], ring_out.at[above, split:], down))

    first_right.wait_recv()
    from_left = left * ny + y
    second_right = send(3, tree_out.at[from_left], tree_out.at[from_left], to_right)
    ring_step(2)
    first_other.wait_recv()
    from_other = x * ny + other
    other_right = send(4, tree_out.at[from_other], tree_out.at[from_other], to_right)
    other_left = send(5, tree_out.at[from_other], tree_out.at[from_other], to_left)
    ring_step(3)
    other_right.wait_recv()
    from_left_other = left * ny + other
    third_right = send(6, tree_out.at[from_left_other], tree_out.at[from_left_other], to_right)
    for s in range(4, steps + 1):
        ring_step(s)
    for copy in (first_left, second_right, other_left, third_right, ups[-1], downs[-1]):
        copy.wait_recv()
    tree = [first_right, first_left, first_other, second_right, other_right, other_left, third_right]
    return tree + ups + downs, [own_tree, own_ring]


def gather_kernel(rows_ref, mid_ring, mid_tree, ring_out, tree_out, send_sem, recv_sem, local_sem):
    barrier = pltpu.get_barrier_semaphore()
    peers = neighbours()
    for peer in peers:
        pl.semaphore_signal(barrier, 1, device_id=peer)
    pl.semaphore_wait(barrier, len(peers))
    half = rows_ref.shape[0] // 2
    ring_src, tree_src = rows_ref.at[pl.ds(half, half)], rows_ref.at[pl.ds(0, half)]
    sends, local = gather_phase(0, ring_src, tree_src, mid_ring, mid_tree, send_sem, recv_sem, local_sem)
    for copy in local:
        copy.wait()
    more, local = gather_phase(1, mid_tree, mid_ring, ring_out, tree_out, send_sem, recv_sem, local_sem)
    for copy in sends + more:
        copy.wait_send()
    for copy in local:
        copy.wait()


def gather_blk(rows, cid):
    nz = lax.axis_size("z")
    nxy = lax.axis_size("x") * lax.axis_size("ylo")
    half = rows.shape[0] // 2
    width = rows.shape[1]
    piece = (half, width)
    any_space = pl.BlockSpec(memory_space=pl.ANY)
    _, _, first, second = pl.pallas_call(
        gather_kernel,
        out_shape=(
            jax.ShapeDtypeStruct((nz, *piece), rows.dtype),
            jax.ShapeDtypeStruct((nxy, *piece), rows.dtype),
            jax.ShapeDtypeStruct((nz, nxy, *piece), rows.dtype),
            jax.ShapeDtypeStruct((nxy, nz, *piece), rows.dtype),
        ),
        in_specs=[any_space],
        out_specs=(any_space,) * 4,
        scratch_shapes=[
            pltpu.SemaphoreType.DMA((2, 7 + nz)),
            pltpu.SemaphoreType.DMA((2, 7 + nz)),
            pltpu.SemaphoreType.DMA((2, 2)),
        ],
        compiler_params=pltpu.CompilerParams(collective_id=cid, has_side_effects=True),
    )(rows)
    return first.reshape(-1, BLOCK, width), second.reshape(-1, BLOCK, width)


def reduce_kernel(src_ref, out_ref, landed, send_sem, recv_sem, local_sem):
    me, sizes = group_place(REP)
    n = landed.shape[0]
    barrier = pltpu.get_barrier_semaphore()
    for d in range(1, n):
        pl.semaphore_signal(barrier, 1, device_id=peer_id(REP, sizes, lax.rem(me + d, n)))
    pl.semaphore_wait(barrier, n - 1)
    copies = []
    for d in range(1, n):
        p = lax.rem(me + d, n)
        copy = pltpu.make_async_remote_copy(
            src_ref=src_ref.at[p],
            dst_ref=landed.at[me],
            send_sem=send_sem.at[d],
            recv_sem=recv_sem.at[d],
            device_id=peer_id(REP, sizes, p),
        )
        copy.start()
        copies.append(copy)
    own = pltpu.make_async_copy(src_ref.at[me], landed.at[me], local_sem)
    own.start()
    for copy in copies:
        copy.wait()
    own.wait()
    total = landed[0]
    for slot in range(1, n):
        total = total + landed[slot]
    out_ref[...] = total


def reduce_rep(partial, cid):
    nrep = lax.axis_size("yhi") * lax.axis_size("core")
    pieces = partial.reshape(nrep, -1, partial.shape[1])
    return pl.pallas_call(
        reduce_kernel,
        out_shape=jax.ShapeDtypeStruct(pieces.shape[1:], pieces.dtype),
        in_specs=[pl.BlockSpec(memory_space=pl.ANY)],
        out_specs=pl.BlockSpec(memory_space=pltpu.VMEM),
        scratch_shapes=[
            pltpu.VMEM(pieces.shape, pieces.dtype),
            pltpu.SemaphoreType.DMA((nrep,)),
            pltpu.SemaphoreType.DMA((nrep,)),
            pltpu.SemaphoreType.DMA,
        ],
        compiler_params=pltpu.CompilerParams(collective_id=cid, has_side_effects=True),
    )(pieces)


def staged_index(col, per_owner):
    nz = lax.axis_size("z")
    nxy = lax.axis_size("x") * lax.axis_size("ylo")
    half = per_owner // 2
    owner = col // per_owner
    sub = col % per_owner
    z = owner % nz
    xy = owner // nz
    in_first = sub < half
    first = (z * nxy + xy) * half + jnp.where(in_first, sub, 0)
    second = (xy * nz + z) * half + jnp.where(in_first, 0, sub - half)
    return in_first.astype(jnp.int32), first, second


def products_kernel(flag_ref, first_ref, second_ref, *refs):
    adj_ref, out_ref = refs[-2:]
    rows, kq = adj_ref.shape[0], adj_ref.shape[1]
    firsts, seconds = refs[: rows * kq], refs[rows * kq : 2 * rows * kq]
    base = pl.program_id(0) * rows
    for r in range(rows):
        acc = jnp.zeros(out_ref.shape[1:], jnp.float32)
        for k in range(kq):
            at = r * kq + k
            block = jnp.where(flag_ref[base + r, k] != 0, firsts[at][0], seconds[at][0])
            acc = acc + jnp.dot(adj_ref[r, k], block, preferred_element_type=jnp.float32)
        out_ref[r] = acc


def tile_products(panels, adj_tiles, index, per_piece):
    flag, first, second = index
    rows, kq = flag.shape
    width = panels[0].shape[2]
    tile = (1, BLOCK, width)

    def pick(table, r, k):
        return pl.BlockSpec(tile, lambda g, f, a, b: (table(f, a, b)[g * per_piece + r, k], 0, 0))

    specs = [pick(lambda f, a, b: a, r, k) for r in range(per_piece) for k in range(kq)]
    specs += [pick(lambda f, a, b: b, r, k) for r in range(per_piece) for k in range(kq)]
    specs.append(pl.BlockSpec((per_piece, kq, BLOCK, BLOCK), lambda g, f, a, b: (g, 0, 0, 0)))
    out_spec = pl.BlockSpec((per_piece, BLOCK, width), lambda g, f, a, b: (g, 0, 0))
    summed = pl.pallas_call(
        products_kernel,
        out_shape=jax.ShapeDtypeStruct((rows, BLOCK, width), jnp.float32),
        grid_spec=pltpu.PrefetchScalarGridSpec(
            num_scalar_prefetch=3,
            grid=(rows // per_piece,),
            in_specs=specs,
            out_specs=out_spec,
        ),
    )(flag, first, second, *([panels[0]] * (per_piece * kq)), *([panels[1]] * (per_piece * kq)), adj_tiles[:, 0])
    return summed.reshape(-1, width)


def local(node_feats, adj_tiles, col_index, w_in, b_in, w_out, b_out, cot_out):
    per_piece = node_feats.shape[0] // BLOCK
    index = staged_index(col_index[:, 0, :], per_piece)
    panels = gather_blk(node_feats, 0)
    partial_sum = tile_products(panels, adj_tiles, index, per_piece)
    agg = reduce_rep(partial_sum, 8)
    agg_b = agg.astype(jnp.bfloat16)
    pre = jnp.dot(agg_b, w_in, preferred_element_type=jnp.float32) + b_in
    hidden = jax.nn.silu(pre).astype(jnp.bfloat16)
    projected = jnp.dot(hidden, w_out, preferred_element_type=jnp.float32) + b_out
    out_feats = (node_feats.astype(jnp.float32) + projected).astype(jnp.bfloat16)
    g_hidden = jnp.einsum("nh,fh->nf", cot_out, w_out, preferred_element_type=jnp.float32)
    sigma = jax.nn.sigmoid(pre)
    g_pre = (g_hidden * sigma * (1.0 + pre * (1.0 - sigma))).astype(jnp.bfloat16)
    g_agg = jnp.einsum("nf,hf->nh", g_pre, w_in, preferred_element_type=jnp.float32).astype(
        jnp.bfloat16
    )
    g_panels = gather_blk(g_agg, 1)
    back_partial = tile_products(g_panels, adj_tiles, index, per_piece)
    back_rows = reduce_rep(back_partial, 9)
    grad_feats = (cot_out.astype(jnp.float32) + back_rows).astype(jnp.bfloat16)
    return (out_feats, grad_feats)


def solution(mesh):
    nblk = mesh.shape["blk"]
    nrep = mesh.shape["rep"]
    fine = Mesh(mesh.devices.reshape(nblk // 16, 2, 8, nrep // 2, 2), NAMES)
    rows = P(BLK + REP, None)
    placed = (
        rows,
        P(BLK, REP, None, None, None),
        P(BLK, REP, None),
        P(),
        P(),
        P(),
        P(),
        rows,
    )
    return jax.shard_map(
        local,
        mesh=fine,
        in_specs=placed,
        out_specs=(rows, rows),
        check_vma=False,
    )
```

```python
import functools

import jax
import jax.numpy as jnp
from jax import lax
from jax.experimental import pallas as pl
from jax.experimental.pallas import tpu as pltpu
from jax.sharding import Mesh
from jax.sharding import PartitionSpec as P

BLOCK = 128
NAMES = ("x", "ylo", "z", "yhi", "core")
BLK = ("x", "ylo", "z")
REP = ("yhi", "core")


def group_place(axes):
    sizes = [lax.axis_size(a) for a in axes]
    me = 0
    for a, n in zip(axes, sizes):
        me = me * n + lax.axis_index(a)
    return me, sizes


def peer_id(axes, sizes, p):
    coords = {}
    for a, n in reversed(list(zip(axes, sizes))):
        coords[a] = p % n
        p = p // n
    return coords


def neighbours():
    nx, ny, nz = lax.axis_size("x"), lax.axis_size("ylo"), lax.axis_size("z")
    x, y, z = lax.axis_index("x"), lax.axis_index("ylo"), lax.axis_index("z")
    right, left, other = lax.rem(x + 1, nx), lax.rem(x + nx - 1, nx), ny - 1 - y
    return {"x": right}, {"x": left}, {"ylo": other}, {"z": lax.rem(z + 1, nz)}, {"z": lax.rem(z + nz - 1, nz)}


def gather_phase(phase, ring_src, tree_src, ring_out, tree_out, send_sem, recv_sem, local_sem):
    nx, ny, nz = lax.axis_size("x"), lax.axis_size("ylo"), lax.axis_size("z")
    x, y, z = lax.axis_index("x"), lax.axis_index("ylo"), lax.axis_index("z")
    left, other = lax.rem(x + nx - 1, nx), ny - 1 - y
    to_right, to_left, to_other, up, down = neighbours()

    def send(kind, src, dst, peer):
        copy = pltpu.make_async_remote_copy(
            src_ref=src,
            dst_ref=dst,
            send_sem=send_sem.at[phase, kind],
            recv_sem=recv_sem.at[phase, kind],
            device_id=peer,
        )
        copy.start()
        return copy

    me = x * ny + y
    own_tree = pltpu.make_async_copy(tree_src, tree_out.at[me], local_sem.at[phase, 0])
    own_tree.start()
    own_ring = pltpu.make_async_copy(ring_src, ring_out.at[z], local_sem.at[phase, 1])
    own_ring.start()
    first_right = send(0, tree_src, tree_out.at[me], to_right)
    first_left = send(1, tree_src, tree_out.at[me], to_left)
    first_other = send(2, tree_src, tree_out.at[me], to_other)
    steps = nz // 2
    split = ring_src.shape[0] // 2
    ups = [send(7, ring_src, ring_out.at[z], up)]
    downs = [send(7 + steps, ring_src, ring_out.at[z], down)]

    def ring_step(s):
        below = lax.rem(z + nz - (s - 1), nz)
        above = lax.rem(z + s - 1, nz)
        ups[-1].wait_recv()
        downs[-1].wait_recv()
        if s < steps:
            ups.append(send(7 + s - 1, ring_out.at[below], ring_out.at[below], up))
            downs.append(send(7 + steps + s - 1, ring_out.at[above], ring_out.at[above], down))
        else:
            ups.append(send(7 + s - 1, ring_out.at[below, :split], ring_out.at[below, :split], up))
            downs.append(send(7 + steps + s - 1, ring_out.at[above, split:], ring_out.at[above, split:], down))

    first_right.wait_recv()
    from_left = left * ny + y
    second_right = send(3, tree_out.at[from_left], tree_out.at[from_left], to_right)
    ring_step(2)
    first_other.wait_recv()
    from_other = x * ny + other
    other_right = send(4, tree_out.at[from_other], tree_out.at[from_other], to_right)
    other_left = send(5, tree_out.at[from_other], tree_out.at[from_other], to_left)
    ring_step(3)
    other_right.wait_recv()
    from_left_other = left * ny + other
    third_right = send(6, tree_out.at[from_left_other], tree_out.at[from_left_other], to_right)
    for s in range(4, steps + 1):
        ring_step(s)
    for copy in (first_left, second_right, other_left, third_right, ups[-1], downs[-1]):
        copy.wait_recv()
    tree = [first_right, first_left, first_other, second_right, other_right, other_left, third_right]
    return tree + ups + downs, [own_tree, own_ring]


def gather_kernel(rows_ref, mid_ring, mid_tree, ring_out, tree_out, send_sem, recv_sem, local_sem):
    barrier = pltpu.get_barrier_semaphore()
    peers = neighbours()
    for peer in peers:
        pl.semaphore_signal(barrier, 1, device_id=peer)
    pl.semaphore_wait(barrier, len(peers))
    half = rows_ref.shape[0] // 2
    ring_src, tree_src = rows_ref.at[pl.ds(half, half)], rows_ref.at[pl.ds(0, half)]
    sends, local = gather_phase(0, ring_src, tree_src, mid_ring, mid_tree, send_sem, recv_sem, local_sem)
    for copy in local:
        copy.wait()
    more, local = gather_phase(1, mid_tree, mid_ring, ring_out, tree_out, send_sem, recv_sem, local_sem)
    for copy in sends + more:
        copy.wait_send()
    for copy in local:
        copy.wait()


def gather_blk(rows, cid):
    nz = lax.axis_size("z")
    nxy = lax.axis_size("x") * lax.axis_size("ylo")
    half = rows.shape[0] // 2
    width = rows.shape[1]
    piece = (half, width)
    any_space = pl.BlockSpec(memory_space=pl.ANY)
    _, _, first, second = pl.pallas_call(
        gather_kernel,
        out_shape=(
            jax.ShapeDtypeStruct((nz, *piece), rows.dtype),
            jax.ShapeDtypeStruct((nxy, *piece), rows.dtype),
            jax.ShapeDtypeStruct((nz, nxy, *piece), rows.dtype),
            jax.ShapeDtypeStruct((nxy, nz, *piece), rows.dtype),
        ),
        in_specs=[any_space],
        out_specs=(any_space,) * 4,
        scratch_shapes=[
            pltpu.SemaphoreType.DMA((2, 7 + nz)),
            pltpu.SemaphoreType.DMA((2, 7 + nz)),
            pltpu.SemaphoreType.DMA((2, 2)),
        ],
        compiler_params=pltpu.CompilerParams(collective_id=cid, has_side_effects=True),
    )(rows)
    return first.reshape(-1, BLOCK, width), second.reshape(-1, BLOCK, width)


def reduce_kernel(src_ref, out_ref, landed, send_sem, recv_sem, local_sem):
    me, sizes = group_place(REP)
    n = landed.shape[0]
    barrier = pltpu.get_barrier_semaphore()
    for d in range(1, n):
        pl.semaphore_signal(barrier, 1, device_id=peer_id(REP, sizes, lax.rem(me + d, n)))
    pl.semaphore_wait(barrier, n - 1)
    copies = []
    for d in range(1, n):
        p = lax.rem(me + d, n)
        copy = pltpu.make_async_remote_copy(
            src_ref=src_ref.at[p],
            dst_ref=landed.at[me],
            send_sem=send_sem.at[d],
            recv_sem=recv_sem.at[d],
            device_id=peer_id(REP, sizes, p),
        )
        copy.start()
        copies.append(copy)
    own = pltpu.make_async_copy(src_ref.at[me], landed.at[me], local_sem)
    own.start()
    for copy in copies:
        copy.wait()
    own.wait()
    total = landed[0]
    for slot in range(1, n):
        total = total + landed[slot]
    out_ref[...] = total


def reduce_rep(partial, cid):
    nrep = lax.axis_size("yhi") * lax.axis_size("core")
    pieces = partial.reshape(nrep, -1, partial.shape[1])
    return pl.pallas_call(
        reduce_kernel,
        out_shape=jax.ShapeDtypeStruct(pieces.shape[1:], pieces.dtype),
        in_specs=[pl.BlockSpec(memory_space=pl.ANY)],
        out_specs=pl.BlockSpec(memory_space=pltpu.VMEM),
        scratch_shapes=[
            pltpu.VMEM(pieces.shape, pieces.dtype),
            pltpu.SemaphoreType.DMA((nrep,)),
            pltpu.SemaphoreType.DMA((nrep,)),
            pltpu.SemaphoreType.DMA,
        ],
        compiler_params=pltpu.CompilerParams(collective_id=cid, has_side_effects=True),
    )(pieces)


def staged_index(col, per_owner):
    nz = lax.axis_size("z")
    nxy = lax.axis_size("x") * lax.axis_size("ylo")
    half = per_owner // 2
    owner = col // per_owner
    sub = col % per_owner
    z = owner % nz
    xy = owner // nz
    in_first = sub < half
    first = (z * nxy + xy) * half + jnp.where(in_first, sub, 0)
    second = (xy * nz + z) * half + jnp.where(in_first, 0, sub - half)
    return in_first.astype(jnp.int32), first, second


def products_kernel(flag_ref, first_ref, second_ref, *refs):
    adj_ref, out_ref = refs[-2:]
    rows, kq = adj_ref.shape[0], adj_ref.shape[1]
    firsts, seconds = refs[: rows * kq], refs[rows * kq : 2 * rows * kq]
    base = pl.program_id(0) * rows
    for r in range(rows):
        acc = jnp.zeros(out_ref.shape[1:], jnp.float32)
        for k in range(kq):
            at = r * kq + k
            block = jnp.where(flag_ref[base + r, k] != 0, firsts[at][0], seconds[at][0])
            acc = acc + jnp.dot(adj_ref[r, k], block, preferred_element_type=jnp.float32)
        out_ref[r] = acc


def tile_products(panels, adj_tiles, index, per_piece):
    flag, first, second = index
    rows, kq = flag.shape
    width = panels[0].shape[2]
    tile = (1, BLOCK, width)

    def pick(table, r, k):
        return pl.BlockSpec(tile, lambda g, f, a, b: (table(f, a, b)[g * per_piece + r, k], 0, 0))

    specs = [pick(lambda f, a, b: a, r, k) for r in range(per_piece) for k in range(kq)]
    specs += [pick(lambda f, a, b: b, r, k) for r in range(per_piece) for k in range(kq)]
    specs.append(pl.BlockSpec((per_piece, kq, BLOCK, BLOCK), lambda g, f, a, b: (g, 0, 0, 0)))
    out_spec = pl.BlockSpec((per_piece, BLOCK, width), lambda g, f, a, b: (g, 0, 0))
    summed = pl.pallas_call(
        products_kernel,
        out_shape=jax.ShapeDtypeStruct((rows, BLOCK, width), jnp.float32),
        grid_spec=pltpu.PrefetchScalarGridSpec(
            num_scalar_prefetch=3,
            grid=(rows // per_piece,),
            in_specs=specs,
            out_specs=out_spec,
        ),
    )(flag, first, second, *([panels[0]] * (per_piece * kq)), *([panels[1]] * (per_piece * kq)), adj_tiles[:, 0])
    return summed.reshape(-1, width)


def local(node_feats, adj_tiles, col_index, w_in, b_in, w_out, b_out, cot_out):
    per_piece = node_feats.shape[0] // BLOCK
    index = staged_index(col_index[:, 0, :], per_piece)
    panels = gather_blk(node_feats, 0)
    partial_sum = tile_products(panels, adj_tiles, index, 2 * per_piece)
    agg = reduce_rep(partial_sum, 8)
    agg_b = agg.astype(jnp.bfloat16)
    pre = jnp.dot(agg_b, w_in, preferred_element_type=jnp.float32) + b_in
    hidden = jax.nn.silu(pre).astype(jnp.bfloat16)
    projected = jnp.dot(hidden, w_out, preferred_element_type=jnp.float32) + b_out
    out_feats = (node_feats.astype(jnp.float32) + projected).astype(jnp.bfloat16)
    g_hidden = jnp.einsum("nh,fh->nf", cot_out, w_out, preferred_element_type=jnp.float32)
    sigma = jax.nn.sigmoid(pre)
    g_pre = (g_hidden * sigma * (1.0 + pre * (1.0 - sigma))).astype(jnp.bfloat16)
    g_agg = jnp.einsum("nf,hf->nh", g_pre, w_in, preferred_element_type=jnp.float32).astype(
        jnp.bfloat16
    )
    g_panels = gather_blk(g_agg, 1)
    back_partial = tile_products(g_panels, adj_tiles, index, 2 * per_piece)
    back_rows = reduce_rep(back_partial, 9)
    grad_feats = (cot_out.astype(jnp.float32) + back_rows).astype(jnp.bfloat16)
    return (out_feats, grad_feats)


def solution(mesh):
    nblk = mesh.shape["blk"]
    nrep = mesh.shape["rep"]
    fine = Mesh(mesh.devices.reshape(nblk // 16, 2, 8, nrep // 2, 2), NAMES)
    rows = P(BLK + REP, None)
    placed = (
        rows,
        P(BLK, REP, None, None, None),
        P(BLK, REP, None),
        P(),
        P(),
        P(),
        P(),
        rows,
    )
    return jax.shard_map(
        local,
        mesh=fine,
        in_specs=placed,
        out_specs=(rows, rows),
        check_vma=False,
    )
```

```python
import functools

import jax
import jax.numpy as jnp
from jax import lax
from jax.experimental import pallas as pl
from jax.experimental.pallas import tpu as pltpu
from jax.sharding import Mesh
from jax.sharding import PartitionSpec as P

BLOCK = 128
NAMES = ("x", "ylo", "z", "yhi", "core")
BLK = ("x", "ylo", "z")
REP = ("yhi", "core")


def group_place(axes):
    sizes = [lax.axis_size(a) for a in axes]
    me = 0
    for a, n in zip(axes, sizes):
        me = me * n + lax.axis_index(a)
    return me, sizes


def peer_id(axes, sizes, p):
    coords = {}
    for a, n in reversed(list(zip(axes, sizes))):
        coords[a] = p % n
        p = p // n
    return coords


def neighbours():
    nx, ny, nz = lax.axis_size("x"), lax.axis_size("ylo"), lax.axis_size("z")
    x, y, z = lax.axis_index("x"), lax.axis_index("ylo"), lax.axis_index("z")
    right, left, other = lax.rem(x + 1, nx), lax.rem(x + nx - 1, nx), ny - 1 - y
    return {"x": right}, {"x": left}, {"ylo": other}, {"z": lax.rem(z + 1, nz)}, {"z": lax.rem(z + nz - 1, nz)}


def gather_phase(phase, ring_src, tree_src, ring_out, tree_out, send_sem, recv_sem, local_sem):
    nx, ny, nz = lax.axis_size("x"), lax.axis_size("ylo"), lax.axis_size("z")
    x, y, z = lax.axis_index("x"), lax.axis_index("ylo"), lax.axis_index("z")
    left, other = lax.rem(x + nx - 1, nx), ny - 1 - y
    to_right, to_left, to_other, up, down = neighbours()

    def send(kind, src, dst, peer):
        copy = pltpu.make_async_remote_copy(
            src_ref=src,
            dst_ref=dst,
            send_sem=send_sem.at[phase, kind],
            recv_sem=recv_sem.at[phase, kind],
            device_id=peer,
        )
        copy.start()
        return copy

    me = x * ny + y
    own_tree = pltpu.make_async_copy(tree_src, tree_out.at[me], local_sem.at[phase, 0])
    own_tree.start()
    own_ring = pltpu.make_async_copy(ring_src, ring_out.at[z], local_sem.at[phase, 1])
    own_ring.start()
    first_right = send(0, tree_src, tree_out.at[me], to_right)
    first_left = send(1, tree_src, tree_out.at[me], to_left)
    first_other = send(2, tree_src, tree_out.at[me], to_other)
    steps = nz // 2
    split = ring_src.shape[0] // 2
    ups = [send(7, ring_src, ring_out.at[z], up)]
    downs = [send(7 + steps, ring_src, ring_out.at[z], down)]

    def ring_step(s):
        below = lax.rem(z + nz - (s - 1), nz)
        above = lax.rem(z + s - 1, nz)
        ups[-1].wait_recv()
        downs[-1].wait_recv()
        if s < steps:
            ups.append(send(7 + s - 1, ring_out.at[below], ring_out.at[below], up))
            downs.append(send(7 + steps + s - 1, ring_out.at[above], ring_out.at[above], down))
        else:
            ups.append(send(7 + s - 1, ring_out.at[below, :split], ring_out.at[below, :split], up))
            downs.append(send(7 + steps + s - 1, ring_out.at[above, split:], ring_out.at[above, split:], down))

    first_right.wait_recv()
    from_left = left * ny + y
    second_right = send(3, tree_out.at[from_left], tree_out.at[from_left], to_right)
    ring_step(2)
    first_other.wait_recv()
    from_other = x * ny + other
    other_right = send(4, tree_out.at[from_other], tree_out.at[from_other], to_right)
    other_left = send(5, tree_out.at[from_other], tree_out.at[from_other], to_left)
    ring_step(3)
    other_right.wait_recv()
    from_left_other = left * ny + other
    third_right = send(6, tree_out.at[from_left_other], tree_out.at[from_left_other], to_right)
    for s in range(4, steps + 1):
        ring_step(s)
    for copy in (first_left, second_right, other_left, third_right, ups[-1], downs[-1]):
        copy.wait_recv()
    tree = [first_right, first_left, first_other, second_right, other_right, other_left, third_right]
    return tree + ups + downs, [own_tree, own_ring]


def phase_one(ring_src, tree_src, ring_out, tree_out, send_sem, recv_sem, local_sem):
    nx, ny, nz = lax.axis_size("x"), lax.axis_size("ylo"), lax.axis_size("z")
    x, y, z = lax.axis_index("x"), lax.axis_index("ylo"), lax.axis_index("z")

    def send(kind, src, dst, peer):
        copy = pltpu.make_async_remote_copy(
            src_ref=src, dst_ref=dst, send_sem=send_sem.at[0, kind], recv_sem=recv_sem.at[0, kind], device_id=peer
        )
        copy.start()
        return copy

    def on_z(step):
        return {"z": lax.rem(z + nz + step, nz)}

    me = x * ny + y
    own_tree = pltpu.make_async_copy(tree_src, tree_out.at[me], local_sem.at[0, 0])
    own_tree.start()
    own_ring = pltpu.make_async_copy(ring_src, ring_out.at[z], local_sem.at[0, 1])
    own_ring.start()
    n = nx * ny
    sends = []
    for d in range(1, n):
        p = lax.rem(me + d, n)
        sends.append(send(d - 1, tree_src, tree_out.at[me], {"x": p // ny, "ylo": p % ny}))
    kind = n - 1
    up_one = send(kind, ring_src, ring_out.at[z], on_z(1))
    down_one = send(kind + 1, ring_src, ring_out.at[z], on_z(-1))
    up_two = send(kind + 2, ring_src, ring_out.at[z], on_z(2))
    down_two = send(kind + 3, ring_src, ring_out.at[z], on_z(-2))
    split = ring_src.shape[0] // 2
    up_two.wait_recv()
    below = lax.rem(z + nz - 2, nz)
    fwd_up_one = send(kind + 4, ring_out.at[below], ring_out.at[below], on_z(1))
    fwd_up_two = send(kind + 5, ring_out.at[below, :split], ring_out.at[below, :split], on_z(2))
    down_two.wait_recv()
    above = lax.rem(z + 2, nz)
    fwd_down_one = send(kind + 6, ring_out.at[above], ring_out.at[above], on_z(-1))
    fwd_down_two = send(kind + 7, ring_out.at[above, split:], ring_out.at[above, split:], on_z(-2))
    ring = [up_one, down_one, up_two, down_two, fwd_up_one, fwd_up_two, fwd_down_one, fwd_down_two]
    for copy in sends + [up_one, down_one, fwd_up_one, fwd_up_two, fwd_down_one, fwd_down_two]:
        copy.wait_recv()
    return sends + ring, [own_tree, own_ring]


def gather_kernel(rows_ref, mid_ring, mid_tree, ring_out, tree_out, send_sem, recv_sem, local_sem):
    nx, ny, nz = lax.axis_size("x"), lax.axis_size("ylo"), lax.axis_size("z")
    x, y, z = lax.axis_index("x"), lax.axis_index("ylo"), lax.axis_index("z")
    me = x * ny + y
    peers = [{"x": lax.rem(me + d, nx * ny) // ny, "ylo": lax.rem(me + d, nx * ny) % ny} for d in range(1, nx * ny)]
    peers += [{"z": lax.rem(z + nz + step, nz)} for step in (1, -1, 2, -2)]
    barrier = pltpu.get_barrier_semaphore()
    for peer in peers:
        pl.semaphore_signal(barrier, 1, device_id=peer)
    pl.semaphore_wait(barrier, len(peers))
    half = rows_ref.shape[0] // 2
    ring_src, tree_src = rows_ref.at[pl.ds(half, half)], rows_ref.at[pl.ds(0, half)]
    sends, local = phase_one(ring_src, tree_src, mid_ring, mid_tree, send_sem, recv_sem, local_sem)
    for copy in local:
        copy.wait()
    more, local = gather_phase(1, mid_tree, mid_ring, ring_out, tree_out, send_sem, recv_sem, local_sem)
    for copy in sends + more:
        copy.wait_send()
    for copy in local:
        copy.wait()


def gather_blk(rows, cid):
    nz = lax.axis_size("z")
    nxy = lax.axis_size("x") * lax.axis_size("ylo")
    half = rows.shape[0] // 2
    width = rows.shape[1]
    piece = (half, width)
    any_space = pl.BlockSpec(memory_space=pl.ANY)
    _, _, first, second = pl.pallas_call(
        gather_kernel,
        out_shape=(
            jax.ShapeDtypeStruct((nz, *piece), rows.dtype),
            jax.ShapeDtypeStruct((nxy, *piece), rows.dtype),
            jax.ShapeDtypeStruct((nz, nxy, *piece), rows.dtype),
            jax.ShapeDtypeStruct((nxy, nz, *piece), rows.dtype),
        ),
        in_specs=[any_space],
        out_specs=(any_space,) * 4,
        scratch_shapes=[
            pltpu.SemaphoreType.DMA((2, 7 + nz)),
            pltpu.SemaphoreType.DMA((2, 7 + nz)),
            pltpu.SemaphoreType.DMA((2, 2)),
        ],
        compiler_params=pltpu.CompilerParams(collective_id=cid, has_side_effects=True),
    )(rows)
    return first.reshape(-1, BLOCK, width), second.reshape(-1, BLOCK, width)


def reduce_kernel(src_ref, out_ref, landed, send_sem, recv_sem, local_sem):
    me, sizes = group_place(REP)
    n = landed.shape[0]
    barrier = pltpu.get_barrier_semaphore()
    for d in range(1, n):
        pl.semaphore_signal(barrier, 1, device_id=peer_id(REP, sizes, lax.rem(me + d, n)))
    pl.semaphore_wait(barrier, n - 1)
    copies = []
    for d in range(1, n):
        p = lax.rem(me + d, n)
        copy = pltpu.make_async_remote_copy(
            src_ref=src_ref.at[p],
            dst_ref=landed.at[me],
            send_sem=send_sem.at[d],
            recv_sem=recv_sem.at[d],
            device_id=peer_id(REP, sizes, p),
        )
        copy.start()
        copies.append(copy)
    own = pltpu.make_async_copy(src_ref.at[me], landed.at[me], local_sem)
    own.start()
    for copy in copies:
        copy.wait()
    own.wait()
    total = landed[0]
    for slot in range(1, n):
        total = total + landed[slot]
    out_ref[...] = total


def reduce_rep(partial, cid):
    nrep = lax.axis_size("yhi") * lax.axis_size("core")
    pieces = partial.reshape(nrep, -1, partial.shape[1])
    return pl.pallas_call(
        reduce_kernel,
        out_shape=jax.ShapeDtypeStruct(pieces.shape[1:], pieces.dtype),
        in_specs=[pl.BlockSpec(memory_space=pl.ANY)],
        out_specs=pl.BlockSpec(memory_space=pltpu.VMEM),
        scratch_shapes=[
            pltpu.VMEM(pieces.shape, pieces.dtype),
            pltpu.SemaphoreType.DMA((nrep,)),
            pltpu.SemaphoreType.DMA((nrep,)),
            pltpu.SemaphoreType.DMA,
        ],
        compiler_params=pltpu.CompilerParams(collective_id=cid, has_side_effects=True),
    )(pieces)


def staged_index(col, per_owner):
    nz = lax.axis_size("z")
    nxy = lax.axis_size("x") * lax.axis_size("ylo")
    half = per_owner // 2
    owner = col // per_owner
    sub = col % per_owner
    z = owner % nz
    xy = owner // nz
    in_first = sub < half
    first = (z * nxy + xy) * half + jnp.where(in_first, sub, 0)
    second = (xy * nz + z) * half + jnp.where(in_first, 0, sub - half)
    return in_first.astype(jnp.int32), first, second


def products_kernel(flag_ref, first_ref, second_ref, *refs):
    adj_ref, out_ref = refs[-2:]
    rows, kq = adj_ref.shape[0], adj_ref.shape[1]
    firsts, seconds = refs[: rows * kq], refs[rows * kq : 2 * rows * kq]
    base = pl.program_id(0) * rows
    for r in range(rows):
        acc = jnp.zeros(out_ref.shape[1:], jnp.float32)
        for k in range(kq):
            at = r * kq + k
            block = jnp.where(flag_ref[base + r, k] != 0, firsts[at][0], seconds[at][0])
            acc = acc + jnp.dot(adj_ref[r, k], block, preferred_element_type=jnp.float32)
        out_ref[r] = acc


def tile_products(panels, adj_tiles, index, per_piece):
    flag, first, second = index
    rows, kq = flag.shape
    width = panels[0].shape[2]
    tile = (1, BLOCK, width)

    def pick(table, r, k):
        return pl.BlockSpec(tile, lambda g, f, a, b: (table(f, a, b)[g * per_piece + r, k], 0, 0))

    specs = [pick(lambda f, a, b: a, r, k) for r in range(per_piece) for k in range(kq)]
    specs += [pick(lambda f, a, b: b, r, k) for r in range(per_piece) for k in range(kq)]
    specs.append(pl.BlockSpec((per_piece, kq, BLOCK, BLOCK), lambda g, f, a, b: (g, 0, 0, 0)))
    out_spec = pl.BlockSpec((per_piece, BLOCK, width), lambda g, f, a, b: (g, 0, 0))
    summed = pl.pallas_call(
        products_kernel,
        out_shape=jax.ShapeDtypeStruct((rows, BLOCK, width), jnp.float32),
        grid_spec=pltpu.PrefetchScalarGridSpec(
            num_scalar_prefetch=3,
            grid=(rows // per_piece,),
            in_specs=specs,
            out_specs=out_spec,
        ),
    )(flag, first, second, *([panels[0]] * (per_piece * kq)), *([panels[1]] * (per_piece * kq)), adj_tiles[:, 0])
    return summed.reshape(-1, width)


def local(node_feats, adj_tiles, col_index, w_in, b_in, w_out, b_out, cot_out):
    per_piece = node_feats.shape[0] // BLOCK
    index = staged_index(col_index[:, 0, :], per_piece)
    panels = gather_blk(node_feats, 0)
    partial_sum = tile_products(panels, adj_tiles, index, 2 * per_piece)
    agg = reduce_rep(partial_sum, 8)
    agg_b = agg.astype(jnp.bfloat16)
    pre = jnp.dot(agg_b, w_in, preferred_element_type=jnp.float32) + b_in
    hidden = jax.nn.silu(pre).astype(jnp.bfloat16)
    projected = jnp.dot(hidden, w_out, preferred_element_type=jnp.float32) + b_out
    out_feats = (node_feats.astype(jnp.float32) + projected).astype(jnp.bfloat16)
    g_hidden = jnp.einsum("nh,fh->nf", cot_out, w_out, preferred_element_type=jnp.float32)
    sigma = jax.nn.sigmoid(pre)
    g_pre = (g_hidden * sigma * (1.0 + pre * (1.0 - sigma))).astype(jnp.bfloat16)
    g_agg = jnp.einsum("nf,hf->nh", g_pre, w_in, preferred_element_type=jnp.float32).astype(
        jnp.bfloat16
    )
    g_panels = gather_blk(g_agg, 1)
    back_partial = tile_products(g_panels, adj_tiles, index, 2 * per_piece)
    back_rows = reduce_rep(back_partial, 9)
    grad_feats = (cot_out.astype(jnp.float32) + back_rows).astype(jnp.bfloat16)
    return (out_feats, grad_feats)


def solution(mesh):
    nblk = mesh.shape["blk"]
    nrep = mesh.shape["rep"]
    fine = Mesh(mesh.devices.reshape(nblk // 16, 2, 8, nrep // 2, 2), NAMES)
    rows = P(BLK + REP, None)
    placed = (
        rows,
        P(BLK, REP, None, None, None),
        P(BLK, REP, None),
        P(),
        P(),
        P(),
        P(),
        rows,
    )
    return jax.shard_map(
        local,
        mesh=fine,
        in_specs=placed,
        out_specs=(rows, rows),
        check_vma=False,
    )
```

```python
import functools

import jax
import jax.numpy as jnp
from jax import lax
from jax.experimental import pallas as pl
from jax.experimental.pallas import tpu as pltpu
from jax.sharding import Mesh
from jax.sharding import PartitionSpec as P

BLOCK = 128
NAMES = ("x", "ylo", "z", "yhi", "core")
BLK = ("x", "ylo", "z")
REP = ("yhi", "core")


def group_place(axes):
    sizes = [lax.axis_size(a) for a in axes]
    me = 0
    for a, n in zip(axes, sizes):
        me = me * n + lax.axis_index(a)
    return me, sizes


def peer_id(axes, sizes, p):
    coords = {}
    for a, n in reversed(list(zip(axes, sizes))):
        coords[a] = p % n
        p = p // n
    return coords


def neighbours():
    nx, ny, nz = lax.axis_size("x"), lax.axis_size("ylo"), lax.axis_size("z")
    x, y, z = lax.axis_index("x"), lax.axis_index("ylo"), lax.axis_index("z")
    right, left, other = lax.rem(x + 1, nx), lax.rem(x + nx - 1, nx), ny - 1 - y
    return {"x": right}, {"x": left}, {"ylo": other}, {"z": lax.rem(z + 1, nz)}, {"z": lax.rem(z + nz - 1, nz)}


def gather_phase(phase, ring_src, tree_src, ring_out, tree_out, send_sem, recv_sem, local_sem):
    nx, ny, nz = lax.axis_size("x"), lax.axis_size("ylo"), lax.axis_size("z")
    x, y, z = lax.axis_index("x"), lax.axis_index("ylo"), lax.axis_index("z")
    right, left, other = lax.rem(x + 1, nx), lax.rem(x + nx - 1, nx), ny - 1 - y
    to_right, to_left, to_other, up, down = neighbours()

    def send(kind, src, dst, peer):
        copy = pltpu.make_async_remote_copy(
            src_ref=src,
            dst_ref=dst,
            send_sem=send_sem.at[phase, kind],
            recv_sem=recv_sem.at[phase, kind],
            device_id=peer,
        )
        copy.start()
        return copy

    me = x * ny + y
    own_tree = pltpu.make_async_copy(tree_src, tree_out.at[me], local_sem.at[phase, 0])
    own_tree.start()
    own_ring = pltpu.make_async_copy(ring_src, ring_out.at[z], local_sem.at[phase, 1])
    own_ring.start()
    first_right = send(0, tree_src, tree_out.at[me], to_right)
    first_left = send(1, tree_src, tree_out.at[me], to_left)
    first_other = send(2, tree_src, tree_out.at[me], to_other)
    steps = nz // 2
    split = ring_src.shape[0] // 2
    ups = [send(9, ring_src, ring_out.at[z], up)]
    downs = [send(9 + steps, ring_src, ring_out.at[z], down)]

    def ring_step(s):
        below = lax.rem(z + nz - (s - 1), nz)
        above = lax.rem(z + s - 1, nz)
        ups[-1].wait_recv()
        downs[-1].wait_recv()
        if s < steps:
            ups.append(send(9 + s - 1, ring_out.at[below], ring_out.at[below], up))
            downs.append(send(9 + steps + s - 1, ring_out.at[above], ring_out.at[above], down))
        else:
            ups.append(send(9 + s - 1, ring_out.at[below, :split], ring_out.at[below, :split], up))
            downs.append(send(9 + steps + s - 1, ring_out.at[above, split:], ring_out.at[above, split:], down))

    tree_split = tree_src.shape[0] // 2
    first_right.wait_recv()
    from_left = left * ny + y
    second_right = send(3, tree_out.at[from_left, :tree_split], tree_out.at[from_left, :tree_split], to_right)
    first_left.wait_recv()
    from_right = right * ny + y
    second_left = send(7, tree_out.at[from_right, tree_split:], tree_out.at[from_right, tree_split:], to_left)
    ring_step(2)
    first_other.wait_recv()
    from_other = x * ny + other
    other_right = send(4, tree_out.at[from_other], tree_out.at[from_other], to_right)
    other_left = send(5, tree_out.at[from_other], tree_out.at[from_other], to_left)
    ring_step(3)
    other_right.wait_recv()
    from_left_other = left * ny + other
    third_right = send(
        6, tree_out.at[from_left_other, :tree_split], tree_out.at[from_left_other, :tree_split], to_right
    )
    other_left.wait_recv()
    from_right_other = right * ny + other
    third_left = send(
        8, tree_out.at[from_right_other, tree_split:], tree_out.at[from_right_other, tree_split:], to_left
    )
    for s in range(4, steps + 1):
        ring_step(s)
    for copy in (second_right, second_left, third_right, third_left, ups[-1], downs[-1]):
        copy.wait_recv()
    tree = [first_right, first_left, first_other, second_right, second_left]
    tree += [other_right, other_left, third_right, third_left]
    return tree + ups + downs, [own_tree, own_ring]


def phase_one(ring_src, tree_src, ring_out, tree_out, send_sem, recv_sem, local_sem):
    nx, ny, nz = lax.axis_size("x"), lax.axis_size("ylo"), lax.axis_size("z")
    x, y, z = lax.axis_index("x"), lax.axis_index("ylo"), lax.axis_index("z")

    def send(kind, src, dst, peer):
        copy = pltpu.make_async_remote_copy(
            src_ref=src, dst_ref=dst, send_sem=send_sem.at[0, kind], recv_sem=recv_sem.at[0, kind], device_id=peer
        )
        copy.start()
        return copy

    def on_z(step):
        return {"z": lax.rem(z + nz + step, nz)}

    me = x * ny + y
    own_tree = pltpu.make_async_copy(tree_src, tree_out.at[me], local_sem.at[0, 0])
    own_tree.start()
    own_ring = pltpu.make_async_copy(ring_src, ring_out.at[z], local_sem.at[0, 1])
    own_ring.start()
    n = nx * ny
    sends = []
    for d in range(1, n):
        p = lax.rem(me + d, n)
        sends.append(send(d - 1, tree_src, tree_out.at[me], {"x": p // ny, "ylo": p % ny}))
    kind = n - 1
    up_one = send(kind, ring_src, ring_out.at[z], on_z(1))
    down_one = send(kind + 1, ring_src, ring_out.at[z], on_z(-1))
    up_two = send(kind + 2, ring_src, ring_out.at[z], on_z(2))
    down_two = send(kind + 3, ring_src, ring_out.at[z], on_z(-2))
    split = ring_src.shape[0] // 2
    up_two.wait_recv()
    below = lax.rem(z + nz - 2, nz)
    fwd_up_one = send(kind + 4, ring_out.at[below], ring_out.at[below], on_z(1))
    fwd_up_two = send(kind + 5, ring_out.at[below, :split], ring_out.at[below, :split], on_z(2))
    down_two.wait_recv()
    above = lax.rem(z + 2, nz)
    fwd_down_one = send(kind + 6, ring_out.at[above], ring_out.at[above], on_z(-1))
    fwd_down_two = send(kind + 7, ring_out.at[above, split:], ring_out.at[above, split:], on_z(-2))
    ring = [up_one, down_one, up_two, down_two, fwd_up_one, fwd_up_two, fwd_down_one, fwd_down_two]
    for copy in sends + [up_one, down_one, fwd_up_one, fwd_up_two, fwd_down_one, fwd_down_two]:
        copy.wait_recv()
    return sends + ring, [own_tree, own_ring]


def gather_kernel(rows_ref, mid_ring, mid_tree, ring_out, tree_out, send_sem, recv_sem, local_sem):
    nx, ny, nz = lax.axis_size("x"), lax.axis_size("ylo"), lax.axis_size("z")
    x, y, z = lax.axis_index("x"), lax.axis_index("ylo"), lax.axis_index("z")
    me = x * ny + y
    peers = [{"x": lax.rem(me + d, nx * ny) // ny, "ylo": lax.rem(me + d, nx * ny) % ny} for d in range(1, nx * ny)]
    peers += [{"z": lax.rem(z + nz + step, nz)} for step in (1, -1, 2, -2)]
    barrier = pltpu.get_barrier_semaphore()
    for peer in peers:
        pl.semaphore_signal(barrier, 1, device_id=peer)
    pl.semaphore_wait(barrier, len(peers))
    half = rows_ref.shape[0] // 2
    ring_src, tree_src = rows_ref.at[pl.ds(half, half)], rows_ref.at[pl.ds(0, half)]
    sends, local = phase_one(ring_src, tree_src, mid_ring, mid_tree, send_sem, recv_sem, local_sem)
    for copy in local:
        copy.wait()
    more, local = gather_phase(1, mid_tree, mid_ring, ring_out, tree_out, send_sem, recv_sem, local_sem)
    for copy in sends + more:
        copy.wait_send()
    for copy in local:
        copy.wait()


def gather_blk(rows, cid):
    nz = lax.axis_size("z")
    nxy = lax.axis_size("x") * lax.axis_size("ylo")
    half = rows.shape[0] // 2
    width = rows.shape[1]
    piece = (half, width)
    any_space = pl.BlockSpec(memory_space=pl.ANY)
    _, _, first, second = pl.pallas_call(
        gather_kernel,
        out_shape=(
            jax.ShapeDtypeStruct((nz, *piece), rows.dtype),
            jax.ShapeDtypeStruct((nxy, *piece), rows.dtype),
            jax.ShapeDtypeStruct((nz, nxy, *piece), rows.dtype),
            jax.ShapeDtypeStruct((nxy, nz, *piece), rows.dtype),
        ),
        in_specs=[any_space],
        out_specs=(any_space,) * 4,
        scratch_shapes=[
            pltpu.SemaphoreType.DMA((2, 9 + nz)),
            pltpu.SemaphoreType.DMA((2, 9 + nz)),
            pltpu.SemaphoreType.DMA((2, 2)),
        ],
        compiler_params=pltpu.CompilerParams(collective_id=cid, has_side_effects=True),
    )(rows)
    return first.reshape(-1, BLOCK, width), second.reshape(-1, BLOCK, width)


def reduce_kernel(src_ref, out_ref, landed, send_sem, recv_sem, local_sem):
    me, sizes = group_place(REP)
    n = landed.shape[0]
    barrier = pltpu.get_barrier_semaphore()
    for d in range(1, n):
        pl.semaphore_signal(barrier, 1, device_id=peer_id(REP, sizes, lax.rem(me + d, n)))
    pl.semaphore_wait(barrier, n - 1)
    copies = []
    for d in range(1, n):
        p = lax.rem(me + d, n)
        copy = pltpu.make_async_remote_copy(
            src_ref=src_ref.at[p],
            dst_ref=landed.at[me],
            send_sem=send_sem.at[d],
            recv_sem=recv_sem.at[d],
            device_id=peer_id(REP, sizes, p),
        )
        copy.start()
        copies.append(copy)
    own = pltpu.make_async_copy(src_ref.at[me], landed.at[me], local_sem)
    own.start()
    for copy in copies:
        copy.wait()
    own.wait()
    total = landed[0]
    for slot in range(1, n):
        total = total + landed[slot]
    out_ref[...] = total


def reduce_rep(partial, cid):
    nrep = lax.axis_size("yhi") * lax.axis_size("core")
    pieces = partial.reshape(nrep, -1, partial.shape[1])
    return pl.pallas_call(
        reduce_kernel,
        out_shape=jax.ShapeDtypeStruct(pieces.shape[1:], pieces.dtype),
        in_specs=[pl.BlockSpec(memory_space=pl.ANY)],
        out_specs=pl.BlockSpec(memory_space=pltpu.VMEM),
        scratch_shapes=[
            pltpu.VMEM(pieces.shape, pieces.dtype),
            pltpu.SemaphoreType.DMA((nrep,)),
            pltpu.SemaphoreType.DMA((nrep,)),
            pltpu.SemaphoreType.DMA,
        ],
        compiler_params=pltpu.CompilerParams(collective_id=cid, has_side_effects=True),
    )(pieces)


def staged_index(col, per_owner):
    nz = lax.axis_size("z")
    nxy = lax.axis_size("x") * lax.axis_size("ylo")
    half = per_owner // 2
    owner = col // per_owner
    sub = col % per_owner
    z = owner % nz
    xy = owner // nz
    in_first = sub < half
    first = (z * nxy + xy) * half + jnp.where(in_first, sub, 0)
    second = (xy * nz + z) * half + jnp.where(in_first, 0, sub - half)
    return in_first.astype(jnp.int32), first, second


def products_kernel(flag_ref, first_ref, second_ref, *refs):
    adj_ref, out_ref = refs[-2:]
    rows, kq = adj_ref.shape[0], adj_ref.shape[1]
    firsts, seconds = refs[: rows * kq], refs[rows * kq : 2 * rows * kq]
    base = pl.program_id(0) * rows
    for r in range(rows):
        acc = jnp.zeros(out_ref.shape[1:], jnp.float32)
        for k in range(kq):
            at = r * kq + k
            block = jnp.where(flag_ref[base + r, k] != 0, firsts[at][0], seconds[at][0])
            acc = acc + jnp.dot(adj_ref[r, k], block, preferred_element_type=jnp.float32)
        out_ref[r] = acc


def tile_products(panels, adj_tiles, index, per_piece):
    flag, first, second = index
    rows, kq = flag.shape
    width = panels[0].shape[2]
    tile = (1, BLOCK, width)

    def pick(table, r, k):
        return pl.BlockSpec(tile, lambda g, f, a, b: (table(f, a, b)[g * per_piece + r, k], 0, 0))

    specs = [pick(lambda f, a, b: a, r, k) for r in range(per_piece) for k in range(kq)]
    specs += [pick(lambda f, a, b: b, r, k) for r in range(per_piece) for k in range(kq)]
    specs.append(pl.BlockSpec((per_piece, kq, BLOCK, BLOCK), lambda g, f, a, b: (g, 0, 0, 0)))
    out_spec = pl.BlockSpec((per_piece, BLOCK, width), lambda g, f, a, b: (g, 0, 0))
    summed = pl.pallas_call(
        products_kernel,
        out_shape=jax.ShapeDtypeStruct((rows, BLOCK, width), jnp.float32),
        grid_spec=pltpu.PrefetchScalarGridSpec(
            num_scalar_prefetch=3,
            grid=(rows // per_piece,),
            in_specs=specs,
            out_specs=out_spec,
        ),
    )(flag, first, second, *([panels[0]] * (per_piece * kq)), *([panels[1]] * (per_piece * kq)), adj_tiles[:, 0])
    return summed.reshape(-1, width)


def local(node_feats, adj_tiles, col_index, w_in, b_in, w_out, b_out, cot_out):
    per_piece = node_feats.shape[0] // BLOCK
    index = staged_index(col_index[:, 0, :], per_piece)
    panels = gather_blk(node_feats, 0)
    partial_sum = tile_products(panels, adj_tiles, index, 2 * per_piece)
    agg = reduce_rep(partial_sum, 8)
    agg_b = agg.astype(jnp.bfloat16)
    pre = jnp.dot(agg_b, w_in, preferred_element_type=jnp.float32) + b_in
    hidden = jax.nn.silu(pre).astype(jnp.bfloat16)
    projected = jnp.dot(hidden, w_out, preferred_element_type=jnp.float32) + b_out
    out_feats = (node_feats.astype(jnp.float32) + projected).astype(jnp.bfloat16)
    g_hidden = jnp.einsum("nh,fh->nf", cot_out, w_out, preferred_element_type=jnp.float32)
    sigma = jax.nn.sigmoid(pre)
    g_pre = (g_hidden * sigma * (1.0 + pre * (1.0 - sigma))).astype(jnp.bfloat16)
    g_agg = jnp.einsum("nf,hf->nh", g_pre, w_in, preferred_element_type=jnp.float32).astype(
        jnp.bfloat16
    )
    g_panels = gather_blk(g_agg, 1)
    back_partial = tile_products(g_panels, adj_tiles, index, 2 * per_piece)
    back_rows = reduce_rep(back_partial, 9)
    grad_feats = (cot_out.astype(jnp.float32) + back_rows).astype(jnp.bfloat16)
    return (out_feats, grad_feats)


def solution(mesh):
    nblk = mesh.shape["blk"]
    nrep = mesh.shape["rep"]
    fine = Mesh(mesh.devices.reshape(nblk // 16, 2, 8, nrep // 2, 2), NAMES)
    rows = P(BLK + REP, None)
    placed = (
        rows,
        P(BLK, REP, None, None, None),
        P(BLK, REP, None),
        P(),
        P(),
        P(),
        P(),
        rows,
    )
    return jax.shard_map(
        local,
        mesh=fine,
        in_specs=placed,
        out_specs=(rows, rows),
        check_vma=False,
    )
```

```python
import functools

import jax
import jax.numpy as jnp
from jax import lax
from jax.experimental import pallas as pl
from jax.experimental.pallas import tpu as pltpu
from jax.sharding import Mesh
from jax.sharding import PartitionSpec as P

BLOCK = 128
NAMES = ("x", "ylo", "z", "yhi", "core")
BLK = ("x", "ylo", "z")
REP = ("yhi", "core")


def group_place(axes):
    sizes = [lax.axis_size(a) for a in axes]
    me = 0
    for a, n in zip(axes, sizes):
        me = me * n + lax.axis_index(a)
    return me, sizes


def peer_id(axes, sizes, p):
    coords = {}
    for a, n in reversed(list(zip(axes, sizes))):
        coords[a] = p % n
        p = p // n
    return coords


def neighbours():
    nx, ny, nz = lax.axis_size("x"), lax.axis_size("ylo"), lax.axis_size("z")
    x, y, z = lax.axis_index("x"), lax.axis_index("ylo"), lax.axis_index("z")
    right, left, other = lax.rem(x + 1, nx), lax.rem(x + nx - 1, nx), ny - 1 - y
    return {"x": right}, {"x": left}, {"ylo": other}, {"z": lax.rem(z + 1, nz)}, {"z": lax.rem(z + nz - 1, nz)}


def gather_phase(phase, ring_src, tree_src, ring_out, tree_out, send_sem, recv_sem, local_sem):
    nx, ny, nz = lax.axis_size("x"), lax.axis_size("ylo"), lax.axis_size("z")
    x, y, z = lax.axis_index("x"), lax.axis_index("ylo"), lax.axis_index("z")
    right, left, other = lax.rem(x + 1, nx), lax.rem(x + nx - 1, nx), ny - 1 - y
    to_right, to_left, to_other, up, down = neighbours()

    def send(kind, src, dst, peer):
        copy = pltpu.make_async_remote_copy(
            src_ref=src,
            dst_ref=dst,
            send_sem=send_sem.at[phase, kind],
            recv_sem=recv_sem.at[phase, kind],
            device_id=peer,
        )
        copy.start()
        return copy

    me = x * ny + y
    own_tree = pltpu.make_async_copy(tree_src, tree_out.at[me], local_sem.at[phase, 0])
    own_tree.start()
    own_ring = pltpu.make_async_copy(ring_src, ring_out.at[z], local_sem.at[phase, 1])
    own_ring.start()
    first_right = send(0, tree_src, tree_out.at[me], to_right)
    first_left = send(1, tree_src, tree_out.at[me], to_left)
    first_other = send(2, tree_src, tree_out.at[me], to_other)
    steps = nz // 2
    split = ring_src.shape[0] // 2
    ups = [send(9, ring_src, ring_out.at[z], up)]
    downs = [send(9 + steps, ring_src, ring_out.at[z], down)]

    def ring_step(s):
        below = lax.rem(z + nz - (s - 1), nz)
        above = lax.rem(z + s - 1, nz)
        ups[-1].wait_recv()
        downs[-1].wait_recv()
        if s < steps:
            ups.append(send(9 + s - 1, ring_out.at[below], ring_out.at[below], up))
            downs.append(send(9 + steps + s - 1, ring_out.at[above], ring_out.at[above], down))
        else:
            ups.append(send(9 + s - 1, ring_out.at[below, :split], ring_out.at[below, :split], up))
            downs.append(send(9 + steps + s - 1, ring_out.at[above, split:], ring_out.at[above, split:], down))

    tree_split = tree_src.shape[0] // 2
    first_right.wait_recv()
    from_left = left * ny + y
    second_right = send(3, tree_out.at[from_left, :tree_split], tree_out.at[from_left, :tree_split], to_right)
    first_left.wait_recv()
    from_right = right * ny + y
    second_left = send(7, tree_out.at[from_right, tree_split:], tree_out.at[from_right, tree_split:], to_left)
    ring_step(2)
    first_other.wait_recv()
    from_other = x * ny + other
    other_right = send(4, tree_out.at[from_other], tree_out.at[from_other], to_right)
    other_left = send(5, tree_out.at[from_other], tree_out.at[from_other], to_left)
    ring_step(3)
    other_right.wait_recv()
    from_left_other = left * ny + other
    third_right = send(
        6, tree_out.at[from_left_other, :tree_split], tree_out.at[from_left_other, :tree_split], to_right
    )
    other_left.wait_recv()
    from_right_other = right * ny + other
    third_left = send(
        8, tree_out.at[from_right_other, tree_split:], tree_out.at[from_right_other, tree_split:], to_left
    )
    for s in range(4, steps + 1):
        ring_step(s)
    for copy in (second_right, second_left, third_right, third_left, ups[-1], downs[-1]):
        copy.wait_recv()
    tree = [first_right, first_left, first_other, second_right, second_left]
    tree += [other_right, other_left, third_right, third_left]
    return tree + ups + downs, [own_tree, own_ring]


def phase_one(ring_src, tree_src, ring_out, tree_out, send_sem, recv_sem, local_sem):
    nx, ny, nz = lax.axis_size("x"), lax.axis_size("ylo"), lax.axis_size("z")
    x, y, z = lax.axis_index("x"), lax.axis_index("ylo"), lax.axis_index("z")

    def send(kind, src, dst, peer):
        copy = pltpu.make_async_remote_copy(
            src_ref=src, dst_ref=dst, send_sem=send_sem.at[0, kind], recv_sem=recv_sem.at[0, kind], device_id=peer
        )
        copy.start()
        return copy

    def on_z(step):
        return {"z": lax.rem(z + nz + step, nz)}

    me = x * ny + y
    own_tree = pltpu.make_async_copy(tree_src, tree_out.at[me], local_sem.at[0, 0])
    own_tree.start()
    own_ring = pltpu.make_async_copy(ring_src, ring_out.at[z], local_sem.at[0, 1])
    own_ring.start()
    n = nx * ny
    sends = []
    for d in range(1, n):
        p = lax.rem(me + d, n)
        sends.append(send(d - 1, tree_src, tree_out.at[me], {"x": p // ny, "ylo": p % ny}))
    kind = n - 1
    up_one = send(kind, ring_src, ring_out.at[z], on_z(1))
    down_one = send(kind + 1, ring_src, ring_out.at[z], on_z(-1))
    up_two = send(kind + 2, ring_src, ring_out.at[z], on_z(2))
    down_two = send(kind + 3, ring_src, ring_out.at[z], on_z(-2))
    split = ring_src.shape[0] // 2
    up_two.wait_recv()
    below = lax.rem(z + nz - 2, nz)
    fwd_up_one = send(kind + 4, ring_out.at[below], ring_out.at[below], on_z(1))
    fwd_up_two = send(kind + 5, ring_out.at[below, :split], ring_out.at[below, :split], on_z(2))
    down_two.wait_recv()
    above = lax.rem(z + 2, nz)
    fwd_down_one = send(kind + 6, ring_out.at[above], ring_out.at[above], on_z(-1))
    fwd_down_two = send(kind + 7, ring_out.at[above, split:], ring_out.at[above, split:], on_z(-2))
    ring = [up_one, down_one, up_two, down_two, fwd_up_one, fwd_up_two, fwd_down_one, fwd_down_two]
    for copy in sends + [up_one, down_one, fwd_up_one, fwd_up_two, fwd_down_one, fwd_down_two]:
        copy.wait_recv()
    return sends + ring, [own_tree, own_ring]


def gather_kernel(rows_ref, mid_ring, mid_tree, ring_out, tree_out, send_sem, recv_sem, local_sem):
    nx, ny, nz = lax.axis_size("x"), lax.axis_size("ylo"), lax.axis_size("z")
    x, y, z = lax.axis_index("x"), lax.axis_index("ylo"), lax.axis_index("z")
    me = x * ny + y
    peers = [{"x": lax.rem(me + d, nx * ny) // ny, "ylo": lax.rem(me + d, nx * ny) % ny} for d in range(1, nx * ny)]
    peers += [{"z": lax.rem(z + nz + step, nz)} for step in (1, -1, 2, -2)]
    barrier = pltpu.get_barrier_semaphore()
    for peer in peers:
        pl.semaphore_signal(barrier, 1, device_id=peer)
    pl.semaphore_wait(barrier, len(peers))
    half = rows_ref.shape[0] // 2
    ring_src, tree_src = rows_ref.at[pl.ds(half, half)], rows_ref.at[pl.ds(0, half)]
    sends, local = phase_one(ring_src, tree_src, mid_ring, mid_tree, send_sem, recv_sem, local_sem)
    for copy in local:
        copy.wait()
    more, local = gather_phase(1, mid_tree, mid_ring, ring_out, tree_out, send_sem, recv_sem, local_sem)
    for copy in sends + more:
        copy.wait_send()
    for copy in local:
        copy.wait()


def gather_blk(rows, cid):
    nz = lax.axis_size("z")
    nxy = lax.axis_size("x") * lax.axis_size("ylo")
    half = rows.shape[0] // 2
    width = rows.shape[1]
    piece = (half, width)
    any_space = pl.BlockSpec(memory_space=pl.ANY)
    _, _, first, second = pl.pallas_call(
        gather_kernel,
        out_shape=(
            jax.ShapeDtypeStruct((nz, *piece), rows.dtype),
            jax.ShapeDtypeStruct((nxy, *piece), rows.dtype),
            jax.ShapeDtypeStruct((nz, nxy, *piece), rows.dtype),
            jax.ShapeDtypeStruct((nxy, nz, *piece), rows.dtype),
        ),
        in_specs=[any_space],
        out_specs=(any_space,) * 4,
        scratch_shapes=[
            pltpu.SemaphoreType.DMA((2, 9 + nz)),
            pltpu.SemaphoreType.DMA((2, 9 + nz)),
            pltpu.SemaphoreType.DMA((2, 2)),
        ],
        compiler_params=pltpu.CompilerParams(collective_id=cid, has_side_effects=True),
    )(rows)
    return first.reshape(-1, BLOCK, width), second.reshape(-1, BLOCK, width)


def reduce_kernel(src_ref, out_ref, own, landed, mid, last, send_sem, recv_sem, local_sem):
    nyhi, ncore = lax.axis_size("yhi"), lax.axis_size("core")
    yhi, core = lax.axis_index("yhi"), lax.axis_index("core")
    other_core, other_yhi = ncore - 1 - core, nyhi - 1 - yhi
    to_core, to_yhi = {"core": other_core}, {"yhi": other_yhi}
    barrier = pltpu.get_barrier_semaphore()
    for peer in (to_core, to_yhi):
        pl.semaphore_signal(barrier, 1, device_id=peer)
    pl.semaphore_wait(barrier, 2)
    copies, locals_ = [], []
    for h in range(nyhi):
        copy = pltpu.make_async_remote_copy(
            src_ref=src_ref.at[h * ncore + other_core],
            dst_ref=landed.at[h],
            send_sem=send_sem.at[h],
            recv_sem=recv_sem.at[h],
            device_id=to_core,
        )
        copy.start()
        copies.append(copy)
        keep = pltpu.make_async_copy(src_ref.at[h * ncore + core], own.at[h], local_sem.at[h])
        keep.start()
        locals_.append(keep)
    for copy in copies:
        copy.wait_recv()
    for keep in locals_:
        keep.wait()
    mid[...] = own[...] + landed[...]
    cross = pltpu.make_async_remote_copy(
        src_ref=mid.at[other_yhi],
        dst_ref=last,
        send_sem=send_sem.at[nyhi],
        recv_sem=recv_sem.at[nyhi],
        device_id=to_yhi,
    )
    cross.start()
    cross.wait_recv()
    out_ref[...] = mid[yhi] + last[...]
    for copy in copies:
        copy.wait_send()
    cross.wait_send()


def reduce_rep(partial, cid):
    nyhi, ncore = lax.axis_size("yhi"), lax.axis_size("core")
    pieces = partial.reshape(nyhi * ncore, -1, partial.shape[1])
    piece = pieces.shape[1:]
    return pl.pallas_call(
        reduce_kernel,
        out_shape=jax.ShapeDtypeStruct(piece, pieces.dtype),
        in_specs=[pl.BlockSpec(memory_space=pl.ANY)],
        out_specs=pl.BlockSpec(memory_space=pltpu.VMEM),
        scratch_shapes=[
            pltpu.VMEM((nyhi, *piece), pieces.dtype),
            pltpu.VMEM((nyhi, *piece), pieces.dtype),
            pltpu.VMEM((nyhi, *piece), pieces.dtype),
            pltpu.VMEM(piece, pieces.dtype),
            pltpu.SemaphoreType.DMA((nyhi + 1,)),
            pltpu.SemaphoreType.DMA((nyhi + 1,)),
            pltpu.SemaphoreType.DMA((nyhi,)),
        ],
        compiler_params=pltpu.CompilerParams(collective_id=cid, has_side_effects=True),
    )(pieces)


def staged_index(col, per_owner):
    nz = lax.axis_size("z")
    nxy = lax.axis_size("x") * lax.axis_size("ylo")
    half = per_owner // 2
    owner = col // per_owner
    sub = col % per_owner
    z = owner % nz
    xy = owner // nz
    in_first = sub < half
    first = (z * nxy + xy) * half + jnp.where(in_first, sub, 0)
    second = (xy * nz + z) * half + jnp.where(in_first, 0, sub - half)
    return in_first.astype(jnp.int32), first, second


def products_kernel(flag_ref, first_ref, second_ref, *refs):
    adj_ref, out_ref = refs[-2:]
    rows, kq = adj_ref.shape[0], adj_ref.shape[1]
    firsts, seconds = refs[: rows * kq], refs[rows * kq : 2 * rows * kq]
    base = pl.program_id(0) * rows
    for r in range(rows):
        acc = jnp.zeros(out_ref.shape[1:], jnp.float32)
        for k in range(kq):
            at = r * kq + k
            block = jnp.where(flag_ref[base + r, k] != 0, firsts[at][0], seconds[at][0])
            acc = acc + jnp.dot(adj_ref[r, k], block, preferred_element_type=jnp.float32)
        out_ref[r] = acc


def tile_products(panels, adj_tiles, index, per_piece):
    flag, first, second = index
    rows, kq = flag.shape
    width = panels[0].shape[2]
    tile = (1, BLOCK, width)

    def pick(table, r, k):
        return pl.BlockSpec(tile, lambda g, f, a, b: (table(f, a, b)[g * per_piece + r, k], 0, 0))

    specs = [pick(lambda f, a, b: a, r, k) for r in range(per_piece) for k in range(kq)]
    specs += [pick(lambda f, a, b: b, r, k) for r in range(per_piece) for k in range(kq)]
    specs.append(pl.BlockSpec((per_piece, kq, BLOCK, BLOCK), lambda g, f, a, b: (g, 0, 0, 0)))
    out_spec = pl.BlockSpec((per_piece, BLOCK, width), lambda g, f, a, b: (g, 0, 0))
    summed = pl.pallas_call(
        products_kernel,
        out_shape=jax.ShapeDtypeStruct((rows, BLOCK, width), jnp.float32),
        grid_spec=pltpu.PrefetchScalarGridSpec(
            num_scalar_prefetch=3,
            grid=(rows // per_piece,),
            in_specs=specs,
            out_specs=out_spec,
        ),
    )(flag, first, second, *([panels[0]] * (per_piece * kq)), *([panels[1]] * (per_piece * kq)), adj_tiles[:, 0])
    return summed.reshape(-1, width)


def local(node_feats, adj_tiles, col_index, w_in, b_in, w_out, b_out, cot_out):
    per_piece = node_feats.shape[0] // BLOCK
    index = staged_index(col_index[:, 0, :], per_piece)
    panels = gather_blk(node_feats, 0)
    partial_sum = tile_products(panels, adj_tiles, index, 2 * per_piece)
    agg = reduce_rep(partial_sum, 8)
    agg_b = agg.astype(jnp.bfloat16)
    pre = jnp.dot(agg_b, w_in, preferred_element_type=jnp.float32) + b_in
    hidden = jax.nn.silu(pre).astype(jnp.bfloat16)
    projected = jnp.dot(hidden, w_out, preferred_element_type=jnp.float32) + b_out
    out_feats = (node_feats.astype(jnp.float32) + projected).astype(jnp.bfloat16)
    g_hidden = jnp.einsum("nh,fh->nf", cot_out, w_out, preferred_element_type=jnp.float32)
    sigma = jax.nn.sigmoid(pre)
    g_pre = (g_hidden * sigma * (1.0 + pre * (1.0 - sigma))).astype(jnp.bfloat16)
    g_agg = jnp.einsum("nf,hf->nh", g_pre, w_in, preferred_element_type=jnp.float32).astype(
        jnp.bfloat16
    )
    g_panels = gather_blk(g_agg, 1)
    back_partial = tile_products(g_panels, adj_tiles, index, 2 * per_piece)
    back_rows = reduce_rep(back_partial, 9)
    grad_feats = (cot_out.astype(jnp.float32) + back_rows).astype(jnp.bfloat16)
    return (out_feats, grad_feats)


def solution(mesh):
    nblk = mesh.shape["blk"]
    nrep = mesh.shape["rep"]
    fine = Mesh(mesh.devices.reshape(nblk // 16, 2, 8, nrep // 2, 2), NAMES)
    rows = P(BLK + REP, None)
    placed = (
        rows,
        P(BLK, REP, None, None, None),
        P(BLK, REP, None),
        P(),
        P(),
        P(),
        P(),
        rows,
    )
    return jax.shard_map(
        local,
        mesh=fine,
        in_specs=placed,
        out_specs=(rows, rows),
        check_vma=False,
    )
```

```python
import functools

import jax
import jax.numpy as jnp
from jax import lax
from jax.experimental import pallas as pl
from jax.experimental.pallas import tpu as pltpu
from jax.sharding import Mesh
from jax.sharding import PartitionSpec as P

BLOCK = 128
NAMES = ("x", "ylo", "z", "yhi", "core")
BLK = ("x", "ylo", "z")
REP = ("yhi", "core")


def group_place(axes):
    sizes = [lax.axis_size(a) for a in axes]
    me = 0
    for a, n in zip(axes, sizes):
        me = me * n + lax.axis_index(a)
    return me, sizes


def peer_id(axes, sizes, p):
    coords = {}
    for a, n in reversed(list(zip(axes, sizes))):
        coords[a] = p % n
        p = p // n
    return coords


def neighbours():
    nx, ny, nz = lax.axis_size("x"), lax.axis_size("ylo"), lax.axis_size("z")
    x, y, z = lax.axis_index("x"), lax.axis_index("ylo"), lax.axis_index("z")
    right, left, other = lax.rem(x + 1, nx), lax.rem(x + nx - 1, nx), ny - 1 - y
    return {"x": right}, {"x": left}, {"ylo": other}, {"z": lax.rem(z + 1, nz)}, {"z": lax.rem(z + nz - 1, nz)}


def gather_phase(phase, ring_src, tree_src, ring_out, tree_out, send_sem, recv_sem, local_sem):
    nx, ny, nz = lax.axis_size("x"), lax.axis_size("ylo"), lax.axis_size("z")
    x, y, z = lax.axis_index("x"), lax.axis_index("ylo"), lax.axis_index("z")
    right, left, other = lax.rem(x + 1, nx), lax.rem(x + nx - 1, nx), ny - 1 - y
    to_right, to_left, to_other, up, down = neighbours()

    def send(kind, src, dst, peer):
        copy = pltpu.make_async_remote_copy(
            src_ref=src,
            dst_ref=dst,
            send_sem=send_sem.at[phase, kind],
            recv_sem=recv_sem.at[phase, kind],
            device_id=peer,
        )
        copy.start()
        return copy

    me = x * ny + y
    own_tree = pltpu.make_async_copy(tree_src, tree_out.at[me], local_sem.at[phase, 0])
    own_tree.start()
    own_ring = pltpu.make_async_copy(ring_src, ring_out.at[z], local_sem.at[phase, 1])
    own_ring.start()
    first_right = send(0, tree_src, tree_out.at[me], to_right)
    first_left = send(1, tree_src, tree_out.at[me], to_left)
    first_other = send(2, tree_src, tree_out.at[me], to_other)
    steps = nz // 2
    split = ring_src.shape[0] // 2
    ups = [send(9, ring_src, ring_out.at[z], up)]
    downs = [send(9 + steps, ring_src, ring_out.at[z], down)]

    def ring_step(s):
        below = lax.rem(z + nz - (s - 1), nz)
        above = lax.rem(z + s - 1, nz)
        ups[-1].wait_recv()
        downs[-1].wait_recv()
        if s < steps:
            ups.append(send(9 + s - 1, ring_out.at[below], ring_out.at[below], up))
            downs.append(send(9 + steps + s - 1, ring_out.at[above], ring_out.at[above], down))
        else:
            ups.append(send(9 + s - 1, ring_out.at[below, :split], ring_out.at[below, :split], up))
            downs.append(send(9 + steps + s - 1, ring_out.at[above, split:], ring_out.at[above, split:], down))

    tree_split = tree_src.shape[0] // 2
    first_right.wait_recv()
    from_left = left * ny + y
    second_right = send(3, tree_out.at[from_left, :tree_split], tree_out.at[from_left, :tree_split], to_right)
    first_left.wait_recv()
    from_right = right * ny + y
    second_left = send(7, tree_out.at[from_right, tree_split:], tree_out.at[from_right, tree_split:], to_left)
    ring_step(2)
    first_other.wait_recv()
    from_other = x * ny + other
    other_right = send(4, tree_out.at[from_other], tree_out.at[from_other], to_right)
    other_left = send(5, tree_out.at[from_other], tree_out.at[from_other], to_left)
    ring_step(3)
    other_right.wait_recv()
    from_left_other = left * ny + other
    third_right = send(
        6, tree_out.at[from_left_other, :tree_split], tree_out.at[from_left_other, :tree_split], to_right
    )
    other_left.wait_recv()
    from_right_other = right * ny + other
    third_left = send(
        8, tree_out.at[from_right_other, tree_split:], tree_out.at[from_right_other, tree_split:], to_left
    )
    for s in range(4, steps + 1):
        ring_step(s)
    for copy in (second_right, second_left, third_right, third_left, ups[-1], downs[-1]):
        copy.wait_recv()
    tree = [first_right, first_left, first_other, second_right, second_left]
    tree += [other_right, other_left, third_right, third_left]
    return tree + ups + downs, [own_tree, own_ring]


def phase_one(ring_src, tree_src, ring_out, tree_out, send_sem, recv_sem, local_sem):
    nx, ny, nz = lax.axis_size("x"), lax.axis_size("ylo"), lax.axis_size("z")
    x, y, z = lax.axis_index("x"), lax.axis_index("ylo"), lax.axis_index("z")

    def send(kind, src, dst, peer):
        copy = pltpu.make_async_remote_copy(
            src_ref=src, dst_ref=dst, send_sem=send_sem.at[0, kind], recv_sem=recv_sem.at[0, kind], device_id=peer
        )
        copy.start()
        return copy

    def on_z(step):
        return {"z": lax.rem(z + nz + step, nz)}

    me = x * ny + y
    own_tree = pltpu.make_async_copy(tree_src, tree_out.at[me], local_sem.at[0, 0])
    own_tree.start()
    own_ring = pltpu.make_async_copy(ring_src, ring_out.at[z], local_sem.at[0, 1])
    own_ring.start()
    n = nx * ny
    sends = []
    for d in range(1, n):
        p = lax.rem(me + d, n)
        sends.append(send(d - 1, tree_src, tree_out.at[me], {"x": p // ny, "ylo": p % ny}))
    kind = n - 1
    up_one = send(kind, ring_src, ring_out.at[z], on_z(1))
    down_one = send(kind + 1, ring_src, ring_out.at[z], on_z(-1))
    up_two = send(kind + 2, ring_src, ring_out.at[z], on_z(2))
    down_two = send(kind + 3, ring_src, ring_out.at[z], on_z(-2))
    split = ring_src.shape[0] // 2
    up_two.wait_recv()
    below = lax.rem(z + nz - 2, nz)
    fwd_up_one = send(kind + 4, ring_out.at[below], ring_out.at[below], on_z(1))
    fwd_up_two = send(kind + 5, ring_out.at[below, :split], ring_out.at[below, :split], on_z(2))
    down_two.wait_recv()
    above = lax.rem(z + 2, nz)
    fwd_down_one = send(kind + 6, ring_out.at[above], ring_out.at[above], on_z(-1))
    fwd_down_two = send(kind + 7, ring_out.at[above, split:], ring_out.at[above, split:], on_z(-2))
    ring = [up_one, down_one, up_two, down_two, fwd_up_one, fwd_up_two, fwd_down_one, fwd_down_two]
    for copy in sends + [up_one, down_one, fwd_up_one, fwd_up_two, fwd_down_one, fwd_down_two]:
        copy.wait_recv()
    return sends + ring, [own_tree, own_ring]


def gather_kernel(rows_ref, mid_ring, mid_tree, ring_out, tree_out, send_sem, recv_sem, local_sem):
    nx, ny, nz = lax.axis_size("x"), lax.axis_size("ylo"), lax.axis_size("z")
    x, y, z = lax.axis_index("x"), lax.axis_index("ylo"), lax.axis_index("z")
    me = x * ny + y
    peers = [{"x": lax.rem(me + d, nx * ny) // ny, "ylo": lax.rem(me + d, nx * ny) % ny} for d in range(1, nx * ny)]
    peers += [{"z": lax.rem(z + nz + step, nz)} for step in (1, -1, 2, -2)]
    barrier = pltpu.get_barrier_semaphore()
    for peer in peers:
        pl.semaphore_signal(barrier, 1, device_id=peer)
    pl.semaphore_wait(barrier, len(peers))
    half = rows_ref.shape[0] // 2
    ring_src, tree_src = rows_ref.at[pl.ds(half, half)], rows_ref.at[pl.ds(0, half)]
    sends, local = phase_one(ring_src, tree_src, mid_ring, mid_tree, send_sem, recv_sem, local_sem)
    for copy in local:
        copy.wait()
    more, local = gather_phase(1, mid_tree, mid_ring, ring_out, tree_out, send_sem, recv_sem, local_sem)
    for copy in sends + more:
        copy.wait_send()
    for copy in local:
        copy.wait()


def gather_blk(rows, cid):
    nz = lax.axis_size("z")
    nxy = lax.axis_size("x") * lax.axis_size("ylo")
    half = rows.shape[0] // 2
    width = rows.shape[1]
    piece = (half, width)
    any_space = pl.BlockSpec(memory_space=pl.ANY)
    _, _, first, second = pl.pallas_call(
        gather_kernel,
        out_shape=(
            jax.ShapeDtypeStruct((nz, *piece), rows.dtype),
            jax.ShapeDtypeStruct((nxy, *piece), rows.dtype),
            jax.ShapeDtypeStruct((nz, nxy, *piece), rows.dtype),
            jax.ShapeDtypeStruct((nxy, nz, *piece), rows.dtype),
        ),
        in_specs=[any_space],
        out_specs=(any_space,) * 4,
        scratch_shapes=[
            pltpu.SemaphoreType.DMA((2, 9 + nz)),
            pltpu.SemaphoreType.DMA((2, 9 + nz)),
            pltpu.SemaphoreType.DMA((2, 2)),
        ],
        compiler_params=pltpu.CompilerParams(collective_id=cid, has_side_effects=True),
    )(rows)
    return first.reshape(-1, BLOCK, width), second.reshape(-1, BLOCK, width)


def reduce_kernel(src_ref, out_ref, own, landed, mid, last, send_sem, recv_sem, local_sem):
    nyhi, ncore = lax.axis_size("yhi"), lax.axis_size("core")
    yhi, core = lax.axis_index("yhi"), lax.axis_index("core")
    other_core, other_yhi = ncore - 1 - core, nyhi - 1 - yhi
    to_core, to_yhi = {"core": other_core}, {"yhi": other_yhi}
    barrier = pltpu.get_barrier_semaphore()
    for peer in (to_core, to_yhi):
        pl.semaphore_signal(barrier, 1, device_id=peer)
    pl.semaphore_wait(barrier, 2)
    copies, locals_ = [], []
    for h in range(nyhi):
        copy = pltpu.make_async_remote_copy(
            src_ref=src_ref.at[h * ncore + other_core],
            dst_ref=landed.at[h],
            send_sem=send_sem.at[h],
            recv_sem=recv_sem.at[h],
            device_id=to_core,
        )
        copy.start()
        copies.append(copy)
        keep = pltpu.make_async_copy(src_ref.at[h * ncore + core], own.at[h], local_sem.at[h])
        keep.start()
        locals_.append(keep)
    for copy in copies:
        copy.wait_recv()
    for keep in locals_:
        keep.wait()
    mid[other_yhi] = own[other_yhi] + landed[other_yhi]
    mid[yhi] = own[yhi] + landed[yhi]
    cross = pltpu.make_async_remote_copy(
        src_ref=mid.at[other_yhi],
        dst_ref=last,
        send_sem=send_sem.at[nyhi],
        recv_sem=recv_sem.at[nyhi],
        device_id=to_yhi,
    )
    cross.start()
    cross.wait_recv()
    out_ref[...] = mid[yhi] + last[...]
    for copy in copies:
        copy.wait_send()
    cross.wait_send()


def reduce_rep(partial, cid):
    nyhi, ncore = lax.axis_size("yhi"), lax.axis_size("core")
    pieces = partial.reshape(nyhi * ncore, -1, partial.shape[1])
    piece = pieces.shape[1:]
    return pl.pallas_call(
        reduce_kernel,
        out_shape=jax.ShapeDtypeStruct(piece, pieces.dtype),
        in_specs=[pl.BlockSpec(memory_space=pl.ANY)],
        out_specs=pl.BlockSpec(memory_space=pltpu.VMEM),
        scratch_shapes=[
            pltpu.VMEM((nyhi, *piece), pieces.dtype),
            pltpu.VMEM((nyhi, *piece), pieces.dtype),
            pltpu.VMEM((nyhi, *piece), pieces.dtype),
            pltpu.VMEM(piece, pieces.dtype),
            pltpu.SemaphoreType.DMA((nyhi + 1,)),
            pltpu.SemaphoreType.DMA((nyhi + 1,)),
            pltpu.SemaphoreType.DMA((nyhi,)),
        ],
        compiler_params=pltpu.CompilerParams(collective_id=cid, has_side_effects=True),
    )(pieces)


def staged_index(col, per_owner):
    nz = lax.axis_size("z")
    nxy = lax.axis_size("x") * lax.axis_size("ylo")
    half = per_owner // 2
    owner = col // per_owner
    sub = col % per_owner
    z = owner % nz
    xy = owner // nz
    in_first = sub < half
    first = (z * nxy + xy) * half + jnp.where(in_first, sub, 0)
    second = (xy * nz + z) * half + jnp.where(in_first, 0, sub - half)
    return in_first.astype(jnp.int32), first, second


def products_kernel(flag_ref, first_ref, second_ref, *refs):
    adj_ref, out_ref = refs[-2:]
    rows, kq = adj_ref.shape[0], adj_ref.shape[1]
    firsts, seconds = refs[: rows * kq], refs[rows * kq : 2 * rows * kq]
    base = pl.program_id(0) * rows
    for r in range(rows):
        acc = jnp.zeros(out_ref.shape[1:], jnp.float32)
        for k in range(kq):
            at = r * kq + k
            block = jnp.where(flag_ref[base + r, k] != 0, firsts[at][0], seconds[at][0])
            acc = acc + jnp.dot(adj_ref[r, k], block, preferred_element_type=jnp.float32)
        out_ref[r] = acc


def tile_products(panels, adj_tiles, index, per_piece):
    flag, first, second = index
    rows, kq = flag.shape
    width = panels[0].shape[2]
    tile = (1, BLOCK, width)

    def pick(table, r, k):
        return pl.BlockSpec(tile, lambda g, f, a, b: (table(f, a, b)[g * per_piece + r, k], 0, 0))

    specs = [pick(lambda f, a, b: a, r, k) for r in range(per_piece) for k in range(kq)]
    specs += [pick(lambda f, a, b: b, r, k) for r in range(per_piece) for k in range(kq)]
    specs.append(pl.BlockSpec((per_piece, kq, BLOCK, BLOCK), lambda g, f, a, b: (g, 0, 0, 0)))
    out_spec = pl.BlockSpec((per_piece, BLOCK, width), lambda g, f, a, b: (g, 0, 0))
    summed = pl.pallas_call(
        products_kernel,
        out_shape=jax.ShapeDtypeStruct((rows, BLOCK, width), jnp.float32),
        grid_spec=pltpu.PrefetchScalarGridSpec(
            num_scalar_prefetch=3,
            grid=(rows // per_piece,),
            in_specs=specs,
            out_specs=out_spec,
        ),
    )(flag, first, second, *([panels[0]] * (per_piece * kq)), *([panels[1]] * (per_piece * kq)), adj_tiles[:, 0])
    return summed.reshape(-1, width)


def local(node_feats, adj_tiles, col_index, w_in, b_in, w_out, b_out, cot_out):
    per_piece = node_feats.shape[0] // BLOCK
    index = staged_index(col_index[:, 0, :], per_piece)
    panels = gather_blk(node_feats, 0)
    partial_sum = tile_products(panels, adj_tiles, index, 2 * per_piece)
    agg = reduce_rep(partial_sum, 8)
    agg_b = agg.astype(jnp.bfloat16)
    pre = jnp.dot(agg_b, w_in, preferred_element_type=jnp.float32) + b_in
    hidden = jax.nn.silu(pre).astype(jnp.bfloat16)
    projected = jnp.dot(hidden, w_out, preferred_element_type=jnp.float32) + b_out
    out_feats = (node_feats.astype(jnp.float32) + projected).astype(jnp.bfloat16)
    g_hidden = jnp.einsum("nh,fh->nf", cot_out, w_out, preferred_element_type=jnp.float32)
    sigma = jax.nn.sigmoid(pre)
    g_pre = (g_hidden * sigma * (1.0 + pre * (1.0 - sigma))).astype(jnp.bfloat16)
    g_agg = jnp.einsum("nf,hf->nh", g_pre, w_in, preferred_element_type=jnp.float32).astype(
        jnp.bfloat16
    )
    g_panels = gather_blk(g_agg, 1)
    back_partial = tile_products(g_panels, adj_tiles, index, 2 * per_piece)
    back_rows = reduce_rep(back_partial, 9)
    grad_feats = (cot_out.astype(jnp.float32) + back_rows).astype(jnp.bfloat16)
    return (out_feats, grad_feats)


def solution(mesh):
    nblk = mesh.shape["blk"]
    nrep = mesh.shape["rep"]
    fine = Mesh(mesh.devices.reshape(nblk // 16, 2, 8, nrep // 2, 2), NAMES)
    rows = P(BLK + REP, None)
    placed = (
        rows,
        P(BLK, REP, None, None, None),
        P(BLK, REP, None),
        P(),
        P(),
        P(),
        P(),
        rows,
    )
    return jax.shard_map(
        local,
        mesh=fine,
        in_specs=placed,
        out_specs=(rows, rows),
        check_vma=False,
    )
```

```python
import functools

import jax
import jax.numpy as jnp
from jax import lax
from jax.experimental import pallas as pl
from jax.experimental.pallas import tpu as pltpu
from jax.sharding import Mesh
from jax.sharding import PartitionSpec as P

BLOCK = 128
NAMES = ("x", "ylo", "z", "yhi", "core")
BLK = ("x", "ylo", "z")
REP = ("yhi", "core")


def group_place(axes):
    sizes = [lax.axis_size(a) for a in axes]
    me = 0
    for a, n in zip(axes, sizes):
        me = me * n + lax.axis_index(a)
    return me, sizes


def peer_id(axes, sizes, p):
    coords = {}
    for a, n in reversed(list(zip(axes, sizes))):
        coords[a] = p % n
        p = p // n
    return coords


def neighbours():
    nx, ny, nz = lax.axis_size("x"), lax.axis_size("ylo"), lax.axis_size("z")
    x, y, z = lax.axis_index("x"), lax.axis_index("ylo"), lax.axis_index("z")
    right, left, other = lax.rem(x + 1, nx), lax.rem(x + nx - 1, nx), ny - 1 - y
    return {"x": right}, {"x": left}, {"ylo": other}, {"z": lax.rem(z + 1, nz)}, {"z": lax.rem(z + nz - 1, nz)}


def gather_phase(phase, ring_src, tree_src, ring_out, tree_out, send_sem, recv_sem, local_sem):
    nx, ny, nz = lax.axis_size("x"), lax.axis_size("ylo"), lax.axis_size("z")
    x, y, z = lax.axis_index("x"), lax.axis_index("ylo"), lax.axis_index("z")
    right, left, other = lax.rem(x + 1, nx), lax.rem(x + nx - 1, nx), ny - 1 - y
    to_right, to_left, to_other, up, down = neighbours()

    def send(kind, src, dst, peer):
        copy = pltpu.make_async_remote_copy(
            src_ref=src,
            dst_ref=dst,
            send_sem=send_sem.at[phase, kind],
            recv_sem=recv_sem.at[phase, kind],
            device_id=peer,
        )
        copy.start()
        return copy

    me = x * ny + y
    own_tree = pltpu.make_async_copy(tree_src, tree_out.at[me], local_sem.at[phase, 0])
    own_tree.start()
    own_ring = pltpu.make_async_copy(ring_src, ring_out.at[z], local_sem.at[phase, 1])
    own_ring.start()
    first_right = send(0, tree_src, tree_out.at[me], to_right)
    first_left = send(1, tree_src, tree_out.at[me], to_left)
    first_other = send(2, tree_src, tree_out.at[me], to_other)
    steps = nz // 2
    slots = ring_src.shape[0]
    miss = slots // 4
    keep = slots - miss
    lo = miss * y
    ups = [send(9, ring_src.at[pl.ds(lo, keep)], ring_out.at[z, pl.ds(lo, keep)], up)]
    downs = [send(9 + steps, ring_src.at[pl.ds(lo, keep)], ring_out.at[z, pl.ds(lo, keep)], down)]
    handed = []

    def hand(origin):
        part = pl.ds(keep * y, miss)
        handed.append(send(9 + 2 * steps + len(handed), ring_out.at[origin, part], ring_out.at[origin, part], to_other))

    def ring_step(s):
        below = lax.rem(z + nz - (s - 1), nz)
        above = lax.rem(z + s - 1, nz)
        ups[-1].wait_recv()
        downs[-1].wait_recv()
        hand(below)
        hand(above)
        if s < steps:
            part = pl.ds(lo, keep)
            ups.append(send(9 + s - 1, ring_out.at[below, part], ring_out.at[below, part], up))
            downs.append(send(9 + steps + s - 1, ring_out.at[above, part], ring_out.at[above, part], down))
        else:
            first, second = pl.ds(lo, keep // 2), pl.ds(lo + keep // 2, keep - keep // 2)
            ups.append(send(9 + s - 1, ring_out.at[below, first], ring_out.at[below, first], up))
            downs.append(send(9 + steps + s - 1, ring_out.at[above, second], ring_out.at[above, second], down))

    tree_split = tree_src.shape[0] // 2
    first_right.wait_recv()
    from_left = left * ny + y
    second_right = send(3, tree_out.at[from_left, :tree_split], tree_out.at[from_left, :tree_split], to_right)
    first_left.wait_recv()
    from_right = right * ny + y
    second_left = send(7, tree_out.at[from_right, tree_split:], tree_out.at[from_right, tree_split:], to_left)
    ring_step(2)
    first_other.wait_recv()
    from_other = x * ny + other
    other_right = send(4, tree_out.at[from_other], tree_out.at[from_other], to_right)
    other_left = send(5, tree_out.at[from_other], tree_out.at[from_other], to_left)
    ring_step(3)
    other_right.wait_recv()
    from_left_other = left * ny + other
    third_right = send(
        6, tree_out.at[from_left_other, :tree_split], tree_out.at[from_left_other, :tree_split], to_right
    )
    other_left.wait_recv()
    from_right_other = right * ny + other
    third_left = send(
        8, tree_out.at[from_right_other, tree_split:], tree_out.at[from_right_other, tree_split:], to_left
    )
    for s in range(4, steps + 1):
        ring_step(s)
    ups[-1].wait_recv()
    downs[-1].wait_recv()
    hand(lax.rem(z + steps, nz))
    for copy in [second_right, second_left, third_right, third_left] + handed:
        copy.wait_recv()
    tree = [first_right, first_left, first_other, second_right, second_left]
    tree += [other_right, other_left, third_right, third_left]
    return tree + ups + downs + handed, [own_tree, own_ring]


def phase_one(ring_src, tree_src, ring_out, tree_out, send_sem, recv_sem, local_sem):
    nx, ny, nz = lax.axis_size("x"), lax.axis_size("ylo"), lax.axis_size("z")
    x, y, z = lax.axis_index("x"), lax.axis_index("ylo"), lax.axis_index("z")

    def send(kind, src, dst, peer):
        copy = pltpu.make_async_remote_copy(
            src_ref=src, dst_ref=dst, send_sem=send_sem.at[0, kind], recv_sem=recv_sem.at[0, kind], device_id=peer
        )
        copy.start()
        return copy

    def on_z(step):
        return {"z": lax.rem(z + nz + step, nz)}

    me = x * ny + y
    own_tree = pltpu.make_async_copy(tree_src, tree_out.at[me], local_sem.at[0, 0])
    own_tree.start()
    own_ring = pltpu.make_async_copy(ring_src, ring_out.at[z], local_sem.at[0, 1])
    own_ring.start()
    n = nx * ny
    sends = []
    for d in range(1, n):
        p = lax.rem(me + d, n)
        sends.append(send(d - 1, tree_src, tree_out.at[me], {"x": p // ny, "ylo": p % ny}))
    kind = n - 1
    up_one = send(kind, ring_src, ring_out.at[z], on_z(1))
    down_one = send(kind + 1, ring_src, ring_out.at[z], on_z(-1))
    up_two = send(kind + 2, ring_src, ring_out.at[z], on_z(2))
    down_two = send(kind + 3, ring_src, ring_out.at[z], on_z(-2))
    split = ring_src.shape[0] // 2
    up_two.wait_recv()
    below = lax.rem(z + nz - 2, nz)
    fwd_up_one = send(kind + 4, ring_out.at[below], ring_out.at[below], on_z(1))
    fwd_up_two = send(kind + 5, ring_out.at[below, :split], ring_out.at[below, :split], on_z(2))
    down_two.wait_recv()
    above = lax.rem(z + 2, nz)
    fwd_down_one = send(kind + 6, ring_out.at[above], ring_out.at[above], on_z(-1))
    fwd_down_two = send(kind + 7, ring_out.at[above, split:], ring_out.at[above, split:], on_z(-2))
    ring = [up_one, down_one, up_two, down_two, fwd_up_one, fwd_up_two, fwd_down_one, fwd_down_two]
    for copy in sends + [up_one, down_one, fwd_up_one, fwd_up_two, fwd_down_one, fwd_down_two]:
        copy.wait_recv()
    return sends + ring, [own_tree, own_ring]


def gather_kernel(rows_ref, mid_ring, mid_tree, ring_out, tree_out, send_sem, recv_sem, local_sem):
    nx, ny, nz = lax.axis_size("x"), lax.axis_size("ylo"), lax.axis_size("z")
    x, y, z = lax.axis_index("x"), lax.axis_index("ylo"), lax.axis_index("z")
    me = x * ny + y
    peers = [{"x": lax.rem(me + d, nx * ny) // ny, "ylo": lax.rem(me + d, nx * ny) % ny} for d in range(1, nx * ny)]
    peers += [{"z": lax.rem(z + nz + step, nz)} for step in (1, -1, 2, -2)]
    barrier = pltpu.get_barrier_semaphore()
    for peer in peers:
        pl.semaphore_signal(barrier, 1, device_id=peer)
    pl.semaphore_wait(barrier, len(peers))
    half = rows_ref.shape[0] // 2
    ring_src, tree_src = rows_ref.at[pl.ds(half, half)], rows_ref.at[pl.ds(0, half)]
    sends, local = phase_one(ring_src, tree_src, mid_ring, mid_tree, send_sem, recv_sem, local_sem)
    for copy in local:
        copy.wait()
    more, local = gather_phase(1, mid_tree, mid_ring, ring_out, tree_out, send_sem, recv_sem, local_sem)
    for copy in sends + more:
        copy.wait_send()
    for copy in local:
        copy.wait()


def gather_blk(rows, cid):
    nz = lax.axis_size("z")
    nxy = lax.axis_size("x") * lax.axis_size("ylo")
    half = rows.shape[0] // 2
    width = rows.shape[1]
    piece = (half, width)
    any_space = pl.BlockSpec(memory_space=pl.ANY)
    _, _, first, second = pl.pallas_call(
        gather_kernel,
        out_shape=(
            jax.ShapeDtypeStruct((nz, *piece), rows.dtype),
            jax.ShapeDtypeStruct((nxy, *piece), rows.dtype),
            jax.ShapeDtypeStruct((nz, nxy, *piece), rows.dtype),
            jax.ShapeDtypeStruct((nxy, nz, *piece), rows.dtype),
        ),
        in_specs=[any_space],
        out_specs=(any_space,) * 4,
        scratch_shapes=[
            pltpu.SemaphoreType.DMA((2, 9 + 2 * nz)),
            pltpu.SemaphoreType.DMA((2, 9 + 2 * nz)),
            pltpu.SemaphoreType.DMA((2, 2)),
        ],
        compiler_params=pltpu.CompilerParams(collective_id=cid, has_side_effects=True),
    )(rows)
    return first.reshape(-1, BLOCK, width), second.reshape(-1, BLOCK, width)


def reduce_kernel(src_ref, out_ref, own, landed, mid, last, send_sem, recv_sem, local_sem):
    nyhi, ncore = lax.axis_size("yhi"), lax.axis_size("core")
    yhi, core = lax.axis_index("yhi"), lax.axis_index("core")
    other_core, other_yhi = ncore - 1 - core, nyhi - 1 - yhi
    to_core, to_yhi = {"core": other_core}, {"yhi": other_yhi}
    barrier = pltpu.get_barrier_semaphore()
    for peer in (to_core, to_yhi):
        pl.semaphore_signal(barrier, 1, device_id=peer)
    pl.semaphore_wait(barrier, 2)
    copies, locals_ = [], []
    for h in range(nyhi):
        copy = pltpu.make_async_remote_copy(
            src_ref=src_ref.at[h * ncore + other_core],
            dst_ref=landed.at[h],
            send_sem=send_sem.at[h],
            recv_sem=recv_sem.at[h],
            device_id=to_core,
        )
        copy.start()
        copies.append(copy)
        keep = pltpu.make_async_copy(src_ref.at[h * ncore + core], own.at[h], local_sem.at[h])
        keep.start()
        locals_.append(keep)
    for copy in copies:
        copy.wait_recv()
    for keep in locals_:
        keep.wait()
    mid[other_yhi] = own[other_yhi] + landed[other_yhi]
    mid[yhi] = own[yhi] + landed[yhi]
    cross = pltpu.make_async_remote_copy(
        src_ref=mid.at[other_yhi],
        dst_ref=last,
        send_sem=send_sem.at[nyhi],
        recv_sem=recv_sem.at[nyhi],
        device_id=to_yhi,
    )
    cross.start()
    cross.wait_recv()
    out_ref[...] = mid[yhi] + last[...]
    for copy in copies:
        copy.wait_send()
    cross.wait_send()


def reduce_rep(partial, cid):
    nyhi, ncore = lax.axis_size("yhi"), lax.axis_size("core")
    pieces = partial.reshape(nyhi * ncore, -1, partial.shape[1])
    piece = pieces.shape[1:]
    return pl.pallas_call(
        reduce_kernel,
        out_shape=jax.ShapeDtypeStruct(piece, pieces.dtype),
        in_specs=[pl.BlockSpec(memory_space=pl.ANY)],
        out_specs=pl.BlockSpec(memory_space=pltpu.VMEM),
        scratch_shapes=[
            pltpu.VMEM((nyhi, *piece), pieces.dtype),
            pltpu.VMEM((nyhi, *piece), pieces.dtype),
            pltpu.VMEM((nyhi, *piece), pieces.dtype),
            pltpu.VMEM(piece, pieces.dtype),
            pltpu.SemaphoreType.DMA((nyhi + 1,)),
            pltpu.SemaphoreType.DMA((nyhi + 1,)),
            pltpu.SemaphoreType.DMA((nyhi,)),
        ],
        compiler_params=pltpu.CompilerParams(collective_id=cid, has_side_effects=True),
    )(pieces)


def staged_index(col, per_owner):
    nz = lax.axis_size("z")
    nxy = lax.axis_size("x") * lax.axis_size("ylo")
    half = per_owner // 2
    owner = col // per_owner
    sub = col % per_owner
    z = owner % nz
    xy = owner // nz
    in_first = sub < half
    first = (z * nxy + xy) * half + jnp.where(in_first, sub, 0)
    second = (xy * nz + z) * half + jnp.where(in_first, 0, sub - half)
    return in_first.astype(jnp.int32), first, second


def products_kernel(flag_ref, first_ref, second_ref, *refs):
    adj_ref, out_ref = refs[-2:]
    rows, kq = adj_ref.shape[0], adj_ref.shape[1]
    firsts, seconds = refs[: rows * kq], refs[rows * kq : 2 * rows * kq]
    base = pl.program_id(0) * rows
    for r in range(rows):
        acc = jnp.zeros(out_ref.shape[1:], jnp.float32)
        for k in range(kq):
            at = r * kq + k
            block = jnp.where(flag_ref[base + r, k] != 0, firsts[at][0], seconds[at][0])
            acc = acc + jnp.dot(adj_ref[r, k], block, preferred_element_type=jnp.float32)
        out_ref[r] = acc


def tile_products(panels, adj_tiles, index, per_piece):
    flag, first, second = index
    rows, kq = flag.shape
    width = panels[0].shape[2]
    tile = (1, BLOCK, width)

    def pick(table, r, k):
        return pl.BlockSpec(tile, lambda g, f, a, b: (table(f, a, b)[g * per_piece + r, k], 0, 0))

    specs = [pick(lambda f, a, b: a, r, k) for r in range(per_piece) for k in range(kq)]
    specs += [pick(lambda f, a, b: b, r, k) for r in range(per_piece) for k in range(kq)]
    specs.append(pl.BlockSpec((per_piece, kq, BLOCK, BLOCK), lambda g, f, a, b: (g, 0, 0, 0)))
    out_spec = pl.BlockSpec((per_piece, BLOCK, width), lambda g, f, a, b: (g, 0, 0))
    summed = pl.pallas_call(
        products_kernel,
        out_shape=jax.ShapeDtypeStruct((rows, BLOCK, width), jnp.float32),
        grid_spec=pltpu.PrefetchScalarGridSpec(
            num_scalar_prefetch=3,
            grid=(rows // per_piece,),
            in_specs=specs,
            out_specs=out_spec,
        ),
    )(flag, first, second, *([panels[0]] * (per_piece * kq)), *([panels[1]] * (per_piece * kq)), adj_tiles[:, 0])
    return summed.reshape(-1, width)


def local(node_feats, adj_tiles, col_index, w_in, b_in, w_out, b_out, cot_out):
    per_piece = node_feats.shape[0] // BLOCK
    index = staged_index(col_index[:, 0, :], per_piece)
    panels = gather_blk(node_feats, 0)
    partial_sum = tile_products(panels, adj_tiles, index, 2 * per_piece)
    agg = reduce_rep(partial_sum, 8)
    agg_b = agg.astype(jnp.bfloat16)
    pre = jnp.dot(agg_b, w_in, preferred_element_type=jnp.float32) + b_in
    hidden = jax.nn.silu(pre).astype(jnp.bfloat16)
    projected = jnp.dot(hidden, w_out, preferred_element_type=jnp.float32) + b_out
    out_feats = (node_feats.astype(jnp.float32) + projected).astype(jnp.bfloat16)
    g_hidden = jnp.einsum("nh,fh->nf", cot_out, w_out, preferred_element_type=jnp.float32)
    sigma = jax.nn.sigmoid(pre)
    g_pre = (g_hidden * sigma * (1.0 + pre * (1.0 - sigma))).astype(jnp.bfloat16)
    g_agg = jnp.einsum("nf,hf->nh", g_pre, w_in, preferred_element_type=jnp.float32).astype(
        jnp.bfloat16
    )
    g_panels = gather_blk(g_agg, 1)
    back_partial = tile_products(g_panels, adj_tiles, index, 2 * per_piece)
    back_rows = reduce_rep(back_partial, 9)
    grad_feats = (cot_out.astype(jnp.float32) + back_rows).astype(jnp.bfloat16)
    return (out_feats, grad_feats)


def solution(mesh):
    nblk = mesh.shape["blk"]
    nrep = mesh.shape["rep"]
    fine = Mesh(mesh.devices.reshape(nblk // 16, 2, 8, nrep // 2, 2), NAMES)
    rows = P(BLK + REP, None)
    placed = (
        rows,
        P(BLK, REP, None, None, None),
        P(BLK, REP, None),
        P(),
        P(),
        P(),
        P(),
        rows,
    )
    return jax.shard_map(
        local,
        mesh=fine,
        in_specs=placed,
        out_specs=(rows, rows),
        check_vma=False,
    )
```

```python
import functools

import jax
import jax.numpy as jnp
from jax import lax
from jax.experimental import pallas as pl
from jax.experimental.pallas import tpu as pltpu
from jax.sharding import Mesh
from jax.sharding import PartitionSpec as P

BLOCK = 128
NAMES = ("x", "ylo", "z", "yhi", "core")
BLK = ("x", "ylo", "z")
REP = ("yhi", "core")


def group_place(axes):
    sizes = [lax.axis_size(a) for a in axes]
    me = 0
    for a, n in zip(axes, sizes):
        me = me * n + lax.axis_index(a)
    return me, sizes


def peer_id(axes, sizes, p):
    coords = {}
    for a, n in reversed(list(zip(axes, sizes))):
        coords[a] = p % n
        p = p // n
    return coords


def neighbours():
    nx, ny, nz = lax.axis_size("x"), lax.axis_size("ylo"), lax.axis_size("z")
    x, y, z = lax.axis_index("x"), lax.axis_index("ylo"), lax.axis_index("z")
    right, left, other = lax.rem(x + 1, nx), lax.rem(x + nx - 1, nx), ny - 1 - y
    return {"x": right}, {"x": left}, {"ylo": other}, {"z": lax.rem(z + 1, nz)}, {"z": lax.rem(z + nz - 1, nz)}


def gather_phase(phase, ring_src, tree_src, ring_out, tree_out, send_sem, recv_sem, local_sem):
    nx, ny, nz = lax.axis_size("x"), lax.axis_size("ylo"), lax.axis_size("z")
    x, y, z = lax.axis_index("x"), lax.axis_index("ylo"), lax.axis_index("z")
    right, left, other = lax.rem(x + 1, nx), lax.rem(x + nx - 1, nx), ny - 1 - y
    to_right, to_left, to_other, up, down = neighbours()

    def send(kind, src, dst, peer):
        copy = pltpu.make_async_remote_copy(
            src_ref=src,
            dst_ref=dst,
            send_sem=send_sem.at[phase, kind],
            recv_sem=recv_sem.at[phase, kind],
            device_id=peer,
        )
        copy.start()
        return copy

    me = x * ny + y
    own_tree = pltpu.make_async_copy(tree_src, tree_out.at[me], local_sem.at[phase, 0])
    own_tree.start()
    own_ring = pltpu.make_async_copy(ring_src, ring_out.at[z], local_sem.at[phase, 1])
    own_ring.start()
    first_right = send(0, tree_src, tree_out.at[me], to_right)
    first_left = send(1, tree_src, tree_out.at[me], to_left)
    first_other = send(2, tree_src, tree_out.at[me], to_other)
    steps = nz // 2
    half = ring_src.shape[0] // 2
    chunks = (pl.ds(0, half), pl.ds(half, half))
    ups = [[send(9 + c, ring_src.at[part], ring_out.at[z, part], up)] for c, part in enumerate(chunks)]
    downs = [
        [send(9 + 4 * steps + c, ring_src.at[part], ring_out.at[z, part], down)]
        for c, part in enumerate(chunks)
    ]

    def ring_step(s):
        below = lax.rem(z + nz - (s - 1), nz)
        above = lax.rem(z + s - 1, nz)
        for c, part in enumerate(chunks):
            ups[c][-1].wait_recv()
            if s < steps or c == 0:
                ups[c].append(send(9 + 2 * (s - 1) + c, ring_out.at[below, part], ring_out.at[below, part], up))
            downs[c][-1].wait_recv()
            if s < steps or c == 1:
                downs[c].append(
                    send(9 + 4 * steps + 2 * (s - 1) + c, ring_out.at[above, part], ring_out.at[above, part], down)
                )

    tree_split = tree_src.shape[0] // 2
    first_right.wait_recv()
    from_left = left * ny + y
    second_right = send(3, tree_out.at[from_left, :tree_split], tree_out.at[from_left, :tree_split], to_right)
    first_left.wait_recv()
    from_right = right * ny + y
    second_left = send(7, tree_out.at[from_right, tree_split:], tree_out.at[from_right, tree_split:], to_left)
    ring_step(2)
    first_other.wait_recv()
    from_other = x * ny + other
    other_right = send(4, tree_out.at[from_other], tree_out.at[from_other], to_right)
    other_left = send(5, tree_out.at[from_other], tree_out.at[from_other], to_left)
    ring_step(3)
    other_right.wait_recv()
    from_left_other = left * ny + other
    third_right = send(
        6, tree_out.at[from_left_other, :tree_split], tree_out.at[from_left_other, :tree_split], to_right
    )
    other_left.wait_recv()
    from_right_other = right * ny + other
    third_left = send(
        8, tree_out.at[from_right_other, tree_split:], tree_out.at[from_right_other, tree_split:], to_left
    )
    for s in range(4, steps + 1):
        ring_step(s)
    for copy in (second_right, second_left, third_right, third_left, ups[0][-1], downs[1][-1]):
        copy.wait_recv()
    tree = [first_right, first_left, first_other, second_right, second_left]
    tree += [other_right, other_left, third_right, third_left]
    return tree + ups[0] + ups[1] + downs[0] + downs[1], [own_tree, own_ring]


def phase_one(ring_src, tree_src, ring_out, tree_out, send_sem, recv_sem, local_sem):
    nx, ny, nz = lax.axis_size("x"), lax.axis_size("ylo"), lax.axis_size("z")
    x, y, z = lax.axis_index("x"), lax.axis_index("ylo"), lax.axis_index("z")

    def send(kind, src, dst, peer):
        copy = pltpu.make_async_remote_copy(
            src_ref=src, dst_ref=dst, send_sem=send_sem.at[0, kind], recv_sem=recv_sem.at[0, kind], device_id=peer
        )
        copy.start()
        return copy

    def on_z(step):
        return {"z": lax.rem(z + nz + step, nz)}

    me = x * ny + y
    own_tree = pltpu.make_async_copy(tree_src, tree_out.at[me], local_sem.at[0, 0])
    own_tree.start()
    own_ring = pltpu.make_async_copy(ring_src, ring_out.at[z], local_sem.at[0, 1])
    own_ring.start()
    n = nx * ny
    sends = []
    for d in range(1, n):
        p = lax.rem(me + d, n)
        sends.append(send(d - 1, tree_src, tree_out.at[me], {"x": p // ny, "ylo": p % ny}))
    kind = n - 1
    up_one = send(kind, ring_src, ring_out.at[z], on_z(1))
    down_one = send(kind + 1, ring_src, ring_out.at[z], on_z(-1))
    up_two = send(kind + 2, ring_src, ring_out.at[z], on_z(2))
    down_two = send(kind + 3, ring_src, ring_out.at[z], on_z(-2))
    split = ring_src.shape[0] // 2
    up_two.wait_recv()
    below = lax.rem(z + nz - 2, nz)
    fwd_up_one = send(kind + 4, ring_out.at[below], ring_out.at[below], on_z(1))
    fwd_up_two = send(kind + 5, ring_out.at[below, :split], ring_out.at[below, :split], on_z(2))
    down_two.wait_recv()
    above = lax.rem(z + 2, nz)
    fwd_down_one = send(kind + 6, ring_out.at[above], ring_out.at[above], on_z(-1))
    fwd_down_two = send(kind + 7, ring_out.at[above, split:], ring_out.at[above, split:], on_z(-2))
    ring = [up_one, down_one, up_two, down_two, fwd_up_one, fwd_up_two, fwd_down_one, fwd_down_two]
    for copy in sends + [up_one, down_one, fwd_up_one, fwd_up_two, fwd_down_one, fwd_down_two]:
        copy.wait_recv()
    return sends + ring, [own_tree, own_ring]


def gather_kernel(rows_ref, mid_ring, mid_tree, ring_out, tree_out, send_sem, recv_sem, local_sem):
    nx, ny, nz = lax.axis_size("x"), lax.axis_size("ylo"), lax.axis_size("z")
    x, y, z = lax.axis_index("x"), lax.axis_index("ylo"), lax.axis_index("z")
    me = x * ny + y
    peers = [{"x": lax.rem(me + d, nx * ny) // ny, "ylo": lax.rem(me + d, nx * ny) % ny} for d in range(1, nx * ny)]
    peers += [{"z": lax.rem(z + nz + step, nz)} for step in (1, -1, 2, -2)]
    barrier = pltpu.get_barrier_semaphore()
    for peer in peers:
        pl.semaphore_signal(barrier, 1, device_id=peer)
    pl.semaphore_wait(barrier, len(peers))
    half = rows_ref.shape[0] // 2
    ring_src, tree_src = rows_ref.at[pl.ds(half, half)], rows_ref.at[pl.ds(0, half)]
    sends, local = phase_one(ring_src, tree_src, mid_ring, mid_tree, send_sem, recv_sem, local_sem)
    for copy in local:
        copy.wait()
    more, local = gather_phase(1, mid_tree, mid_ring, ring_out, tree_out, send_sem, recv_sem, local_sem)
    for copy in sends + more:
        copy.wait_send()
    for copy in local:
        copy.wait()


def gather_blk(rows, cid):
    nz = lax.axis_size("z")
    nxy = lax.axis_size("x") * lax.axis_size("ylo")
    half = rows.shape[0] // 2
    width = rows.shape[1]
    piece = (half, width)
    any_space = pl.BlockSpec(memory_space=pl.ANY)
    _, _, first, second = pl.pallas_call(
        gather_kernel,
        out_shape=(
            jax.ShapeDtypeStruct((nz, *piece), rows.dtype),
            jax.ShapeDtypeStruct((nxy, *piece), rows.dtype),
            jax.ShapeDtypeStruct((nz, nxy, *piece), rows.dtype),
            jax.ShapeDtypeStruct((nxy, nz, *piece), rows.dtype),
        ),
        in_specs=[any_space],
        out_specs=(any_space,) * 4,
        scratch_shapes=[
            pltpu.SemaphoreType.DMA((2, 9 + 4 * nz)),
            pltpu.SemaphoreType.DMA((2, 9 + 4 * nz)),
            pltpu.SemaphoreType.DMA((2, 2)),
        ],
        compiler_params=pltpu.CompilerParams(collective_id=cid, has_side_effects=True),
    )(rows)
    return first.reshape(-1, BLOCK, width), second.reshape(-1, BLOCK, width)


def reduce_kernel(src_ref, out_ref, own, landed, mid, last, send_sem, recv_sem, local_sem):
    nyhi, ncore = lax.axis_size("yhi"), lax.axis_size("core")
    yhi, core = lax.axis_index("yhi"), lax.axis_index("core")
    other_core, other_yhi = ncore - 1 - core, nyhi - 1 - yhi
    to_core, to_yhi = {"core": other_core}, {"yhi": other_yhi}
    barrier = pltpu.get_barrier_semaphore()
    for peer in (to_core, to_yhi):
        pl.semaphore_signal(barrier, 1, device_id=peer)
    pl.semaphore_wait(barrier, 2)
    copies, locals_ = [], []
    for h in range(nyhi):
        copy = pltpu.make_async_remote_copy(
            src_ref=src_ref.at[h * ncore + other_core],
            dst_ref=landed.at[h],
            send_sem=send_sem.at[h],
            recv_sem=recv_sem.at[h],
            device_id=to_core,
        )
        copy.start()
        copies.append(copy)
        keep = pltpu.make_async_copy(src_ref.at[h * ncore + core], own.at[h], local_sem.at[h])
        keep.start()
        locals_.append(keep)
    for copy in copies:
        copy.wait_recv()
    for keep in locals_:
        keep.wait()
    mid[other_yhi] = own[other_yhi] + landed[other_yhi]
    mid[yhi] = own[yhi] + landed[yhi]
    cross = pltpu.make_async_remote_copy(
        src_ref=mid.at[other_yhi],
        dst_ref=last,
        send_sem=send_sem.at[nyhi],
        recv_sem=recv_sem.at[nyhi],
        device_id=to_yhi,
    )
    cross.start()
    cross.wait_recv()
    out_ref[...] = mid[yhi] + last[...]
    for copy in copies:
        copy.wait_send()
    cross.wait_send()


def reduce_rep(partial, cid):
    nyhi, ncore = lax.axis_size("yhi"), lax.axis_size("core")
    pieces = partial.reshape(nyhi * ncore, -1, partial.shape[1])
    piece = pieces.shape[1:]
    return pl.pallas_call(
        reduce_kernel,
        out_shape=jax.ShapeDtypeStruct(piece, pieces.dtype),
        in_specs=[pl.BlockSpec(memory_space=pl.ANY)],
        out_specs=pl.BlockSpec(memory_space=pltpu.VMEM),
        scratch_shapes=[
            pltpu.VMEM((nyhi, *piece), pieces.dtype),
            pltpu.VMEM((nyhi, *piece), pieces.dtype),
            pltpu.VMEM((nyhi, *piece), pieces.dtype),
            pltpu.VMEM(piece, pieces.dtype),
            pltpu.SemaphoreType.DMA((nyhi + 1,)),
            pltpu.SemaphoreType.DMA((nyhi + 1,)),
            pltpu.SemaphoreType.DMA((nyhi,)),
        ],
        compiler_params=pltpu.CompilerParams(collective_id=cid, has_side_effects=True),
    )(pieces)


def staged_index(col, per_owner):
    nz = lax.axis_size("z")
    nxy = lax.axis_size("x") * lax.axis_size("ylo")
    half = per_owner // 2
    owner = col // per_owner
    sub = col % per_owner
    z = owner % nz
    xy = owner // nz
    in_first = sub < half
    first = (z * nxy + xy) * half + jnp.where(in_first, sub, 0)
    second = (xy * nz + z) * half + jnp.where(in_first, 0, sub - half)
    return in_first.astype(jnp.int32), first, second


def products_kernel(flag_ref, first_ref, second_ref, *refs):
    adj_ref, out_ref = refs[-2:]
    rows, kq = adj_ref.shape[0], adj_ref.shape[1]
    firsts, seconds = refs[: rows * kq], refs[rows * kq : 2 * rows * kq]
    base = pl.program_id(0) * rows
    for r in range(rows):
        acc = jnp.zeros(out_ref.shape[1:], jnp.float32)
        for k in range(kq):
            at = r * kq + k
            block = jnp.where(flag_ref[base + r, k] != 0, firsts[at][0], seconds[at][0])
            acc = acc + jnp.dot(adj_ref[r, k], block, preferred_element_type=jnp.float32)
        out_ref[r] = acc


def tile_products(panels, adj_tiles, index, per_piece):
    flag, first, second = index
    rows, kq = flag.shape
    width = panels[0].shape[2]
    tile = (1, BLOCK, width)

    def pick(table, r, k):
        return pl.BlockSpec(tile, lambda g, f, a, b: (table(f, a, b)[g * per_piece + r, k], 0, 0))

    specs = [pick(lambda f, a, b: a, r, k) for r in range(per_piece) for k in range(kq)]
    specs += [pick(lambda f, a, b: b, r, k) for r in range(per_piece) for k in range(kq)]
    specs.append(pl.BlockSpec((per_piece, kq, BLOCK, BLOCK), lambda g, f, a, b: (g, 0, 0, 0)))
    out_spec = pl.BlockSpec((per_piece, BLOCK, width), lambda g, f, a, b: (g, 0, 0))
    summed = pl.pallas_call(
        products_kernel,
        out_shape=jax.ShapeDtypeStruct((rows, BLOCK, width), jnp.float32),
        grid_spec=pltpu.PrefetchScalarGridSpec(
            num_scalar_prefetch=3,
            grid=(rows // per_piece,),
            in_specs=specs,
            out_specs=out_spec,
        ),
    )(flag, first, second, *([panels[0]] * (per_piece * kq)), *([panels[1]] * (per_piece * kq)), adj_tiles[:, 0])
    return summed.reshape(-1, width)


def local(node_feats, adj_tiles, col_index, w_in, b_in, w_out, b_out, cot_out):
    per_piece = node_feats.shape[0] // BLOCK
    index = staged_index(col_index[:, 0, :], per_piece)
    panels = gather_blk(node_feats, 0)
    partial_sum = tile_products(panels, adj_tiles, index, 2 * per_piece)
    agg = reduce_rep(partial_sum, 8)
    agg_b = agg.astype(jnp.bfloat16)
    pre = jnp.dot(agg_b, w_in, preferred_element_type=jnp.float32) + b_in
    hidden = jax.nn.silu(pre).astype(jnp.bfloat16)
    projected = jnp.dot(hidden, w_out, preferred_element_type=jnp.float32) + b_out
    out_feats = (node_feats.astype(jnp.float32) + projected).astype(jnp.bfloat16)
    g_hidden = jnp.einsum("nh,fh->nf", cot_out, w_out, preferred_element_type=jnp.float32)
    sigma = jax.nn.sigmoid(pre)
    g_pre = (g_hidden * sigma * (1.0 + pre * (1.0 - sigma))).astype(jnp.bfloat16)
    g_agg = jnp.einsum("nf,hf->nh", g_pre, w_in, preferred_element_type=jnp.float32).astype(
        jnp.bfloat16
    )
    g_panels = gather_blk(g_agg, 1)
    back_partial = tile_products(g_panels, adj_tiles, index, 2 * per_piece)
    back_rows = reduce_rep(back_partial, 9)
    grad_feats = (cot_out.astype(jnp.float32) + back_rows).astype(jnp.bfloat16)
    return (out_feats, grad_feats)


def solution(mesh):
    nblk = mesh.shape["blk"]
    nrep = mesh.shape["rep"]
    fine = Mesh(mesh.devices.reshape(nblk // 16, 2, 8, nrep // 2, 2), NAMES)
    rows = P(BLK + REP, None)
    placed = (
        rows,
        P(BLK, REP, None, None, None),
        P(BLK, REP, None),
        P(),
        P(),
        P(),
        P(),
        rows,
    )
    return jax.shard_map(
        local,
        mesh=fine,
        in_specs=placed,
        out_specs=(rows, rows),
        check_vma=False,
    )
```

```python
import functools

import jax
import jax.numpy as jnp
from jax import lax
from jax.experimental import pallas as pl
from jax.experimental.pallas import tpu as pltpu
from jax.sharding import Mesh
from jax.sharding import PartitionSpec as P

BLOCK = 128
NAMES = ("x", "ylo", "z", "yhi", "core")
BLK = ("x", "ylo", "z")
REP = ("yhi", "core")


def group_place(axes):
    sizes = [lax.axis_size(a) for a in axes]
    me = 0
    for a, n in zip(axes, sizes):
        me = me * n + lax.axis_index(a)
    return me, sizes


def peer_id(axes, sizes, p):
    coords = {}
    for a, n in reversed(list(zip(axes, sizes))):
        coords[a] = p % n
        p = p // n
    return coords


def neighbours():
    nx, ny, nz = lax.axis_size("x"), lax.axis_size("ylo"), lax.axis_size("z")
    x, y, z = lax.axis_index("x"), lax.axis_index("ylo"), lax.axis_index("z")
    right, left, other = lax.rem(x + 1, nx), lax.rem(x + nx - 1, nx), ny - 1 - y
    return {"x": right}, {"x": left}, {"ylo": other}, {"z": lax.rem(z + 1, nz)}, {"z": lax.rem(z + nz - 1, nz)}


def gather_phase(phase, ring_src, tree_src, ring_out, tree_out, send_sem, recv_sem, local_sem, ready):
    nx, ny, nz = lax.axis_size("x"), lax.axis_size("ylo"), lax.axis_size("z")
    x, y, z = lax.axis_index("x"), lax.axis_index("ylo"), lax.axis_index("z")
    right, left, other = lax.rem(x + 1, nx), lax.rem(x + nx - 1, nx), ny - 1 - y
    to_right, to_left, to_other, up, down = neighbours()

    def send(kind, src, dst, peer):
        copy = pltpu.make_async_remote_copy(
            src_ref=src,
            dst_ref=dst,
            send_sem=send_sem.at[phase, kind],
            recv_sem=recv_sem.at[phase, kind],
            device_id=peer,
        )
        copy.start()
        return copy

    me = x * ny + y
    own_ring = pltpu.make_async_copy(ring_src, ring_out.at[z], local_sem.at[phase, 1])
    own_ring.start()
    steps = nz // 2
    half = ring_src.shape[0] // 2
    chunks = (pl.ds(0, half), pl.ds(half, half))
    ups = [[send(9 + c, ring_src.at[part], ring_out.at[z, part], up)] for c, part in enumerate(chunks)]
    downs = [
        [send(9 + 4 * steps + c, ring_src.at[part], ring_out.at[z, part], down)]
        for c, part in enumerate(chunks)
    ]

    ready()
    own_tree = pltpu.make_async_copy(tree_src, tree_out.at[me], local_sem.at[phase, 0])
    own_tree.start()
    first_right = send(0, tree_src, tree_out.at[me], to_right)
    first_left = send(1, tree_src, tree_out.at[me], to_left)
    first_other = send(2, tree_src, tree_out.at[me], to_other)

    def ring_step(s):
        below = lax.rem(z + nz - (s - 1), nz)
        above = lax.rem(z + s - 1, nz)
        for c, part in enumerate(chunks):
            ups[c][-1].wait_recv()
            if s < steps or c == 0:
                ups[c].append(send(9 + 2 * (s - 1) + c, ring_out.at[below, part], ring_out.at[below, part], up))
            downs[c][-1].wait_recv()
            if s < steps or c == 1:
                downs[c].append(
                    send(9 + 4 * steps + 2 * (s - 1) + c, ring_out.at[above, part], ring_out.at[above, part], down)
                )

    tree_split = tree_src.shape[0] // 2
    first_right.wait_recv()
    from_left = left * ny + y
    second_right = send(3, tree_out.at[from_left, :tree_split], tree_out.at[from_left, :tree_split], to_right)
    first_left.wait_recv()
    from_right = right * ny + y
    second_left = send(7, tree_out.at[from_right, tree_split:], tree_out.at[from_right, tree_split:], to_left)
    ring_step(2)
    first_other.wait_recv()
    from_other = x * ny + other
    other_right = send(4, tree_out.at[from_other], tree_out.at[from_other], to_right)
    other_left = send(5, tree_out.at[from_other], tree_out.at[from_other], to_left)
    ring_step(3)
    other_right.wait_recv()
    from_left_other = left * ny + other
    third_right = send(
        6, tree_out.at[from_left_other, :tree_split], tree_out.at[from_left_other, :tree_split], to_right
    )
    other_left.wait_recv()
    from_right_other = right * ny + other
    third_left = send(
        8, tree_out.at[from_right_other, tree_split:], tree_out.at[from_right_other, tree_split:], to_left
    )
    for s in range(4, steps + 1):
        ring_step(s)
    for copy in (second_right, second_left, third_right, third_left, ups[0][-1], downs[1][-1]):
        copy.wait_recv()
    tree = [first_right, first_left, first_other, second_right, second_left]
    tree += [other_right, other_left, third_right, third_left]
    return tree + ups[0] + ups[1] + downs[0] + downs[1], [own_tree, own_ring]


def phase_one(ring_src, tree_src, ring_out, tree_out, send_sem, recv_sem, local_sem):
    nx, ny, nz = lax.axis_size("x"), lax.axis_size("ylo"), lax.axis_size("z")
    x, y, z = lax.axis_index("x"), lax.axis_index("ylo"), lax.axis_index("z")

    def send(kind, src, dst, peer):
        copy = pltpu.make_async_remote_copy(
            src_ref=src, dst_ref=dst, send_sem=send_sem.at[0, kind], recv_sem=recv_sem.at[0, kind], device_id=peer
        )
        copy.start()
        return copy

    def on_z(step):
        return {"z": lax.rem(z + nz + step, nz)}

    me = x * ny + y
    own_tree = pltpu.make_async_copy(tree_src, tree_out.at[me], local_sem.at[0, 0])
    own_tree.start()
    own_ring = pltpu.make_async_copy(ring_src, ring_out.at[z], local_sem.at[0, 1])
    own_ring.start()
    n = nx * ny
    sends = []
    for d in range(1, n):
        p = lax.rem(me + d, n)
        sends.append(send(d - 1, tree_src, tree_out.at[me], {"x": p // ny, "ylo": p % ny}))
    kind = n - 1
    up_one = send(kind, ring_src, ring_out.at[z], on_z(1))
    down_one = send(kind + 1, ring_src, ring_out.at[z], on_z(-1))
    up_two = send(kind + 2, ring_src, ring_out.at[z], on_z(2))
    down_two = send(kind + 3, ring_src, ring_out.at[z], on_z(-2))
    split = ring_src.shape[0] // 2
    up_two.wait_recv()
    below = lax.rem(z + nz - 2, nz)
    fwd_up_one = send(kind + 4, ring_out.at[below], ring_out.at[below], on_z(1))
    fwd_up_two = send(kind + 5, ring_out.at[below, :split], ring_out.at[below, :split], on_z(2))
    down_two.wait_recv()
    above = lax.rem(z + 2, nz)
    fwd_down_one = send(kind + 6, ring_out.at[above], ring_out.at[above], on_z(-1))
    fwd_down_two = send(kind + 7, ring_out.at[above, split:], ring_out.at[above, split:], on_z(-2))
    ring = [up_one, down_one, up_two, down_two, fwd_up_one, fwd_up_two, fwd_down_one, fwd_down_two]
    for copy in sends:
        copy.wait_recv()
    own_tree.wait()

    def ring_landed():
        for copy in (up_one, down_one, fwd_up_one, fwd_up_two, fwd_down_one, fwd_down_two):
            copy.wait_recv()
        own_ring.wait()

    return sends + ring, ring_landed


def gather_kernel(rows_ref, mid_ring, mid_tree, ring_out, tree_out, send_sem, recv_sem, local_sem):
    nx, ny, nz = lax.axis_size("x"), lax.axis_size("ylo"), lax.axis_size("z")
    x, y, z = lax.axis_index("x"), lax.axis_index("ylo"), lax.axis_index("z")
    me = x * ny + y
    peers = [{"x": lax.rem(me + d, nx * ny) // ny, "ylo": lax.rem(me + d, nx * ny) % ny} for d in range(1, nx * ny)]
    peers += [{"z": lax.rem(z + nz + step, nz)} for step in (1, -1, 2, -2)]
    barrier = pltpu.get_barrier_semaphore()
    for peer in peers:
        pl.semaphore_signal(barrier, 1, device_id=peer)
    pl.semaphore_wait(barrier, len(peers))
    half = rows_ref.shape[0] // 2
    ring_src, tree_src = rows_ref.at[pl.ds(half, half)], rows_ref.at[pl.ds(0, half)]
    sends, ring_landed = phase_one(ring_src, tree_src, mid_ring, mid_tree, send_sem, recv_sem, local_sem)
    more, local = gather_phase(
        1, mid_tree, mid_ring, ring_out, tree_out, send_sem, recv_sem, local_sem, ring_landed
    )
    for copy in sends + more:
        copy.wait_send()
    for copy in local:
        copy.wait()


def gather_blk(rows, cid):
    nz = lax.axis_size("z")
    nxy = lax.axis_size("x") * lax.axis_size("ylo")
    half = rows.shape[0] // 2
    width = rows.shape[1]
    piece = (half, width)
    any_space = pl.BlockSpec(memory_space=pl.ANY)
    _, _, first, second = pl.pallas_call(
        gather_kernel,
        out_shape=(
            jax.ShapeDtypeStruct((nz, *piece), rows.dtype),
            jax.ShapeDtypeStruct((nxy, *piece), rows.dtype),
            jax.ShapeDtypeStruct((nz, nxy, *piece), rows.dtype),
            jax.ShapeDtypeStruct((nxy, nz, *piece), rows.dtype),
        ),
        in_specs=[any_space],
        out_specs=(any_space,) * 4,
        scratch_shapes=[
            pltpu.SemaphoreType.DMA((2, 9 + 4 * nz)),
            pltpu.SemaphoreType.DMA((2, 9 + 4 * nz)),
            pltpu.SemaphoreType.DMA((2, 2)),
        ],
        compiler_params=pltpu.CompilerParams(collective_id=cid, has_side_effects=True),
    )(rows)
    return first.reshape(-1, BLOCK, width), second.reshape(-1, BLOCK, width)


def reduce_kernel(src_ref, out_ref, own, landed, mid, last, send_sem, recv_sem, local_sem):
    nyhi, ncore = lax.axis_size("yhi"), lax.axis_size("core")
    yhi, core = lax.axis_index("yhi"), lax.axis_index("core")
    other_core, other_yhi = ncore - 1 - core, nyhi - 1 - yhi
    to_core, to_yhi = {"core": other_core}, {"yhi": other_yhi}
    barrier = pltpu.get_barrier_semaphore()
    for peer in (to_core, to_yhi):
        pl.semaphore_signal(barrier, 1, device_id=peer)
    pl.semaphore_wait(barrier, 2)
    copies, locals_ = [], []
    for h in range(nyhi):
        copy = pltpu.make_async_remote_copy(
            src_ref=src_ref.at[h * ncore + other_core],
            dst_ref=landed.at[h],
            send_sem=send_sem.at[h],
            recv_sem=recv_sem.at[h],
            device_id=to_core,
        )
        copy.start()
        copies.append(copy)
        keep = pltpu.make_async_copy(src_ref.at[h * ncore + core], own.at[h], local_sem.at[h])
        keep.start()
        locals_.append(keep)
    for copy in copies:
        copy.wait_recv()
    for keep in locals_:
        keep.wait()
    mid[other_yhi] = own[other_yhi] + landed[other_yhi]
    mid[yhi] = own[yhi] + landed[yhi]
    cross = pltpu.make_async_remote_copy(
        src_ref=mid.at[other_yhi],
        dst_ref=last,
        send_sem=send_sem.at[nyhi],
        recv_sem=recv_sem.at[nyhi],
        device_id=to_yhi,
    )
    cross.start()
    cross.wait_recv()
    out_ref[...] = mid[yhi] + last[...]
    for copy in copies:
        copy.wait_send()
    cross.wait_send()


def reduce_rep(partial, cid):
    nyhi, ncore = lax.axis_size("yhi"), lax.axis_size("core")
    pieces = partial.reshape(nyhi * ncore, -1, partial.shape[1])
    piece = pieces.shape[1:]
    return pl.pallas_call(
        reduce_kernel,
        out_shape=jax.ShapeDtypeStruct(piece, pieces.dtype),
        in_specs=[pl.BlockSpec(memory_space=pl.ANY)],
        out_specs=pl.BlockSpec(memory_space=pltpu.VMEM),
        scratch_shapes=[
            pltpu.VMEM((nyhi, *piece), pieces.dtype),
            pltpu.VMEM((nyhi, *piece), pieces.dtype),
            pltpu.VMEM((nyhi, *piece), pieces.dtype),
            pltpu.VMEM(piece, pieces.dtype),
            pltpu.SemaphoreType.DMA((nyhi + 1,)),
            pltpu.SemaphoreType.DMA((nyhi + 1,)),
            pltpu.SemaphoreType.DMA((nyhi,)),
        ],
        compiler_params=pltpu.CompilerParams(collective_id=cid, has_side_effects=True),
    )(pieces)


def staged_index(col, per_owner):
    nz = lax.axis_size("z")
    nxy = lax.axis_size("x") * lax.axis_size("ylo")
    half = per_owner // 2
    owner = col // per_owner
    sub = col % per_owner
    z = owner % nz
    xy = owner // nz
    in_first = sub < half
    first = (z * nxy + xy) * half + jnp.where(in_first, sub, 0)
    second = (xy * nz + z) * half + jnp.where(in_first, 0, sub - half)
    return in_first.astype(jnp.int32), first, second


def products_kernel(flag_ref, first_ref, second_ref, *refs):
    adj_ref, out_ref = refs[-2:]
    rows, kq = adj_ref.shape[0], adj_ref.shape[1]
    firsts, seconds = refs[: rows * kq], refs[rows * kq : 2 * rows * kq]
    base = pl.program_id(0) * rows
    for r in range(rows):
        acc = jnp.zeros(out_ref.shape[1:], jnp.float32)
        for k in range(kq):
            at = r * kq + k
            block = jnp.where(flag_ref[base + r, k] != 0, firsts[at][0], seconds[at][0])
            acc = acc + jnp.dot(adj_ref[r, k], block, preferred_element_type=jnp.float32)
        out_ref[r] = acc


def tile_products(panels, adj_tiles, index, per_piece):
    flag, first, second = index
    rows, kq = flag.shape
    width = panels[0].shape[2]
    tile = (1, BLOCK, width)

    def pick(table, r, k):
        return pl.BlockSpec(tile, lambda g, f, a, b: (table(f, a, b)[g * per_piece + r, k], 0, 0))

    specs = [pick(lambda f, a, b: a, r, k) for r in range(per_piece) for k in range(kq)]
    specs += [pick(lambda f, a, b: b, r, k) for r in range(per_piece) for k in range(kq)]
    specs.append(pl.BlockSpec((per_piece, kq, BLOCK, BLOCK), lambda g, f, a, b: (g, 0, 0, 0)))
    out_spec = pl.BlockSpec((per_piece, BLOCK, width), lambda g, f, a, b: (g, 0, 0))
    summed = pl.pallas_call(
        products_kernel,
        out_shape=jax.ShapeDtypeStruct((rows, BLOCK, width), jnp.float32),
        grid_spec=pltpu.PrefetchScalarGridSpec(
            num_scalar_prefetch=3,
            grid=(rows // per_piece,),
            in_specs=specs,
            out_specs=out_spec,
        ),
    )(flag, first, second, *([panels[0]] * (per_piece * kq)), *([panels[1]] * (per_piece * kq)), adj_tiles[:, 0])
    return summed.reshape(-1, width)


def local(node_feats, adj_tiles, col_index, w_in, b_in, w_out, b_out, cot_out):
    per_piece = node_feats.shape[0] // BLOCK
    index = staged_index(col_index[:, 0, :], per_piece)
    panels = gather_blk(node_feats, 0)
    partial_sum = tile_products(panels, adj_tiles, index, 2 * per_piece)
    agg = reduce_rep(partial_sum, 8)
    agg_b = agg.astype(jnp.bfloat16)
    pre = jnp.dot(agg_b, w_in, preferred_element_type=jnp.float32) + b_in
    hidden = jax.nn.silu(pre).astype(jnp.bfloat16)
    projected = jnp.dot(hidden, w_out, preferred_element_type=jnp.float32) + b_out
    out_feats = (node_feats.astype(jnp.float32) + projected).astype(jnp.bfloat16)
    g_hidden = jnp.einsum("nh,fh->nf", cot_out, w_out, preferred_element_type=jnp.float32)
    sigma = jax.nn.sigmoid(pre)
    g_pre = (g_hidden * sigma * (1.0 + pre * (1.0 - sigma))).astype(jnp.bfloat16)
    g_agg = jnp.einsum("nf,hf->nh", g_pre, w_in, preferred_element_type=jnp.float32).astype(
        jnp.bfloat16
    )
    g_panels = gather_blk(g_agg, 1)
    back_partial = tile_products(g_panels, adj_tiles, index, 2 * per_piece)
    back_rows = reduce_rep(back_partial, 9)
    grad_feats = (cot_out.astype(jnp.float32) + back_rows).astype(jnp.bfloat16)
    return (out_feats, grad_feats)


def solution(mesh):
    nblk = mesh.shape["blk"]
    nrep = mesh.shape["rep"]
    fine = Mesh(mesh.devices.reshape(nblk // 16, 2, 8, nrep // 2, 2), NAMES)
    rows = P(BLK + REP, None)
    placed = (
        rows,
        P(BLK, REP, None, None, None),
        P(BLK, REP, None),
        P(),
        P(),
        P(),
        P(),
        rows,
    )
    return jax.shard_map(
        local,
        mesh=fine,
        in_specs=placed,
        out_specs=(rows, rows),
        check_vma=False,
    )
```

```python
import functools

import jax
import jax.numpy as jnp
from jax import lax
from jax.experimental import pallas as pl
from jax.experimental.pallas import tpu as pltpu
from jax.sharding import Mesh
from jax.sharding import PartitionSpec as P

BLOCK = 128
NAMES = ("x", "ylo", "z", "yhi", "core")
BLK = ("x", "ylo", "z")
REP = ("yhi", "core")


def group_place(axes):
    sizes = [lax.axis_size(a) for a in axes]
    me = 0
    for a, n in zip(axes, sizes):
        me = me * n + lax.axis_index(a)
    return me, sizes


def peer_id(axes, sizes, p):
    coords = {}
    for a, n in reversed(list(zip(axes, sizes))):
        coords[a] = p % n
        p = p // n
    return coords


def neighbours():
    nx, ny, nz = lax.axis_size("x"), lax.axis_size("ylo"), lax.axis_size("z")
    x, y, z = lax.axis_index("x"), lax.axis_index("ylo"), lax.axis_index("z")
    right, left, other = lax.rem(x + 1, nx), lax.rem(x + nx - 1, nx), ny - 1 - y
    return {"x": right}, {"x": left}, {"ylo": other}, {"z": lax.rem(z + 1, nz)}, {"z": lax.rem(z + nz - 1, nz)}


def gather_phase(phase, ring_src, tree_src, ring_out, tree_out, send_sem, recv_sem, local_sem, ready):
    nx, ny, nz = lax.axis_size("x"), lax.axis_size("ylo"), lax.axis_size("z")
    x, y, z = lax.axis_index("x"), lax.axis_index("ylo"), lax.axis_index("z")
    right, left, other = lax.rem(x + 1, nx), lax.rem(x + nx - 1, nx), ny - 1 - y
    to_right, to_left, to_other, up, down = neighbours()

    def send(kind, src, dst, peer):
        copy = pltpu.make_async_remote_copy(
            src_ref=src,
            dst_ref=dst,
            send_sem=send_sem.at[phase, kind],
            recv_sem=recv_sem.at[phase, kind],
            device_id=peer,
        )
        copy.start()
        return copy

    me = x * ny + y
    own_ring = pltpu.make_async_copy(ring_src, ring_out.at[z], local_sem.at[phase, 1])
    own_ring.start()
    steps = nz // 2
    half = ring_src.shape[0] // 2
    chunks = (pl.ds(0, half), pl.ds(half, half))
    ups = [[send(9 + c, ring_src.at[part], ring_out.at[z, part], up)] for c, part in enumerate(chunks)]
    downs = [
        [send(9 + 4 * steps + c, ring_src.at[part], ring_out.at[z, part], down)]
        for c, part in enumerate(chunks)
    ]

    ready()
    own_tree = pltpu.make_async_copy(tree_src, tree_out.at[me], local_sem.at[phase, 0])
    own_tree.start()
    first_right = send(0, tree_src, tree_out.at[me], to_right)
    first_left = send(1, tree_src, tree_out.at[me], to_left)
    first_other = send(2, tree_src, tree_out.at[me], to_other)

    def ring_step(s):
        below = lax.rem(z + nz - (s - 1), nz)
        above = lax.rem(z + s - 1, nz)
        for c, part in enumerate(chunks):
            ups[c][-1].wait_recv()
            if s < steps or c == 0:
                ups[c].append(send(9 + 2 * (s - 1) + c, ring_out.at[below, part], ring_out.at[below, part], up))
            downs[c][-1].wait_recv()
            if s < steps or c == 1:
                downs[c].append(
                    send(9 + 4 * steps + 2 * (s - 1) + c, ring_out.at[above, part], ring_out.at[above, part], down)
                )

    tree_split = tree_src.shape[0] // 2
    first_right.wait_recv()
    from_left = left * ny + y
    second_right = send(3, tree_out.at[from_left, :tree_split], tree_out.at[from_left, :tree_split], to_right)
    first_left.wait_recv()
    from_right = right * ny + y
    second_left = send(7, tree_out.at[from_right, tree_split:], tree_out.at[from_right, tree_split:], to_left)
    ring_step(2)
    first_other.wait_recv()
    from_other = x * ny + other
    other_right = send(4, tree_out.at[from_other], tree_out.at[from_other], to_right)
    other_left = send(5, tree_out.at[from_other], tree_out.at[from_other], to_left)
    ring_step(3)
    other_right.wait_recv()
    from_left_other = left * ny + other
    third_right = send(
        6, tree_out.at[from_left_other, :tree_split], tree_out.at[from_left_other, :tree_split], to_right
    )
    other_left.wait_recv()
    from_right_other = right * ny + other
    third_left = send(
        8, tree_out.at[from_right_other, tree_split:], tree_out.at[from_right_other, tree_split:], to_left
    )
    for s in range(4, steps + 1):
        ring_step(s)
    for copy in (second_right, second_left, third_right, third_left, ups[0][-1], downs[1][-1]):
        copy.wait_recv()
    tree = [first_right, first_left, first_other, second_right, second_left]
    tree += [other_right, other_left, third_right, third_left]
    return tree + ups[0] + ups[1] + downs[0] + downs[1], [own_tree, own_ring]


def phase_one(ring_src, tree_src, ring_out, tree_out, send_sem, recv_sem, local_sem):
    nx, ny, nz = lax.axis_size("x"), lax.axis_size("ylo"), lax.axis_size("z")
    x, y, z = lax.axis_index("x"), lax.axis_index("ylo"), lax.axis_index("z")

    def send(kind, src, dst, peer):
        copy = pltpu.make_async_remote_copy(
            src_ref=src, dst_ref=dst, send_sem=send_sem.at[0, kind], recv_sem=recv_sem.at[0, kind], device_id=peer
        )
        copy.start()
        return copy

    def on_z(step):
        return {"z": lax.rem(z + nz + step, nz)}

    me = x * ny + y
    own_tree = pltpu.make_async_copy(tree_src, tree_out.at[me], local_sem.at[0, 0])
    own_tree.start()
    own_ring = pltpu.make_async_copy(ring_src, ring_out.at[z], local_sem.at[0, 1])
    own_ring.start()
    n = nx * ny
    sends = []
    for d in range(1, n):
        p = lax.rem(me + d, n)
        sends.append(send(d - 1, tree_src, tree_out.at[me], {"x": p // ny, "ylo": p % ny}))
    kind = n - 1
    up_one = send(kind, ring_src, ring_out.at[z], on_z(1))
    down_one = send(kind + 1, ring_src, ring_out.at[z], on_z(-1))
    up_two = send(kind + 2, ring_src, ring_out.at[z], on_z(2))
    down_two = send(kind + 3, ring_src, ring_out.at[z], on_z(-2))
    split = ring_src.shape[0] // 2
    up_two.wait_recv()
    below = lax.rem(z + nz - 2, nz)
    fwd_up_one = send(kind + 4, ring_out.at[below], ring_out.at[below], on_z(1))
    fwd_up_two = send(kind + 5, ring_out.at[below, :split], ring_out.at[below, :split], on_z(2))
    down_two.wait_recv()
    above = lax.rem(z + 2, nz)
    fwd_down_one = send(kind + 6, ring_out.at[above], ring_out.at[above], on_z(-1))
    fwd_down_two = send(kind + 7, ring_out.at[above, split:], ring_out.at[above, split:], on_z(-2))
    ring = [up_one, down_one, up_two, down_two, fwd_up_one, fwd_up_two, fwd_down_one, fwd_down_two]
    for copy in sends:
        copy.wait_recv()
    own_tree.wait()

    def ring_landed():
        for copy in (up_one, down_one, fwd_up_one, fwd_up_two, fwd_down_one, fwd_down_two):
            copy.wait_recv()
        own_ring.wait()

    return sends + ring, ring_landed


def gather_kernel(rows_ref, mid_ring, mid_tree, ring_out, tree_out, send_sem, recv_sem, local_sem):
    nx, ny, nz = lax.axis_size("x"), lax.axis_size("ylo"), lax.axis_size("z")
    x, y, z = lax.axis_index("x"), lax.axis_index("ylo"), lax.axis_index("z")
    me = x * ny + y
    peers = [{"x": lax.rem(me + d, nx * ny) // ny, "ylo": lax.rem(me + d, nx * ny) % ny} for d in range(1, nx * ny)]
    peers += [{"z": lax.rem(z + nz + step, nz)} for step in (1, -1, 2, -2)]
    barrier = pltpu.get_barrier_semaphore()
    for peer in peers:
        pl.semaphore_signal(barrier, 1, device_id=peer)
    pl.semaphore_wait(barrier, len(peers))
    half = rows_ref.shape[0] // 2
    ring_src, tree_src = rows_ref.at[pl.ds(half, half)], rows_ref.at[pl.ds(0, half)]
    sends, ring_landed = phase_one(ring_src, tree_src, mid_ring, mid_tree, send_sem, recv_sem, local_sem)
    more, local = gather_phase(
        1, mid_tree, mid_ring, ring_out, tree_out, send_sem, recv_sem, local_sem, ring_landed
    )
    for copy in sends + more:
        copy.wait_send()
    for copy in local:
        copy.wait()


def gather_blk(rows, cid):
    nz = lax.axis_size("z")
    nxy = lax.axis_size("x") * lax.axis_size("ylo")
    half = rows.shape[0] // 2
    width = rows.shape[1]
    piece = (half, width)
    any_space = pl.BlockSpec(memory_space=pl.ANY)
    _, _, first, second = pl.pallas_call(
        gather_kernel,
        out_shape=(
            jax.ShapeDtypeStruct((nz, *piece), rows.dtype),
            jax.ShapeDtypeStruct((nxy, *piece), rows.dtype),
            jax.ShapeDtypeStruct((nz, nxy, *piece), rows.dtype),
            jax.ShapeDtypeStruct((nxy, nz, *piece), rows.dtype),
        ),
        in_specs=[any_space],
        out_specs=(any_space,) * 4,
        scratch_shapes=[
            pltpu.SemaphoreType.DMA((2, 9 + 4 * nz)),
            pltpu.SemaphoreType.DMA((2, 9 + 4 * nz)),
            pltpu.SemaphoreType.DMA((2, 2)),
        ],
        compiler_params=pltpu.CompilerParams(collective_id=cid, has_side_effects=True),
    )(rows)
    return first.reshape(-1, BLOCK, width), second.reshape(-1, BLOCK, width)


def reduce_kernel(src_ref, out_ref, own, landed, mid, last, send_sem, recv_sem, local_sem):
    nyhi, ncore = lax.axis_size("yhi"), lax.axis_size("core")
    yhi, core = lax.axis_index("yhi"), lax.axis_index("core")
    other_core, other_yhi = ncore - 1 - core, nyhi - 1 - yhi
    to_core, to_yhi = {"core": other_core}, {"yhi": other_yhi}
    barrier = pltpu.get_barrier_semaphore()
    for peer in (to_core, to_yhi):
        pl.semaphore_signal(barrier, 1, device_id=peer)
    pl.semaphore_wait(barrier, 2)
    rows = last.shape[0] // 2
    parts = (pl.ds(0, rows), pl.ds(rows, rows))
    copies, locals_ = [], []
    for k, part in enumerate(parts):
        for h in range(nyhi):
            copy = pltpu.make_async_remote_copy(
                src_ref=src_ref.at[h * ncore + other_core, part],
                dst_ref=landed.at[h, part],
                send_sem=send_sem.at[k, h],
                recv_sem=recv_sem.at[k, h],
                device_id=to_core,
            )
            copy.start()
            copies.append(copy)
            keep = pltpu.make_async_copy(src_ref.at[h * ncore + core, part], own.at[h, part], local_sem.at[k, h])
            keep.start()
            locals_.append(keep)
    crosses = []
    for k, part in enumerate(parts):
        for h in range(nyhi):
            copies[k * nyhi + h].wait_recv()
            locals_[k * nyhi + h].wait()
        mid[other_yhi, part] = own[other_yhi, part] + landed[other_yhi, part]
        mid[yhi, part] = own[yhi, part] + landed[yhi, part]
        cross = pltpu.make_async_remote_copy(
            src_ref=mid.at[other_yhi, part],
            dst_ref=last.at[part],
            send_sem=send_sem.at[k, nyhi],
            recv_sem=recv_sem.at[k, nyhi],
            device_id=to_yhi,
        )
        cross.start()
        crosses.append(cross)
    for k, part in enumerate(parts):
        crosses[k].wait_recv()
        out_ref[part] = mid[yhi, part] + last[part]
    for copy in copies + crosses:
        copy.wait_send()


def reduce_rep(partial, cid):
    nyhi, ncore = lax.axis_size("yhi"), lax.axis_size("core")
    pieces = partial.reshape(nyhi * ncore, -1, partial.shape[1])
    piece = pieces.shape[1:]
    return pl.pallas_call(
        reduce_kernel,
        out_shape=jax.ShapeDtypeStruct(piece, pieces.dtype),
        in_specs=[pl.BlockSpec(memory_space=pl.ANY)],
        out_specs=pl.BlockSpec(memory_space=pltpu.VMEM),
        scratch_shapes=[
            pltpu.VMEM((nyhi, *piece), pieces.dtype),
            pltpu.VMEM((nyhi, *piece), pieces.dtype),
            pltpu.VMEM((nyhi, *piece), pieces.dtype),
            pltpu.VMEM(piece, pieces.dtype),
            pltpu.SemaphoreType.DMA((2, nyhi + 1)),
            pltpu.SemaphoreType.DMA((2, nyhi + 1)),
            pltpu.SemaphoreType.DMA((2, nyhi)),
        ],
        compiler_params=pltpu.CompilerParams(collective_id=cid, has_side_effects=True),
    )(pieces)


def staged_index(col, per_owner):
    nz = lax.axis_size("z")
    nxy = lax.axis_size("x") * lax.axis_size("ylo")
    half = per_owner // 2
    owner = col // per_owner
    sub = col % per_owner
    z = owner % nz
    xy = owner // nz
    in_first = sub < half
    first = (z * nxy + xy) * half + jnp.where(in_first, sub, 0)
    second = (xy * nz + z) * half + jnp.where(in_first, 0, sub - half)
    return in_first.astype(jnp.int32), first, second


def products_kernel(flag_ref, first_ref, second_ref, *refs):
    adj_ref, out_ref = refs[-2:]
    rows, kq = adj_ref.shape[0], adj_ref.shape[1]
    firsts, seconds = refs[: rows * kq], refs[rows * kq : 2 * rows * kq]
    base = pl.program_id(0) * rows
    for r in range(rows):
        acc = jnp.zeros(out_ref.shape[1:], jnp.float32)
        for k in range(kq):
            at = r * kq + k
            block = jnp.where(flag_ref[base + r, k] != 0, firsts[at][0], seconds[at][0])
            acc = acc + jnp.dot(adj_ref[r, k], block, preferred_element_type=jnp.float32)
        out_ref[r] = acc


def tile_products(panels, adj_tiles, index, per_piece):
    flag, first, second = index
    rows, kq = flag.shape
    width = panels[0].shape[2]
    tile = (1, BLOCK, width)

    def pick(table, r, k):
        return pl.BlockSpec(tile, lambda g, f, a, b: (table(f, a, b)[g * per_piece + r, k], 0, 0))

    specs = [pick(lambda f, a, b: a, r, k) for r in range(per_piece) for k in range(kq)]
    specs += [pick(lambda f, a, b: b, r, k) for r in range(per_piece) for k in range(kq)]
    specs.append(pl.BlockSpec((per_piece, kq, BLOCK, BLOCK), lambda g, f, a, b: (g, 0, 0, 0)))
    out_spec = pl.BlockSpec((per_piece, BLOCK, width), lambda g, f, a, b: (g, 0, 0))
    summed = pl.pallas_call(
        products_kernel,
        out_shape=jax.ShapeDtypeStruct((rows, BLOCK, width), jnp.float32),
        grid_spec=pltpu.PrefetchScalarGridSpec(
            num_scalar_prefetch=3,
            grid=(rows // per_piece,),
            in_specs=specs,
            out_specs=out_spec,
        ),
    )(flag, first, second, *([panels[0]] * (per_piece * kq)), *([panels[1]] * (per_piece * kq)), adj_tiles[:, 0])
    return summed.reshape(-1, width)


def local(node_feats, adj_tiles, col_index, w_in, b_in, w_out, b_out, cot_out):
    per_piece = node_feats.shape[0] // BLOCK
    index = staged_index(col_index[:, 0, :], per_piece)
    panels = gather_blk(node_feats, 0)
    partial_sum = tile_products(panels, adj_tiles, index, 2 * per_piece)
    agg = reduce_rep(partial_sum, 8)
    agg_b = agg.astype(jnp.bfloat16)
    pre = jnp.dot(agg_b, w_in, preferred_element_type=jnp.float32) + b_in
    hidden = jax.nn.silu(pre).astype(jnp.bfloat16)
    projected = jnp.dot(hidden, w_out, preferred_element_type=jnp.float32) + b_out
    out_feats = (node_feats.astype(jnp.float32) + projected).astype(jnp.bfloat16)
    g_hidden = jnp.einsum("nh,fh->nf", cot_out, w_out, preferred_element_type=jnp.float32)
    sigma = jax.nn.sigmoid(pre)
    g_pre = (g_hidden * sigma * (1.0 + pre * (1.0 - sigma))).astype(jnp.bfloat16)
    g_agg = jnp.einsum("nf,hf->nh", g_pre, w_in, preferred_element_type=jnp.float32).astype(
        jnp.bfloat16
    )
    g_panels = gather_blk(g_agg, 1)
    back_partial = tile_products(g_panels, adj_tiles, index, 2 * per_piece)
    back_rows = reduce_rep(back_partial, 9)
    grad_feats = (cot_out.astype(jnp.float32) + back_rows).astype(jnp.bfloat16)
    return (out_feats, grad_feats)


def solution(mesh):
    nblk = mesh.shape["blk"]
    nrep = mesh.shape["rep"]
    fine = Mesh(mesh.devices.reshape(nblk // 16, 2, 8, nrep // 2, 2), NAMES)
    rows = P(BLK + REP, None)
    placed = (
        rows,
        P(BLK, REP, None, None, None),
        P(BLK, REP, None),
        P(),
        P(),
        P(),
        P(),
        rows,
    )
    return jax.shard_map(
        local,
        mesh=fine,
        in_specs=placed,
        out_specs=(rows, rows),
        check_vma=False,
    )
```

```python
import functools

import jax
import jax.numpy as jnp
from jax import lax
from jax.experimental import pallas as pl
from jax.experimental.pallas import tpu as pltpu
from jax.sharding import Mesh
from jax.sharding import PartitionSpec as P

BLOCK = 128
NAMES = ("x", "ylo", "z", "yhi", "core")
BLK = ("x", "ylo", "z")
REP = ("yhi", "core")


def group_place(axes):
    sizes = [lax.axis_size(a) for a in axes]
    me = 0
    for a, n in zip(axes, sizes):
        me = me * n + lax.axis_index(a)
    return me, sizes


def peer_id(axes, sizes, p):
    coords = {}
    for a, n in reversed(list(zip(axes, sizes))):
        coords[a] = p % n
        p = p // n
    return coords


def neighbours():
    nx, ny, nz = lax.axis_size("x"), lax.axis_size("ylo"), lax.axis_size("z")
    x, y, z = lax.axis_index("x"), lax.axis_index("ylo"), lax.axis_index("z")
    right, left, other = lax.rem(x + 1, nx), lax.rem(x + nx - 1, nx), ny - 1 - y
    return {"x": right}, {"x": left}, {"ylo": other}, {"z": lax.rem(z + 1, nz)}, {"z": lax.rem(z + nz - 1, nz)}


def gather_phase(phase, ring_src, tree_src, ring_out, tree_out, send_sem, recv_sem, local_sem, ready):
    nx, ny, nz = lax.axis_size("x"), lax.axis_size("ylo"), lax.axis_size("z")
    x, y, z = lax.axis_index("x"), lax.axis_index("ylo"), lax.axis_index("z")
    right, left, other = lax.rem(x + 1, nx), lax.rem(x + nx - 1, nx), ny - 1 - y
    to_right, to_left, to_other, up, down = neighbours()

    def send(kind, src, dst, peer):
        copy = pltpu.make_async_remote_copy(
            src_ref=src,
            dst_ref=dst,
            send_sem=send_sem.at[phase, kind],
            recv_sem=recv_sem.at[phase, kind],
            device_id=peer,
        )
        copy.start()
        return copy

    me = x * ny + y
    own_ring = pltpu.make_async_copy(ring_src, ring_out.at[z], local_sem.at[phase, 1])
    own_ring.start()
    steps = nz // 2
    half = ring_src.shape[0] // 2
    chunks = (pl.ds(0, half), pl.ds(half, half))
    ups = [[send(9 + c, ring_src.at[part], ring_out.at[z, part], up)] for c, part in enumerate(chunks)]
    downs = [
        [send(9 + 4 * steps + c, ring_src.at[part], ring_out.at[z, part], down)]
        for c, part in enumerate(chunks)
    ]

    ready()
    own_tree = pltpu.make_async_copy(tree_src, tree_out.at[me], local_sem.at[phase, 0])
    own_tree.start()
    first_right = send(0, tree_src, tree_out.at[me], to_right)
    first_left = send(1, tree_src, tree_out.at[me], to_left)
    tree_split = tree_src.shape[0] // 2
    tree_parts = (pl.ds(0, tree_split), pl.ds(tree_split, tree_split))
    extra = 9 + 4 * nz
    first_other = [
        send(2 if c == 0 else extra, tree_src.at[part], tree_out.at[me, part], to_other)
        for c, part in enumerate(tree_parts)
    ]

    def ring_step(s):
        below = lax.rem(z + nz - (s - 1), nz)
        above = lax.rem(z + s - 1, nz)
        for c, part in enumerate(chunks):
            ups[c][-1].wait_recv()
            if s < steps or c == 0:
                ups[c].append(send(9 + 2 * (s - 1) + c, ring_out.at[below, part], ring_out.at[below, part], up))
            downs[c][-1].wait_recv()
            if s < steps or c == 1:
                downs[c].append(
                    send(9 + 4 * steps + 2 * (s - 1) + c, ring_out.at[above, part], ring_out.at[above, part], down)
                )

    first_right.wait_recv()
    from_left = left * ny + y
    second_right = send(3, tree_out.at[from_left, :tree_split], tree_out.at[from_left, :tree_split], to_right)
    first_left.wait_recv()
    from_right = right * ny + y
    second_left = send(7, tree_out.at[from_right, tree_split:], tree_out.at[from_right, tree_split:], to_left)
    ring_step(2)
    from_other = x * ny + other
    other_right, other_left = [], []
    for c, part in enumerate(tree_parts):
        first_other[c].wait_recv()
        src = tree_out.at[from_other, part]
        other_right.append(send(4 if c == 0 else extra + 1, src, src, to_right))
        other_left.append(send(5 if c == 0 else extra + 2, src, src, to_left))
    ring_step(3)
    other_right[0].wait_recv()
    from_left_other = left * ny + other
    third_right = send(
        6, tree_out.at[from_left_other, :tree_split], tree_out.at[from_left_other, :tree_split], to_right
    )
    other_left[1].wait_recv()
    from_right_other = right * ny + other
    third_left = send(
        8, tree_out.at[from_right_other, tree_split:], tree_out.at[from_right_other, tree_split:], to_left
    )
    for s in range(4, steps + 1):
        ring_step(s)
    for copy in (second_right, second_left, third_right, third_left, ups[0][-1], downs[1][-1]):
        copy.wait_recv()
    other_right[1].wait_recv()
    other_left[0].wait_recv()
    tree = [first_right, first_left, *first_other, second_right, second_left]
    tree += [*other_right, *other_left, third_right, third_left]
    return tree + ups[0] + ups[1] + downs[0] + downs[1], [own_tree, own_ring]


def phase_one(ring_src, tree_src, ring_out, tree_out, send_sem, recv_sem, local_sem):
    nx, ny, nz = lax.axis_size("x"), lax.axis_size("ylo"), lax.axis_size("z")
    x, y, z = lax.axis_index("x"), lax.axis_index("ylo"), lax.axis_index("z")

    def send(kind, src, dst, peer):
        copy = pltpu.make_async_remote_copy(
            src_ref=src, dst_ref=dst, send_sem=send_sem.at[0, kind], recv_sem=recv_sem.at[0, kind], device_id=peer
        )
        copy.start()
        return copy

    def on_z(step):
        return {"z": lax.rem(z + nz + step, nz)}

    me = x * ny + y
    own_tree = pltpu.make_async_copy(tree_src, tree_out.at[me], local_sem.at[0, 0])
    own_tree.start()
    own_ring = pltpu.make_async_copy(ring_src, ring_out.at[z], local_sem.at[0, 1])
    own_ring.start()
    n = nx * ny
    sends = []
    for d in range(1, n):
        p = lax.rem(me + d, n)
        sends.append(send(d - 1, tree_src, tree_out.at[me], {"x": p // ny, "ylo": p % ny}))
    kind = n - 1
    up_one = send(kind, ring_src, ring_out.at[z], on_z(1))
    down_one = send(kind + 1, ring_src, ring_out.at[z], on_z(-1))
    up_two = send(kind + 2, ring_src, ring_out.at[z], on_z(2))
    down_two = send(kind + 3, ring_src, ring_out.at[z], on_z(-2))
    split = ring_src.shape[0] // 2
    up_two.wait_recv()
    below = lax.rem(z + nz - 2, nz)
    fwd_up_one = send(kind + 4, ring_out.at[below], ring_out.at[below], on_z(1))
    fwd_up_two = send(kind + 5, ring_out.at[below, :split], ring_out.at[below, :split], on_z(2))
    down_two.wait_recv()
    above = lax.rem(z + 2, nz)
    fwd_down_one = send(kind + 6, ring_out.at[above], ring_out.at[above], on_z(-1))
    fwd_down_two = send(kind + 7, ring_out.at[above, split:], ring_out.at[above, split:], on_z(-2))
    ring = [up_one, down_one, up_two, down_two, fwd_up_one, fwd_up_two, fwd_down_one, fwd_down_two]
    for copy in sends:
        copy.wait_recv()
    own_tree.wait()

    def ring_landed():
        for copy in (up_one, down_one, fwd_up_one, fwd_up_two, fwd_down_one, fwd_down_two):
            copy.wait_recv()
        own_ring.wait()

    return sends + ring, ring_landed


def gather_kernel(rows_ref, mid_ring, mid_tree, ring_out, tree_out, send_sem, recv_sem, local_sem):
    nx, ny, nz = lax.axis_size("x"), lax.axis_size("ylo"), lax.axis_size("z")
    x, y, z = lax.axis_index("x"), lax.axis_index("ylo"), lax.axis_index("z")
    me = x * ny + y
    peers = [{"x": lax.rem(me + d, nx * ny) // ny, "ylo": lax.rem(me + d, nx * ny) % ny} for d in range(1, nx * ny)]
    peers += [{"z": lax.rem(z + nz + step, nz)} for step in (1, -1, 2, -2)]
    barrier = pltpu.get_barrier_semaphore()
    for peer in peers:
        pl.semaphore_signal(barrier, 1, device_id=peer)
    pl.semaphore_wait(barrier, len(peers))
    half = rows_ref.shape[0] // 2
    ring_src, tree_src = rows_ref.at[pl.ds(half, half)], rows_ref.at[pl.ds(0, half)]
    sends, ring_landed = phase_one(ring_src, tree_src, mid_ring, mid_tree, send_sem, recv_sem, local_sem)
    more, local = gather_phase(
        1, mid_tree, mid_ring, ring_out, tree_out, send_sem, recv_sem, local_sem, ring_landed
    )
    for copy in sends + more:
        copy.wait_send()
    for copy in local:
        copy.wait()


def gather_blk(rows, cid):
    nz = lax.axis_size("z")
    nxy = lax.axis_size("x") * lax.axis_size("ylo")
    half = rows.shape[0] // 2
    width = rows.shape[1]
    piece = (half, width)
    any_space = pl.BlockSpec(memory_space=pl.ANY)
    _, _, first, second = pl.pallas_call(
        gather_kernel,
        out_shape=(
            jax.ShapeDtypeStruct((nz, *piece), rows.dtype),
            jax.ShapeDtypeStruct((nxy, *piece), rows.dtype),
            jax.ShapeDtypeStruct((nz, nxy, *piece), rows.dtype),
            jax.ShapeDtypeStruct((nxy, nz, *piece), rows.dtype),
        ),
        in_specs=[any_space],
        out_specs=(any_space,) * 4,
        scratch_shapes=[
            pltpu.SemaphoreType.DMA((2, 12 + 4 * nz)),
            pltpu.SemaphoreType.DMA((2, 12 + 4 * nz)),
            pltpu.SemaphoreType.DMA((2, 2)),
        ],
        compiler_params=pltpu.CompilerParams(collective_id=cid, has_side_effects=True),
    )(rows)
    return first.reshape(-1, BLOCK, width), second.reshape(-1, BLOCK, width)


def reduce_kernel(src_ref, out_ref, own, landed, mid, last, send_sem, recv_sem, local_sem):
    nyhi, ncore = lax.axis_size("yhi"), lax.axis_size("core")
    yhi, core = lax.axis_index("yhi"), lax.axis_index("core")
    other_core, other_yhi = ncore - 1 - core, nyhi - 1 - yhi
    to_core, to_yhi = {"core": other_core}, {"yhi": other_yhi}
    barrier = pltpu.get_barrier_semaphore()
    for peer in (to_core, to_yhi):
        pl.semaphore_signal(barrier, 1, device_id=peer)
    pl.semaphore_wait(barrier, 2)
    rows = last.shape[0] // 2
    parts = (pl.ds(0, rows), pl.ds(rows, rows))
    copies, locals_ = [], []
    for k, part in enumerate(parts):
        for h in range(nyhi):
            copy = pltpu.make_async_remote_copy(
                src_ref=src_ref.at[h * ncore + other_core, part],
                dst_ref=landed.at[h, part],
                send_sem=send_sem.at[k, h],
                recv_sem=recv_sem.at[k, h],
                device_id=to_core,
            )
            copy.start()
            copies.append(copy)
            keep = pltpu.make_async_copy(src_ref.at[h * ncore + core, part], own.at[h, part], local_sem.at[k, h])
            keep.start()
            locals_.append(keep)
    crosses = []
    for k, part in enumerate(parts):
        for h in range(nyhi):
            copies[k * nyhi + h].wait_recv()
            locals_[k * nyhi + h].wait()
        mid[other_yhi, part] = own[other_yhi, part] + landed[other_yhi, part]
        mid[yhi, part] = own[yhi, part] + landed[yhi, part]
        cross = pltpu.make_async_remote_copy(
            src_ref=mid.at[other_yhi, part],
            dst_ref=last.at[part],
            send_sem=send_sem.at[k, nyhi],
            recv_sem=recv_sem.at[k, nyhi],
            device_id=to_yhi,
        )
        cross.start()
        crosses.append(cross)
    for k, part in enumerate(parts):
        crosses[k].wait_recv()
        out_ref[part] = mid[yhi, part] + last[part]
    for copy in copies + crosses:
        copy.wait_send()


def reduce_rep(partial, cid):
    nyhi, ncore = lax.axis_size("yhi"), lax.axis_size("core")
    pieces = partial.reshape(nyhi * ncore, -1, partial.shape[1])
    piece = pieces.shape[1:]
    return pl.pallas_call(
        reduce_kernel,
        out_shape=jax.ShapeDtypeStruct(piece, pieces.dtype),
        in_specs=[pl.BlockSpec(memory_space=pl.ANY)],
        out_specs=pl.BlockSpec(memory_space=pltpu.VMEM),
        scratch_shapes=[
            pltpu.VMEM((nyhi, *piece), pieces.dtype),
            pltpu.VMEM((nyhi, *piece), pieces.dtype),
            pltpu.VMEM((nyhi, *piece), pieces.dtype),
            pltpu.VMEM(piece, pieces.dtype),
            pltpu.SemaphoreType.DMA((2, nyhi + 1)),
            pltpu.SemaphoreType.DMA((2, nyhi + 1)),
            pltpu.SemaphoreType.DMA((2, nyhi)),
        ],
        compiler_params=pltpu.CompilerParams(collective_id=cid, has_side_effects=True),
    )(pieces)


def staged_index(col, per_owner):
    nz = lax.axis_size("z")
    nxy = lax.axis_size("x") * lax.axis_size("ylo")
    half = per_owner // 2
    owner = col // per_owner
    sub = col % per_owner
    z = owner % nz
    xy = owner // nz
    in_first = sub < half
    first = (z * nxy + xy) * half + jnp.where(in_first, sub, 0)
    second = (xy * nz + z) * half + jnp.where(in_first, 0, sub - half)
    return in_first.astype(jnp.int32), first, second


def products_kernel(flag_ref, first_ref, second_ref, *refs):
    adj_ref, out_ref = refs[-2:]
    rows, kq = adj_ref.shape[0], adj_ref.shape[1]
    firsts, seconds = refs[: rows * kq], refs[rows * kq : 2 * rows * kq]
    base = pl.program_id(0) * rows
    for r in range(rows):
        acc = jnp.zeros(out_ref.shape[1:], jnp.float32)
        for k in range(kq):
            at = r * kq + k
            block = jnp.where(flag_ref[base + r, k] != 0, firsts[at][0], seconds[at][0])
            acc = acc + jnp.dot(adj_ref[r, k], block, preferred_element_type=jnp.float32)
        out_ref[r] = acc


def tile_products(panels, adj_tiles, index, per_piece):
    flag, first, second = index
    rows, kq = flag.shape
    width = panels[0].shape[2]
    tile = (1, BLOCK, width)

    def pick(table, r, k):
        return pl.BlockSpec(tile, lambda g, f, a, b: (table(f, a, b)[g * per_piece + r, k], 0, 0))

    specs = [pick(lambda f, a, b: a, r, k) for r in range(per_piece) for k in range(kq)]
    specs += [pick(lambda f, a, b: b, r, k) for r in range(per_piece) for k in range(kq)]
    specs.append(pl.BlockSpec((per_piece, kq, BLOCK, BLOCK), lambda g, f, a, b: (g, 0, 0, 0)))
    out_spec = pl.BlockSpec((per_piece, BLOCK, width), lambda g, f, a, b: (g, 0, 0))
    summed = pl.pallas_call(
        products_kernel,
        out_shape=jax.ShapeDtypeStruct((rows, BLOCK, width), jnp.float32),
        grid_spec=pltpu.PrefetchScalarGridSpec(
            num_scalar_prefetch=3,
            grid=(rows // per_piece,),
            in_specs=specs,
            out_specs=out_spec,
        ),
    )(flag, first, second, *([panels[0]] * (per_piece * kq)), *([panels[1]] * (per_piece * kq)), adj_tiles[:, 0])
    return summed.reshape(-1, width)


def local(node_feats, adj_tiles, col_index, w_in, b_in, w_out, b_out, cot_out):
    per_piece = node_feats.shape[0] // BLOCK
    index = staged_index(col_index[:, 0, :], per_piece)
    panels = gather_blk(node_feats, 0)
    partial_sum = tile_products(panels, adj_tiles, index, 2 * per_piece)
    agg = reduce_rep(partial_sum, 8)
    agg_b = agg.astype(jnp.bfloat16)
    pre = jnp.dot(agg_b, w_in, preferred_element_type=jnp.float32) + b_in
    hidden = jax.nn.silu(pre).astype(jnp.bfloat16)
    projected = jnp.dot(hidden, w_out, preferred_element_type=jnp.float32) + b_out
    out_feats = (node_feats.astype(jnp.float32) + projected).astype(jnp.bfloat16)
    g_hidden = jnp.einsum("nh,fh->nf", cot_out, w_out, preferred_element_type=jnp.float32)
    sigma = jax.nn.sigmoid(pre)
    g_pre = (g_hidden * sigma * (1.0 + pre * (1.0 - sigma))).astype(jnp.bfloat16)
    g_agg = jnp.einsum("nf,hf->nh", g_pre, w_in, preferred_element_type=jnp.float32).astype(
        jnp.bfloat16
    )
    g_panels = gather_blk(g_agg, 1)
    back_partial = tile_products(g_panels, adj_tiles, index, 2 * per_piece)
    back_rows = reduce_rep(back_partial, 9)
    grad_feats = (cot_out.astype(jnp.float32) + back_rows).astype(jnp.bfloat16)
    return (out_feats, grad_feats)


def solution(mesh):
    nblk = mesh.shape["blk"]
    nrep = mesh.shape["rep"]
    fine = Mesh(mesh.devices.reshape(nblk // 16, 2, 8, nrep // 2, 2), NAMES)
    rows = P(BLK + REP, None)
    placed = (
        rows,
        P(BLK, REP, None, None, None),
        P(BLK, REP, None),
        P(),
        P(),
        P(),
        P(),
        rows,
    )
    return jax.shard_map(
        local,
        mesh=fine,
        in_specs=placed,
        out_specs=(rows, rows),
        check_vma=False,
    )
```

```python
import functools

import jax
import jax.numpy as jnp
from jax import lax
from jax.experimental import pallas as pl
from jax.experimental.pallas import tpu as pltpu
from jax.sharding import Mesh
from jax.sharding import PartitionSpec as P

BLOCK = 128
NAMES = ("x", "ylo", "z", "yhi", "core")
BLK = ("x", "ylo", "z")
REP = ("yhi", "core")


def group_place(axes):
    sizes = [lax.axis_size(a) for a in axes]
    me = 0
    for a, n in zip(axes, sizes):
        me = me * n + lax.axis_index(a)
    return me, sizes


def peer_id(axes, sizes, p):
    coords = {}
    for a, n in reversed(list(zip(axes, sizes))):
        coords[a] = p % n
        p = p // n
    return coords


def neighbours():
    nx, ny, nz = lax.axis_size("x"), lax.axis_size("ylo"), lax.axis_size("z")
    x, y, z = lax.axis_index("x"), lax.axis_index("ylo"), lax.axis_index("z")
    right, left, other = lax.rem(x + 1, nx), lax.rem(x + nx - 1, nx), ny - 1 - y
    return {"x": right}, {"x": left}, {"ylo": other}, {"z": lax.rem(z + 1, nz)}, {"z": lax.rem(z + nz - 1, nz)}


def gather_phase(phase, ring_src, tree_src, ring_out, tree_out, send_sem, recv_sem, local_sem, ready):
    nx, ny, nz = lax.axis_size("x"), lax.axis_size("ylo"), lax.axis_size("z")
    x, y, z = lax.axis_index("x"), lax.axis_index("ylo"), lax.axis_index("z")
    right, left, other = lax.rem(x + 1, nx), lax.rem(x + nx - 1, nx), ny - 1 - y
    to_right, to_left, to_other, up, down = neighbours()

    def send(kind, src, dst, peer):
        copy = pltpu.make_async_remote_copy(
            src_ref=src,
            dst_ref=dst,
            send_sem=send_sem.at[phase, kind],
            recv_sem=recv_sem.at[phase, kind],
            device_id=peer,
        )
        copy.start()
        return copy

    me = x * ny + y
    own_ring = pltpu.make_async_copy(ring_src, ring_out.at[z], local_sem.at[phase, 1])
    own_ring.start()
    steps = nz // 2
    half = ring_src.shape[0] // 2
    chunks = (pl.ds(0, half), pl.ds(half, half))
    ups = [[send(9 + c, ring_src.at[part], ring_out.at[z, part], up)] for c, part in enumerate(chunks)]
    downs = [
        [send(9 + 4 * steps + c, ring_src.at[part], ring_out.at[z, part], down)]
        for c, part in enumerate(chunks)
    ]

    ready()
    own_tree = pltpu.make_async_copy(tree_src, tree_out.at[me], local_sem.at[phase, 0])
    own_tree.start()
    quarter = tree_src.shape[0] // 4
    p_all, p_lo, p_hi = pl.ds(0, 2 * quarter), pl.ds(0, quarter), pl.ds(quarter, quarter)
    q_all, q_lo, q_hi = pl.ds(2 * quarter, 2 * quarter), pl.ds(2 * quarter, quarter), pl.ds(3 * quarter, quarter)
    extra = 9 + 4 * nz
    first_right = send(0, tree_src.at[p_all], tree_out.at[me, p_all], to_right)
    first_left = send(1, tree_src.at[p_all], tree_out.at[me, p_all], to_left)
    first_other = send(2, tree_src.at[p_all], tree_out.at[me, p_all], to_other)
    q_right = send(extra, tree_src.at[q_all], tree_out.at[me, q_all], to_right)
    q_left = send(extra + 1, tree_src.at[q_all], tree_out.at[me, q_all], to_left)
    q_own = send(extra + 2, tree_src.at[q_all], tree_out.at[me, q_all], to_other)

    def ring_step(s):
        below = lax.rem(z + nz - (s - 1), nz)
        above = lax.rem(z + s - 1, nz)
        for c, part in enumerate(chunks):
            ups[c][-1].wait_recv()
            if s < steps or c == 0:
                ups[c].append(send(9 + 2 * (s - 1) + c, ring_out.at[below, part], ring_out.at[below, part], up))
            downs[c][-1].wait_recv()
            if s < steps or c == 1:
                downs[c].append(
                    send(9 + 4 * steps + 2 * (s - 1) + c, ring_out.at[above, part], ring_out.at[above, part], down)
                )

    first_right.wait_recv()
    from_left = left * ny + y
    second_right = send(3, tree_out.at[from_left, p_lo], tree_out.at[from_left, p_lo], to_right)
    q_right.wait_recv()
    q_second_right = send(extra + 3, tree_out.at[from_left, q_lo], tree_out.at[from_left, q_lo], to_right)
    q_from_left = send(extra + 4, tree_out.at[from_left, q_all], tree_out.at[from_left, q_all], to_other)
    first_left.wait_recv()
    from_right = right * ny + y
    second_left = send(7, tree_out.at[from_right, p_hi], tree_out.at[from_right, p_hi], to_left)
    q_left.wait_recv()
    q_second_left = send(extra + 5, tree_out.at[from_right, q_hi], tree_out.at[from_right, q_hi], to_left)
    q_from_right = send(extra + 6, tree_out.at[from_right, q_all], tree_out.at[from_right, q_all], to_other)
    ring_step(2)
    first_other.wait_recv()
    from_other = x * ny + other
    other_right = send(4, tree_out.at[from_other, p_all], tree_out.at[from_other, p_all], to_right)
    other_left = send(5, tree_out.at[from_other, p_all], tree_out.at[from_other, p_all], to_left)
    ring_step(3)
    other_right.wait_recv()
    from_left_other = left * ny + other
    third_right = send(6, tree_out.at[from_left_other, p_lo], tree_out.at[from_left_other, p_lo], to_right)
    other_left.wait_recv()
    from_right_other = right * ny + other
    third_left = send(8, tree_out.at[from_right_other, p_hi], tree_out.at[from_right_other, p_hi], to_left)
    q_second_right.wait_recv()
    q_second_left.wait_recv()
    from_far = lax.rem(x + 2, nx) * ny + y
    q_from_far = send(extra + 7, tree_out.at[from_far, q_all], tree_out.at[from_far, q_all], to_other)
    for s in range(4, steps + 1):
        ring_step(s)
    for copy in (second_right, second_left, third_right, third_left, ups[0][-1], downs[1][-1]):
        copy.wait_recv()
    for copy in (q_own, q_from_left, q_from_right, q_from_far):
        copy.wait_recv()
    tree = [first_right, first_left, first_other, second_right, second_left]
    tree += [other_right, other_left, third_right, third_left]
    tree += [q_right, q_left, q_own, q_second_right, q_from_left, q_second_left, q_from_right, q_from_far]
    return tree + ups[0] + ups[1] + downs[0] + downs[1], [own_tree, own_ring]


def phase_one(ring_src, tree_src, ring_out, tree_out, send_sem, recv_sem, local_sem):
    nx, ny, nz = lax.axis_size("x"), lax.axis_size("ylo"), lax.axis_size("z")
    x, y, z = lax.axis_index("x"), lax.axis_index("ylo"), lax.axis_index("z")

    def send(kind, src, dst, peer):
        copy = pltpu.make_async_remote_copy(
            src_ref=src, dst_ref=dst, send_sem=send_sem.at[0, kind], recv_sem=recv_sem.at[0, kind], device_id=peer
        )
        copy.start()
        return copy

    def on_z(step):
        return {"z": lax.rem(z + nz + step, nz)}

    me = x * ny + y
    own_tree = pltpu.make_async_copy(tree_src, tree_out.at[me], local_sem.at[0, 0])
    own_tree.start()
    own_ring = pltpu.make_async_copy(ring_src, ring_out.at[z], local_sem.at[0, 1])
    own_ring.start()
    n = nx * ny
    sends = []
    for d in range(1, n):
        p = lax.rem(me + d, n)
        sends.append(send(d - 1, tree_src, tree_out.at[me], {"x": p // ny, "ylo": p % ny}))
    kind = n - 1
    up_one = send(kind, ring_src, ring_out.at[z], on_z(1))
    down_one = send(kind + 1, ring_src, ring_out.at[z], on_z(-1))
    up_two = send(kind + 2, ring_src, ring_out.at[z], on_z(2))
    down_two = send(kind + 3, ring_src, ring_out.at[z], on_z(-2))
    split = ring_src.shape[0] // 2
    up_two.wait_recv()
    below = lax.rem(z + nz - 2, nz)
    fwd_up_one = send(kind + 4, ring_out.at[below], ring_out.at[below], on_z(1))
    fwd_up_two = send(kind + 5, ring_out.at[below, :split], ring_out.at[below, :split], on_z(2))
    down_two.wait_recv()
    above = lax.rem(z + 2, nz)
    fwd_down_one = send(kind + 6, ring_out.at[above], ring_out.at[above], on_z(-1))
    fwd_down_two = send(kind + 7, ring_out.at[above, split:], ring_out.at[above, split:], on_z(-2))
    ring = [up_one, down_one, up_two, down_two, fwd_up_one, fwd_up_two, fwd_down_one, fwd_down_two]
    for copy in sends:
        copy.wait_recv()
    own_tree.wait()

    def ring_landed():
        for copy in (up_one, down_one, fwd_up_one, fwd_up_two, fwd_down_one, fwd_down_two):
            copy.wait_recv()
        own_ring.wait()

    return sends + ring, ring_landed


def gather_kernel(rows_ref, mid_ring, mid_tree, ring_out, tree_out, send_sem, recv_sem, local_sem):
    nx, ny, nz = lax.axis_size("x"), lax.axis_size("ylo"), lax.axis_size("z")
    x, y, z = lax.axis_index("x"), lax.axis_index("ylo"), lax.axis_index("z")
    me = x * ny + y
    peers = [{"x": lax.rem(me + d, nx * ny) // ny, "ylo": lax.rem(me + d, nx * ny) % ny} for d in range(1, nx * ny)]
    peers += [{"z": lax.rem(z + nz + step, nz)} for step in (1, -1, 2, -2)]
    barrier = pltpu.get_barrier_semaphore()
    for peer in peers:
        pl.semaphore_signal(barrier, 1, device_id=peer)
    pl.semaphore_wait(barrier, len(peers))
    half = rows_ref.shape[0] // 2
    ring_src, tree_src = rows_ref.at[pl.ds(half, half)], rows_ref.at[pl.ds(0, half)]
    sends, ring_landed = phase_one(ring_src, tree_src, mid_ring, mid_tree, send_sem, recv_sem, local_sem)
    more, local = gather_phase(
        1, mid_tree, mid_ring, ring_out, tree_out, send_sem, recv_sem, local_sem, ring_landed
    )
    for copy in sends + more:
        copy.wait_send()
    for copy in local:
        copy.wait()


def gather_blk(rows, cid):
    nz = lax.axis_size("z")
    nxy = lax.axis_size("x") * lax.axis_size("ylo")
    half = rows.shape[0] // 2
    width = rows.shape[1]
    piece = (half, width)
    any_space = pl.BlockSpec(memory_space=pl.ANY)
    _, _, first, second = pl.pallas_call(
        gather_kernel,
        out_shape=(
            jax.ShapeDtypeStruct((nz, *piece), rows.dtype),
            jax.ShapeDtypeStruct((nxy, *piece), rows.dtype),
            jax.ShapeDtypeStruct((nz, nxy, *piece), rows.dtype),
            jax.ShapeDtypeStruct((nxy, nz, *piece), rows.dtype),
        ),
        in_specs=[any_space],
        out_specs=(any_space,) * 4,
        scratch_shapes=[
            pltpu.SemaphoreType.DMA((2, 17 + 4 * nz)),
            pltpu.SemaphoreType.DMA((2, 17 + 4 * nz)),
            pltpu.SemaphoreType.DMA((2, 2)),
        ],
        compiler_params=pltpu.CompilerParams(collective_id=cid, has_side_effects=True),
    )(rows)
    return first.reshape(-1, BLOCK, width), second.reshape(-1, BLOCK, width)


def reduce_kernel(src_ref, out_ref, own, landed, mid, last, send_sem, recv_sem, local_sem):
    nyhi, ncore = lax.axis_size("yhi"), lax.axis_size("core")
    yhi, core = lax.axis_index("yhi"), lax.axis_index("core")
    other_core, other_yhi = ncore - 1 - core, nyhi - 1 - yhi
    to_core, to_yhi = {"core": other_core}, {"yhi": other_yhi}
    barrier = pltpu.get_barrier_semaphore()
    for peer in (to_core, to_yhi):
        pl.semaphore_signal(barrier, 1, device_id=peer)
    pl.semaphore_wait(barrier, 2)
    rows = last.shape[0] // 2
    parts = (pl.ds(0, rows), pl.ds(rows, rows))
    copies, locals_ = [], []
    for k, part in enumerate(parts):
        for h in range(nyhi):
            copy = pltpu.make_async_remote_copy(
                src_ref=src_ref.at[h * ncore + other_core, part],
                dst_ref=landed.at[h, part],
                send_sem=send_sem.at[k, h],
                recv_sem=recv_sem.at[k, h],
                device_id=to_core,
            )
            copy.start()
            copies.append(copy)
            keep = pltpu.make_async_copy(src_ref.at[h * ncore + core, part], own.at[h, part], local_sem.at[k, h])
            keep.start()
            locals_.append(keep)
    crosses = []
    for k, part in enumerate(parts):
        for h in range(nyhi):
            copies[k * nyhi + h].wait_recv()
            locals_[k * nyhi + h].wait()
        mid[other_yhi, part] = own[other_yhi, part] + landed[other_yhi, part]
        mid[yhi, part] = own[yhi, part] + landed[yhi, part]
        cross = pltpu.make_async_remote_copy(
            src_ref=mid.at[other_yhi, part],
            dst_ref=last.at[part],
            send_sem=send_sem.at[k, nyhi],
            recv_sem=recv_sem.at[k, nyhi],
            device_id=to_yhi,
        )
        cross.start()
        crosses.append(cross)
    for k, part in enumerate(parts):
        crosses[k].wait_recv()
        out_ref[part] = mid[yhi, part] + last[part]
    for copy in copies + crosses:
        copy.wait_send()


def reduce_rep(partial, cid):
    nyhi, ncore = lax.axis_size("yhi"), lax.axis_size("core")
    pieces = partial.reshape(nyhi * ncore, -1, partial.shape[1])
    piece = pieces.shape[1:]
    return pl.pallas_call(
        reduce_kernel,
        out_shape=jax.ShapeDtypeStruct(piece, pieces.dtype),
        in_specs=[pl.BlockSpec(memory_space=pl.ANY)],
        out_specs=pl.BlockSpec(memory_space=pltpu.VMEM),
        scratch_shapes=[
            pltpu.VMEM((nyhi, *piece), pieces.dtype),
            pltpu.VMEM((nyhi, *piece), pieces.dtype),
            pltpu.VMEM((nyhi, *piece), pieces.dtype),
            pltpu.VMEM(piece, pieces.dtype),
            pltpu.SemaphoreType.DMA((2, nyhi + 1)),
            pltpu.SemaphoreType.DMA((2, nyhi + 1)),
            pltpu.SemaphoreType.DMA((2, nyhi)),
        ],
        compiler_params=pltpu.CompilerParams(collective_id=cid, has_side_effects=True),
    )(pieces)


def staged_index(col, per_owner):
    nz = lax.axis_size("z")
    nxy = lax.axis_size("x") * lax.axis_size("ylo")
    half = per_owner // 2
    owner = col // per_owner
    sub = col % per_owner
    z = owner % nz
    xy = owner // nz
    in_first = sub < half
    first = (z * nxy + xy) * half + jnp.where(in_first, sub, 0)
    second = (xy * nz + z) * half + jnp.where(in_first, 0, sub - half)
    return in_first.astype(jnp.int32), first, second


def products_kernel(flag_ref, first_ref, second_ref, *refs):
    adj_ref, out_ref = refs[-2:]
    rows, kq = adj_ref.shape[0], adj_ref.shape[1]
    firsts, seconds = refs[: rows * kq], refs[rows * kq : 2 * rows * kq]
    base = pl.program_id(0) * rows
    for r in range(rows):
        acc = jnp.zeros(out_ref.shape[1:], jnp.float32)
        for k in range(kq):
            at = r * kq + k
            block = jnp.where(flag_ref[base + r, k] != 0, firsts[at][0], seconds[at][0])
            acc = acc + jnp.dot(adj_ref[r, k], block, preferred_element_type=jnp.float32)
        out_ref[r] = acc


def tile_products(panels, adj_tiles, index, per_piece):
    flag, first, second = index
    rows, kq = flag.shape
    width = panels[0].shape[2]
    tile = (1, BLOCK, width)

    def pick(table, r, k):
        return pl.BlockSpec(tile, lambda g, f, a, b: (table(f, a, b)[g * per_piece + r, k], 0, 0))

    specs = [pick(lambda f, a, b: a, r, k) for r in range(per_piece) for k in range(kq)]
    specs += [pick(lambda f, a, b: b, r, k) for r in range(per_piece) for k in range(kq)]
    specs.append(pl.BlockSpec((per_piece, kq, BLOCK, BLOCK), lambda g, f, a, b: (g, 0, 0, 0)))
    out_spec = pl.BlockSpec((per_piece, BLOCK, width), lambda g, f, a, b: (g, 0, 0))
    summed = pl.pallas_call(
        products_kernel,
        out_shape=jax.ShapeDtypeStruct((rows, BLOCK, width), jnp.float32),
        grid_spec=pltpu.PrefetchScalarGridSpec(
            num_scalar_prefetch=3,
            grid=(rows // per_piece,),
            in_specs=specs,
            out_specs=out_spec,
        ),
    )(flag, first, second, *([panels[0]] * (per_piece * kq)), *([panels[1]] * (per_piece * kq)), adj_tiles[:, 0])
    return summed.reshape(-1, width)


def local(node_feats, adj_tiles, col_index, w_in, b_in, w_out, b_out, cot_out):
    per_piece = node_feats.shape[0] // BLOCK
    index = staged_index(col_index[:, 0, :], per_piece)
    panels = gather_blk(node_feats, 0)
    partial_sum = tile_products(panels, adj_tiles, index, 2 * per_piece)
    agg = reduce_rep(partial_sum, 8)
    agg_b = agg.astype(jnp.bfloat16)
    pre = jnp.dot(agg_b, w_in, preferred_element_type=jnp.float32) + b_in
    hidden = jax.nn.silu(pre).astype(jnp.bfloat16)
    projected = jnp.dot(hidden, w_out, preferred_element_type=jnp.float32) + b_out
    out_feats = (node_feats.astype(jnp.float32) + projected).astype(jnp.bfloat16)
    g_hidden = jnp.einsum("nh,fh->nf", cot_out, w_out, preferred_element_type=jnp.float32)
    sigma = jax.nn.sigmoid(pre)
    g_pre = (g_hidden * sigma * (1.0 + pre * (1.0 - sigma))).astype(jnp.bfloat16)
    g_agg = jnp.einsum("nf,hf->nh", g_pre, w_in, preferred_element_type=jnp.float32).astype(
        jnp.bfloat16
    )
    g_panels = gather_blk(g_agg, 1)
    back_partial = tile_products(g_panels, adj_tiles, index, 2 * per_piece)
    back_rows = reduce_rep(back_partial, 9)
    grad_feats = (cot_out.astype(jnp.float32) + back_rows).astype(jnp.bfloat16)
    return (out_feats, grad_feats)


def solution(mesh):
    nblk = mesh.shape["blk"]
    nrep = mesh.shape["rep"]
    fine = Mesh(mesh.devices.reshape(nblk // 16, 2, 8, nrep // 2, 2), NAMES)
    rows = P(BLK + REP, None)
    placed = (
        rows,
        P(BLK, REP, None, None, None),
        P(BLK, REP, None),
        P(),
        P(),
        P(),
        P(),
        rows,
    )
    return jax.shard_map(
        local,
        mesh=fine,
        in_specs=placed,
        out_specs=(rows, rows),
        check_vma=False,
    )
```

```python
import functools

import jax
import jax.numpy as jnp
from jax import lax
from jax.experimental import pallas as pl
from jax.experimental.pallas import tpu as pltpu
from jax.sharding import Mesh
from jax.sharding import PartitionSpec as P

BLOCK = 128
NAMES = ("x", "ylo", "z", "yhi", "core")
BLK = ("x", "ylo", "z")
REP = ("yhi", "core")


def group_place(axes):
    sizes = [lax.axis_size(a) for a in axes]
    me = 0
    for a, n in zip(axes, sizes):
        me = me * n + lax.axis_index(a)
    return me, sizes


def peer_id(axes, sizes, p):
    coords = {}
    for a, n in reversed(list(zip(axes, sizes))):
        coords[a] = p % n
        p = p // n
    return coords


def neighbours():
    nx, ny, nz = lax.axis_size("x"), lax.axis_size("ylo"), lax.axis_size("z")
    x, y, z = lax.axis_index("x"), lax.axis_index("ylo"), lax.axis_index("z")
    right, left, other = lax.rem(x + 1, nx), lax.rem(x + nx - 1, nx), ny - 1 - y
    return {"x": right}, {"x": left}, {"ylo": other}, {"z": lax.rem(z + 1, nz)}, {"z": lax.rem(z + nz - 1, nz)}


def gather_phase(phase, ring_src, tree_src, ring_out, tree_out, send_sem, recv_sem, local_sem, ready):
    nx, ny, nz = lax.axis_size("x"), lax.axis_size("ylo"), lax.axis_size("z")
    x, y, z = lax.axis_index("x"), lax.axis_index("ylo"), lax.axis_index("z")
    right, left, other = lax.rem(x + 1, nx), lax.rem(x + nx - 1, nx), ny - 1 - y
    to_right, to_left, to_other, up, down = neighbours()

    def send(kind, src, dst, peer):
        copy = pltpu.make_async_remote_copy(
            src_ref=src,
            dst_ref=dst,
            send_sem=send_sem.at[phase, kind],
            recv_sem=recv_sem.at[phase, kind],
            device_id=peer,
        )
        copy.start()
        return copy

    me = x * ny + y
    own_ring = pltpu.make_async_copy(ring_src, ring_out.at[z], local_sem.at[phase, 1])
    own_ring.start()
    steps = nz // 2
    half = ring_src.shape[0] // 2
    chunks = (pl.ds(0, half), pl.ds(half, half))
    ups = [[send(9 + c, ring_src.at[part], ring_out.at[z, part], up)] for c, part in enumerate(chunks)]
    downs = [
        [send(9 + 4 * steps + c, ring_src.at[part], ring_out.at[z, part], down)]
        for c, part in enumerate(chunks)
    ]

    ready()
    own_tree = pltpu.make_async_copy(tree_src, tree_out.at[me], local_sem.at[phase, 0])
    own_tree.start()
    first_right = send(0, tree_src, tree_out.at[me], to_right)
    first_left = send(1, tree_src, tree_out.at[me], to_left)
    first_other = send(2, tree_src, tree_out.at[me], to_other)

    def ring_step(s):
        below = lax.rem(z + nz - (s - 1), nz)
        above = lax.rem(z + s - 1, nz)
        for c, part in enumerate(chunks):
            ups[c][-1].wait_recv()
            if s < steps or c == 0:
                ups[c].append(send(9 + 2 * (s - 1) + c, ring_out.at[below, part], ring_out.at[below, part], up))
            downs[c][-1].wait_recv()
            if s < steps or c == 1:
                downs[c].append(
                    send(9 + 4 * steps + 2 * (s - 1) + c, ring_out.at[above, part], ring_out.at[above, part], down)
                )

    tree_split = tree_src.shape[0] // 2
    first_right.wait_recv()
    from_left = left * ny + y
    second_right = send(3, tree_out.at[from_left, :tree_split], tree_out.at[from_left, :tree_split], to_right)
    first_left.wait_recv()
    from_right = right * ny + y
    second_left = send(7, tree_out.at[from_right, tree_split:], tree_out.at[from_right, tree_split:], to_left)
    ring_step(2)
    first_other.wait_recv()
    from_other = x * ny + other
    other_right = send(4, tree_out.at[from_other], tree_out.at[from_other], to_right)
    other_left = send(5, tree_out.at[from_other], tree_out.at[from_other], to_left)
    ring_step(3)
    other_right.wait_recv()
    from_left_other = left * ny + other
    third_right = send(
        6, tree_out.at[from_left_other, :tree_split], tree_out.at[from_left_other, :tree_split], to_right
    )
    other_left.wait_recv()
    from_right_other = right * ny + other
    third_left = send(
        8, tree_out.at[from_right_other, tree_split:], tree_out.at[from_right_other, tree_split:], to_left
    )
    for s in range(4, steps + 1):
        ring_step(s)
    for copy in (second_right, second_left, third_right, third_left, ups[0][-1], downs[1][-1]):
        copy.wait_recv()
    tree = [first_right, first_left, first_other, second_right, second_left]
    tree += [other_right, other_left, third_right, third_left]
    return tree + ups[0] + ups[1] + downs[0] + downs[1], [own_tree, own_ring]


def phase_one(ring_src, tree_src, ring_out, tree_out, send_sem, recv_sem, local_sem):
    nx, ny, nz = lax.axis_size("x"), lax.axis_size("ylo"), lax.axis_size("z")
    x, y, z = lax.axis_index("x"), lax.axis_index("ylo"), lax.axis_index("z")

    def send(kind, src, dst, peer):
        copy = pltpu.make_async_remote_copy(
            src_ref=src, dst_ref=dst, send_sem=send_sem.at[0, kind], recv_sem=recv_sem.at[0, kind], device_id=peer
        )
        copy.start()
        return copy

    def on_z(step):
        return {"z": lax.rem(z + nz + step, nz)}

    me = x * ny + y
    own_tree = pltpu.make_async_copy(tree_src, tree_out.at[me], local_sem.at[0, 0])
    own_tree.start()
    own_ring = pltpu.make_async_copy(ring_src, ring_out.at[z], local_sem.at[0, 1])
    own_ring.start()
    n = nx * ny
    kind = n - 1
    up_two = send(kind + 2, ring_src, ring_out.at[z], on_z(2))
    down_two = send(kind + 3, ring_src, ring_out.at[z], on_z(-2))
    up_one = send(kind, ring_src, ring_out.at[z], on_z(1))
    down_one = send(kind + 1, ring_src, ring_out.at[z], on_z(-1))
    sends = []
    for d in range(1, n):
        p = lax.rem(me + d, n)
        sends.append(send(d - 1, tree_src, tree_out.at[me], {"x": p // ny, "ylo": p % ny}))
    split = ring_src.shape[0] // 2
    up_two.wait_recv()
    below = lax.rem(z + nz - 2, nz)
    fwd_up_one = send(kind + 4, ring_out.at[below], ring_out.at[below], on_z(1))
    fwd_up_two = send(kind + 5, ring_out.at[below, :split], ring_out.at[below, :split], on_z(2))
    down_two.wait_recv()
    above = lax.rem(z + 2, nz)
    fwd_down_one = send(kind + 6, ring_out.at[above], ring_out.at[above], on_z(-1))
    fwd_down_two = send(kind + 7, ring_out.at[above, split:], ring_out.at[above, split:], on_z(-2))
    ring = [up_one, down_one, up_two, down_two, fwd_up_one, fwd_up_two, fwd_down_one, fwd_down_two]
    for copy in sends:
        copy.wait_recv()
    own_tree.wait()

    def ring_landed():
        for copy in (up_one, down_one, fwd_up_one, fwd_up_two, fwd_down_one, fwd_down_two):
            copy.wait_recv()
        own_ring.wait()

    return sends + ring, ring_landed


def gather_kernel(rows_ref, mid_ring, mid_tree, ring_out, tree_out, send_sem, recv_sem, local_sem):
    nx, ny, nz = lax.axis_size("x"), lax.axis_size("ylo"), lax.axis_size("z")
    x, y, z = lax.axis_index("x"), lax.axis_index("ylo"), lax.axis_index("z")
    me = x * ny + y
    peers = [{"x": lax.rem(me + d, nx * ny) // ny, "ylo": lax.rem(me + d, nx * ny) % ny} for d in range(1, nx * ny)]
    peers += [{"z": lax.rem(z + nz + step, nz)} for step in (1, -1, 2, -2)]
    barrier = pltpu.get_barrier_semaphore()
    for peer in peers:
        pl.semaphore_signal(barrier, 1, device_id=peer)
    pl.semaphore_wait(barrier, len(peers))
    half = rows_ref.shape[0] // 2
    ring_src, tree_src = rows_ref.at[pl.ds(half, half)], rows_ref.at[pl.ds(0, half)]
    sends, ring_landed = phase_one(ring_src, tree_src, mid_ring, mid_tree, send_sem, recv_sem, local_sem)
    more, local = gather_phase(
        1, mid_tree, mid_ring, ring_out, tree_out, send_sem, recv_sem, local_sem, ring_landed
    )
    for copy in sends + more:
        copy.wait_send()
    for copy in local:
        copy.wait()


def gather_blk(rows, cid):
    nz = lax.axis_size("z")
    nxy = lax.axis_size("x") * lax.axis_size("ylo")
    half = rows.shape[0] // 2
    width = rows.shape[1]
    piece = (half, width)
    any_space = pl.BlockSpec(memory_space=pl.ANY)
    _, _, first, second = pl.pallas_call(
        gather_kernel,
        out_shape=(
            jax.ShapeDtypeStruct((nz, *piece), rows.dtype),
            jax.ShapeDtypeStruct((nxy, *piece), rows.dtype),
            jax.ShapeDtypeStruct((nz, nxy, *piece), rows.dtype),
            jax.ShapeDtypeStruct((nxy, nz, *piece), rows.dtype),
        ),
        in_specs=[any_space],
        out_specs=(any_space,) * 4,
        scratch_shapes=[
            pltpu.SemaphoreType.DMA((2, 9 + 4 * nz)),
            pltpu.SemaphoreType.DMA((2, 9 + 4 * nz)),
            pltpu.SemaphoreType.DMA((2, 2)),
        ],
        compiler_params=pltpu.CompilerParams(collective_id=cid, has_side_effects=True),
    )(rows)
    return first.reshape(-1, BLOCK, width), second.reshape(-1, BLOCK, width)


def reduce_kernel(src_ref, out_ref, own, landed, mid, last, send_sem, recv_sem, local_sem):
    nyhi, ncore = lax.axis_size("yhi"), lax.axis_size("core")
    yhi, core = lax.axis_index("yhi"), lax.axis_index("core")
    other_core, other_yhi = ncore - 1 - core, nyhi - 1 - yhi
    to_core, to_yhi = {"core": other_core}, {"yhi": other_yhi}
    barrier = pltpu.get_barrier_semaphore()
    for peer in (to_core, to_yhi):
        pl.semaphore_signal(barrier, 1, device_id=peer)
    pl.semaphore_wait(barrier, 2)
    rows = last.shape[0] // 2
    parts = (pl.ds(0, rows), pl.ds(rows, rows))
    copies, locals_ = [], []
    for k, part in enumerate(parts):
        for h in range(nyhi):
            copy = pltpu.make_async_remote_copy(
                src_ref=src_ref.at[h * ncore + other_core, part],
                dst_ref=landed.at[h, part],
                send_sem=send_sem.at[k, h],
                recv_sem=recv_sem.at[k, h],
                device_id=to_core,
            )
            copy.start()
            copies.append(copy)
            keep = pltpu.make_async_copy(src_ref.at[h * ncore + core, part], own.at[h, part], local_sem.at[k, h])
            keep.start()
            locals_.append(keep)
    crosses = []
    for k, part in enumerate(parts):
        for h in range(nyhi):
            copies[k * nyhi + h].wait_recv()
            locals_[k * nyhi + h].wait()
        mid[other_yhi, part] = own[other_yhi, part] + landed[other_yhi, part]
        mid[yhi, part] = own[yhi, part] + landed[yhi, part]
        cross = pltpu.make_async_remote_copy(
            src_ref=mid.at[other_yhi, part],
            dst_ref=last.at[part],
            send_sem=send_sem.at[k, nyhi],
            recv_sem=recv_sem.at[k, nyhi],
            device_id=to_yhi,
        )
        cross.start()
        crosses.append(cross)
    for k, part in enumerate(parts):
        crosses[k].wait_recv()
        out_ref[part] = mid[yhi, part] + last[part]
    for copy in copies + crosses:
        copy.wait_send()


def reduce_rep(partial, cid):
    nyhi, ncore = lax.axis_size("yhi"), lax.axis_size("core")
    pieces = partial.reshape(nyhi * ncore, -1, partial.shape[1])
    piece = pieces.shape[1:]
    return pl.pallas_call(
        reduce_kernel,
        out_shape=jax.ShapeDtypeStruct(piece, pieces.dtype),
        in_specs=[pl.BlockSpec(memory_space=pl.ANY)],
        out_specs=pl.BlockSpec(memory_space=pltpu.VMEM),
        scratch_shapes=[
            pltpu.VMEM((nyhi, *piece), pieces.dtype),
            pltpu.VMEM((nyhi, *piece), pieces.dtype),
            pltpu.VMEM((nyhi, *piece), pieces.dtype),
            pltpu.VMEM(piece, pieces.dtype),
            pltpu.SemaphoreType.DMA((2, nyhi + 1)),
            pltpu.SemaphoreType.DMA((2, nyhi + 1)),
            pltpu.SemaphoreType.DMA((2, nyhi)),
        ],
        compiler_params=pltpu.CompilerParams(collective_id=cid, has_side_effects=True),
    )(pieces)


def staged_index(col, per_owner):
    nz = lax.axis_size("z")
    nxy = lax.axis_size("x") * lax.axis_size("ylo")
    half = per_owner // 2
    owner = col // per_owner
    sub = col % per_owner
    z = owner % nz
    xy = owner // nz
    in_first = sub < half
    first = (z * nxy + xy) * half + jnp.where(in_first, sub, 0)
    second = (xy * nz + z) * half + jnp.where(in_first, 0, sub - half)
    return in_first.astype(jnp.int32), first, second


def products_kernel(flag_ref, first_ref, second_ref, *refs):
    adj_ref, out_ref = refs[-2:]
    rows, kq = adj_ref.shape[0], adj_ref.shape[1]
    firsts, seconds = refs[: rows * kq], refs[rows * kq : 2 * rows * kq]
    base = pl.program_id(0) * rows
    for r in range(rows):
        acc = jnp.zeros(out_ref.shape[1:], jnp.float32)
        for k in range(kq):
            at = r * kq + k
            block = jnp.where(flag_ref[base + r, k] != 0, firsts[at][0], seconds[at][0])
            acc = acc + jnp.dot(adj_ref[r, k], block, preferred_element_type=jnp.float32)
        out_ref[r] = acc


def tile_products(panels, adj_tiles, index, per_piece):
    flag, first, second = index
    rows, kq = flag.shape
    width = panels[0].shape[2]
    tile = (1, BLOCK, width)

    def pick(table, r, k):
        return pl.BlockSpec(tile, lambda g, f, a, b: (table(f, a, b)[g * per_piece + r, k], 0, 0))

    specs = [pick(lambda f, a, b: a, r, k) for r in range(per_piece) for k in range(kq)]
    specs += [pick(lambda f, a, b: b, r, k) for r in range(per_piece) for k in range(kq)]
    specs.append(pl.BlockSpec((per_piece, kq, BLOCK, BLOCK), lambda g, f, a, b: (g, 0, 0, 0)))
    out_spec = pl.BlockSpec((per_piece, BLOCK, width), lambda g, f, a, b: (g, 0, 0))
    summed = pl.pallas_call(
        products_kernel,
        out_shape=jax.ShapeDtypeStruct((rows, BLOCK, width), jnp.float32),
        grid_spec=pltpu.PrefetchScalarGridSpec(
            num_scalar_prefetch=3,
            grid=(rows // per_piece,),
            in_specs=specs,
            out_specs=out_spec,
        ),
    )(flag, first, second, *([panels[0]] * (per_piece * kq)), *([panels[1]] * (per_piece * kq)), adj_tiles[:, 0])
    return summed.reshape(-1, width)


def local(node_feats, adj_tiles, col_index, w_in, b_in, w_out, b_out, cot_out):
    per_piece = node_feats.shape[0] // BLOCK
    index = staged_index(col_index[:, 0, :], per_piece)
    panels = gather_blk(node_feats, 0)
    partial_sum = tile_products(panels, adj_tiles, index, 2 * per_piece)
    agg = reduce_rep(partial_sum, 8)
    agg_b = agg.astype(jnp.bfloat16)
    pre = jnp.dot(agg_b, w_in, preferred_element_type=jnp.float32) + b_in
    hidden = jax.nn.silu(pre).astype(jnp.bfloat16)
    projected = jnp.dot(hidden, w_out, preferred_element_type=jnp.float32) + b_out
    out_feats = (node_feats.astype(jnp.float32) + projected).astype(jnp.bfloat16)
    g_hidden = jnp.einsum("nh,fh->nf", cot_out, w_out, preferred_element_type=jnp.float32)
    sigma = jax.nn.sigmoid(pre)
    g_pre = (g_hidden * sigma * (1.0 + pre * (1.0 - sigma))).astype(jnp.bfloat16)
    g_agg = jnp.einsum("nf,hf->nh", g_pre, w_in, preferred_element_type=jnp.float32).astype(
        jnp.bfloat16
    )
    g_panels = gather_blk(g_agg, 1)
    back_partial = tile_products(g_panels, adj_tiles, index, 2 * per_piece)
    back_rows = reduce_rep(back_partial, 9)
    grad_feats = (cot_out.astype(jnp.float32) + back_rows).astype(jnp.bfloat16)
    return (out_feats, grad_feats)


def solution(mesh):
    nblk = mesh.shape["blk"]
    nrep = mesh.shape["rep"]
    fine = Mesh(mesh.devices.reshape(nblk // 16, 2, 8, nrep // 2, 2), NAMES)
    rows = P(BLK + REP, None)
    placed = (
        rows,
        P(BLK, REP, None, None, None),
        P(BLK, REP, None),
        P(),
        P(),
        P(),
        P(),
        rows,
    )
    return jax.shard_map(
        local,
        mesh=fine,
        in_specs=placed,
        out_specs=(rows, rows),
        check_vma=False,
    )
```

```python
import functools

import jax
import jax.numpy as jnp
from jax import lax
from jax.experimental import pallas as pl
from jax.experimental.pallas import tpu as pltpu
from jax.sharding import Mesh
from jax.sharding import PartitionSpec as P

BLOCK = 128
NAMES = ("x", "ylo", "z", "yhi", "core")
BLK = ("x", "ylo", "z")
REP = ("yhi", "core")


def group_place(axes):
    sizes = [lax.axis_size(a) for a in axes]
    me = 0
    for a, n in zip(axes, sizes):
        me = me * n + lax.axis_index(a)
    return me, sizes


def peer_id(axes, sizes, p):
    coords = {}
    for a, n in reversed(list(zip(axes, sizes))):
        coords[a] = p % n
        p = p // n
    return coords


def neighbours():
    nx, ny, nz = lax.axis_size("x"), lax.axis_size("ylo"), lax.axis_size("z")
    x, y, z = lax.axis_index("x"), lax.axis_index("ylo"), lax.axis_index("z")
    right, left, other = lax.rem(x + 1, nx), lax.rem(x + nx - 1, nx), ny - 1 - y
    return {"x": right}, {"x": left}, {"ylo": other}, {"z": lax.rem(z + 1, nz)}, {"z": lax.rem(z + nz - 1, nz)}


def gather_phase(phase, ring_src, tree_src, ring_out, tree_out, send_sem, recv_sem, local_sem, ready):
    nx, ny, nz = lax.axis_size("x"), lax.axis_size("ylo"), lax.axis_size("z")
    x, y, z = lax.axis_index("x"), lax.axis_index("ylo"), lax.axis_index("z")
    right, left, other = lax.rem(x + 1, nx), lax.rem(x + nx - 1, nx), ny - 1 - y
    to_right, to_left, to_other, up, down = neighbours()

    def send(kind, src, dst, peer):
        copy = pltpu.make_async_remote_copy(
            src_ref=src,
            dst_ref=dst,
            send_sem=send_sem.at[phase, kind],
            recv_sem=recv_sem.at[phase, kind],
            device_id=peer,
        )
        copy.start()
        return copy

    me = x * ny + y
    own_ring = pltpu.make_async_copy(ring_src, ring_out.at[z], local_sem.at[phase, 1])
    own_ring.start()
    steps = nz // 2
    half = ring_src.shape[0] // 2
    chunks = (pl.ds(0, half), pl.ds(half, half))
    ups = [[send(9 + c, ring_src.at[part], ring_out.at[z, part], up)] for c, part in enumerate(chunks)]
    downs = [
        [send(9 + 4 * steps + c, ring_src.at[part], ring_out.at[z, part], down)]
        for c, part in enumerate(chunks)
    ]

    ready()
    own_tree = pltpu.make_async_copy(tree_src, tree_out.at[me], local_sem.at[phase, 0])
    own_tree.start()
    first_right = send(0, tree_src, tree_out.at[me], to_right)
    first_left = send(1, tree_src, tree_out.at[me], to_left)
    first_other = send(2, tree_src, tree_out.at[me], to_other)

    def ring_step(s):
        below = lax.rem(z + nz - (s - 1), nz)
        above = lax.rem(z + s - 1, nz)
        for c, part in enumerate(chunks):
            ups[c][-1].wait_recv()
            if s < steps or c == 0:
                ups[c].append(send(9 + 2 * (s - 1) + c, ring_out.at[below, part], ring_out.at[below, part], up))
            downs[c][-1].wait_recv()
            if s < steps or c == 1:
                downs[c].append(
                    send(9 + 4 * steps + 2 * (s - 1) + c, ring_out.at[above, part], ring_out.at[above, part], down)
                )

    tree_split = tree_src.shape[0] // 2
    ring_step(2)
    first_right.wait_recv()
    from_left = left * ny + y
    second_right = send(3, tree_out.at[from_left, :tree_split], tree_out.at[from_left, :tree_split], to_right)
    first_left.wait_recv()
    from_right = right * ny + y
    second_left = send(7, tree_out.at[from_right, tree_split:], tree_out.at[from_right, tree_split:], to_left)
    first_other.wait_recv()
    from_other = x * ny + other
    other_right = send(4, tree_out.at[from_other], tree_out.at[from_other], to_right)
    other_left = send(5, tree_out.at[from_other], tree_out.at[from_other], to_left)
    ring_step(3)
    other_right.wait_recv()
    from_left_other = left * ny + other
    third_right = send(
        6, tree_out.at[from_left_other, :tree_split], tree_out.at[from_left_other, :tree_split], to_right
    )
    other_left.wait_recv()
    from_right_other = right * ny + other
    third_left = send(
        8, tree_out.at[from_right_other, tree_split:], tree_out.at[from_right_other, tree_split:], to_left
    )
    for s in range(4, steps + 1):
        ring_step(s)
    for copy in (second_right, second_left, third_right, third_left, ups[0][-1], downs[1][-1]):
        copy.wait_recv()
    tree = [first_right, first_left, first_other, second_right, second_left]
    tree += [other_right, other_left, third_right, third_left]
    return tree + ups[0] + ups[1] + downs[0] + downs[1], [own_tree, own_ring]


def phase_one(ring_src, tree_src, ring_out, tree_out, send_sem, recv_sem, local_sem):
    nx, ny, nz = lax.axis_size("x"), lax.axis_size("ylo"), lax.axis_size("z")
    x, y, z = lax.axis_index("x"), lax.axis_index("ylo"), lax.axis_index("z")

    def send(kind, src, dst, peer):
        copy = pltpu.make_async_remote_copy(
            src_ref=src, dst_ref=dst, send_sem=send_sem.at[0, kind], recv_sem=recv_sem.at[0, kind], device_id=peer
        )
        copy.start()
        return copy

    def on_z(step):
        return {"z": lax.rem(z + nz + step, nz)}

    me = x * ny + y
    own_tree = pltpu.make_async_copy(tree_src, tree_out.at[me], local_sem.at[0, 0])
    own_tree.start()
    own_ring = pltpu.make_async_copy(ring_src, ring_out.at[z], local_sem.at[0, 1])
    own_ring.start()
    n = nx * ny
    kind = n - 1
    up_two = send(kind + 2, ring_src, ring_out.at[z], on_z(2))
    down_two = send(kind + 3, ring_src, ring_out.at[z], on_z(-2))
    up_one = send(kind, ring_src, ring_out.at[z], on_z(1))
    down_one = send(kind + 1, ring_src, ring_out.at[z], on_z(-1))
    sends = []
    for d in range(1, n):
        p = lax.rem(me + d, n)
        sends.append(send(d - 1, tree_src, tree_out.at[me], {"x": p // ny, "ylo": p % ny}))
    split = ring_src.shape[0] // 2
    up_two.wait_recv()
    below = lax.rem(z + nz - 2, nz)
    fwd_up_one = send(kind + 4, ring_out.at[below], ring_out.at[below], on_z(1))
    fwd_up_two = send(kind + 5, ring_out.at[below, :split], ring_out.at[below, :split], on_z(2))
    down_two.wait_recv()
    above = lax.rem(z + 2, nz)
    fwd_down_one = send(kind + 6, ring_out.at[above], ring_out.at[above], on_z(-1))
    fwd_down_two = send(kind + 7, ring_out.at[above, split:], ring_out.at[above, split:], on_z(-2))
    ring = [up_one, down_one, up_two, down_two, fwd_up_one, fwd_up_two, fwd_down_one, fwd_down_two]
    for copy in sends:
        copy.wait_recv()
    own_tree.wait()

    def ring_landed():
        for copy in (up_one, down_one, fwd_up_one, fwd_up_two, fwd_down_one, fwd_down_two):
            copy.wait_recv()
        own_ring.wait()

    return sends + ring, ring_landed


def gather_kernel(rows_ref, mid_ring, mid_tree, ring_out, tree_out, send_sem, recv_sem, local_sem):
    nx, ny, nz = lax.axis_size("x"), lax.axis_size("ylo"), lax.axis_size("z")
    x, y, z = lax.axis_index("x"), lax.axis_index("ylo"), lax.axis_index("z")
    me = x * ny + y
    peers = [{"x": lax.rem(me + d, nx * ny) // ny, "ylo": lax.rem(me + d, nx * ny) % ny} for d in range(1, nx * ny)]
    peers += [{"z": lax.rem(z + nz + step, nz)} for step in (1, -1, 2, -2)]
    barrier = pltpu.get_barrier_semaphore()
    for peer in peers:
        pl.semaphore_signal(barrier, 1, device_id=peer)
    pl.semaphore_wait(barrier, len(peers))
    half = rows_ref.shape[0] // 2
    ring_src, tree_src = rows_ref.at[pl.ds(half, half)], rows_ref.at[pl.ds(0, half)]
    sends, ring_landed = phase_one(ring_src, tree_src, mid_ring, mid_tree, send_sem, recv_sem, local_sem)
    more, local = gather_phase(
        1, mid_tree, mid_ring, ring_out, tree_out, send_sem, recv_sem, local_sem, ring_landed
    )
    for copy in sends + more:
        copy.wait_send()
    for copy in local:
        copy.wait()


def gather_blk(rows, cid):
    nz = lax.axis_size("z")
    nxy = lax.axis_size("x") * lax.axis_size("ylo")
    half = rows.shape[0] // 2
    width = rows.shape[1]
    piece = (half, width)
    any_space = pl.BlockSpec(memory_space=pl.ANY)
    _, _, first, second = pl.pallas_call(
        gather_kernel,
        out_shape=(
            jax.ShapeDtypeStruct((nz, *piece), rows.dtype),
            jax.ShapeDtypeStruct((nxy, *piece), rows.dtype),
            jax.ShapeDtypeStruct((nz, nxy, *piece), rows.dtype),
            jax.ShapeDtypeStruct((nxy, nz, *piece), rows.dtype),
        ),
        in_specs=[any_space],
        out_specs=(any_space,) * 4,
        scratch_shapes=[
            pltpu.SemaphoreType.DMA((2, 9 + 4 * nz)),
            pltpu.SemaphoreType.DMA((2, 9 + 4 * nz)),
            pltpu.SemaphoreType.DMA((2, 2)),
        ],
        compiler_params=pltpu.CompilerParams(collective_id=cid, has_side_effects=True),
    )(rows)
    return first.reshape(-1, BLOCK, width), second.reshape(-1, BLOCK, width)


def reduce_kernel(src_ref, out_ref, own, landed, mid, last, send_sem, recv_sem, local_sem):
    nyhi, ncore = lax.axis_size("yhi"), lax.axis_size("core")
    yhi, core = lax.axis_index("yhi"), lax.axis_index("core")
    other_core, other_yhi = ncore - 1 - core, nyhi - 1 - yhi
    to_core, to_yhi = {"core": other_core}, {"yhi": other_yhi}
    barrier = pltpu.get_barrier_semaphore()
    for peer in (to_core, to_yhi):
        pl.semaphore_signal(barrier, 1, device_id=peer)
    pl.semaphore_wait(barrier, 2)
    rows = last.shape[0] // 2
    parts = (pl.ds(0, rows), pl.ds(rows, rows))
    copies, locals_ = [], []
    for k, part in enumerate(parts):
        for h in range(nyhi):
            copy = pltpu.make_async_remote_copy(
                src_ref=src_ref.at[h * ncore + other_core, part],
                dst_ref=landed.at[h, part],
                send_sem=send_sem.at[k, h],
                recv_sem=recv_sem.at[k, h],
                device_id=to_core,
            )
            copy.start()
            copies.append(copy)
            keep = pltpu.make_async_copy(src_ref.at[h * ncore + core, part], own.at[h, part], local_sem.at[k, h])
            keep.start()
            locals_.append(keep)
    crosses = []
    for k, part in enumerate(parts):
        for h in range(nyhi):
            copies[k * nyhi + h].wait_recv()
            locals_[k * nyhi + h].wait()
        mid[other_yhi, part] = own[other_yhi, part] + landed[other_yhi, part]
        mid[yhi, part] = own[yhi, part] + landed[yhi, part]
        cross = pltpu.make_async_remote_copy(
            src_ref=mid.at[other_yhi, part],
            dst_ref=last.at[part],
            send_sem=send_sem.at[k, nyhi],
            recv_sem=recv_sem.at[k, nyhi],
            device_id=to_yhi,
        )
        cross.start()
        crosses.append(cross)
    for k, part in enumerate(parts):
        crosses[k].wait_recv()
        out_ref[part] = mid[yhi, part] + last[part]
    for copy in copies + crosses:
        copy.wait_send()


def reduce_rep(partial, cid):
    nyhi, ncore = lax.axis_size("yhi"), lax.axis_size("core")
    pieces = partial.reshape(nyhi * ncore, -1, partial.shape[1])
    piece = pieces.shape[1:]
    return pl.pallas_call(
        reduce_kernel,
        out_shape=jax.ShapeDtypeStruct(piece, pieces.dtype),
        in_specs=[pl.BlockSpec(memory_space=pl.ANY)],
        out_specs=pl.BlockSpec(memory_space=pltpu.VMEM),
        scratch_shapes=[
            pltpu.VMEM((nyhi, *piece), pieces.dtype),
            pltpu.VMEM((nyhi, *piece), pieces.dtype),
            pltpu.VMEM((nyhi, *piece), pieces.dtype),
            pltpu.VMEM(piece, pieces.dtype),
            pltpu.SemaphoreType.DMA((2, nyhi + 1)),
            pltpu.SemaphoreType.DMA((2, nyhi + 1)),
            pltpu.SemaphoreType.DMA((2, nyhi)),
        ],
        compiler_params=pltpu.CompilerParams(collective_id=cid, has_side_effects=True),
    )(pieces)


def staged_index(col, per_owner):
    nz = lax.axis_size("z")
    nxy = lax.axis_size("x") * lax.axis_size("ylo")
    half = per_owner // 2
    owner = col // per_owner
    sub = col % per_owner
    z = owner % nz
    xy = owner // nz
    in_first = sub < half
    first = (z * nxy + xy) * half + jnp.where(in_first, sub, 0)
    second = (xy * nz + z) * half + jnp.where(in_first, 0, sub - half)
    return in_first.astype(jnp.int32), first, second


def products_kernel(flag_ref, first_ref, second_ref, *refs):
    adj_ref, out_ref = refs[-2:]
    rows, kq = adj_ref.shape[0], adj_ref.shape[1]
    firsts, seconds = refs[: rows * kq], refs[rows * kq : 2 * rows * kq]
    base = pl.program_id(0) * rows
    for r in range(rows):
        acc = jnp.zeros(out_ref.shape[1:], jnp.float32)
        for k in range(kq):
            at = r * kq + k
            block = jnp.where(flag_ref[base + r, k] != 0, firsts[at][0], seconds[at][0])
            acc = acc + jnp.dot(adj_ref[r, k], block, preferred_element_type=jnp.float32)
        out_ref[r] = acc


def tile_products(panels, adj_tiles, index, per_piece):
    flag, first, second = index
    rows, kq = flag.shape
    width = panels[0].shape[2]
    tile = (1, BLOCK, width)

    def pick(table, r, k):
        return pl.BlockSpec(tile, lambda g, f, a, b: (table(f, a, b)[g * per_piece + r, k], 0, 0))

    specs = [pick(lambda f, a, b: a, r, k) for r in range(per_piece) for k in range(kq)]
    specs += [pick(lambda f, a, b: b, r, k) for r in range(per_piece) for k in range(kq)]
    specs.append(pl.BlockSpec((per_piece, kq, BLOCK, BLOCK), lambda g, f, a, b: (g, 0, 0, 0)))
    out_spec = pl.BlockSpec((per_piece, BLOCK, width), lambda g, f, a, b: (g, 0, 0))
    summed = pl.pallas_call(
        products_kernel,
        out_shape=jax.ShapeDtypeStruct((rows, BLOCK, width), jnp.float32),
        grid_spec=pltpu.PrefetchScalarGridSpec(
            num_scalar_prefetch=3,
            grid=(rows // per_piece,),
            in_specs=specs,
            out_specs=out_spec,
        ),
    )(flag, first, second, *([panels[0]] * (per_piece * kq)), *([panels[1]] * (per_piece * kq)), adj_tiles[:, 0])
    return summed.reshape(-1, width)


def local(node_feats, adj_tiles, col_index, w_in, b_in, w_out, b_out, cot_out):
    per_piece = node_feats.shape[0] // BLOCK
    index = staged_index(col_index[:, 0, :], per_piece)
    panels = gather_blk(node_feats, 0)
    partial_sum = tile_products(panels, adj_tiles, index, 2 * per_piece)
    agg = reduce_rep(partial_sum, 8)
    agg_b = agg.astype(jnp.bfloat16)
    pre = jnp.dot(agg_b, w_in, preferred_element_type=jnp.float32) + b_in
    hidden = jax.nn.silu(pre).astype(jnp.bfloat16)
    projected = jnp.dot(hidden, w_out, preferred_element_type=jnp.float32) + b_out
    out_feats = (node_feats.astype(jnp.float32) + projected).astype(jnp.bfloat16)
    g_hidden = jnp.einsum("nh,fh->nf", cot_out, w_out, preferred_element_type=jnp.float32)
    sigma = jax.nn.sigmoid(pre)
    g_pre = (g_hidden * sigma * (1.0 + pre * (1.0 - sigma))).astype(jnp.bfloat16)
    g_agg = jnp.einsum("nf,hf->nh", g_pre, w_in, preferred_element_type=jnp.float32).astype(
        jnp.bfloat16
    )
    g_panels = gather_blk(g_agg, 1)
    back_partial = tile_products(g_panels, adj_tiles, index, 2 * per_piece)
    back_rows = reduce_rep(back_partial, 9)
    grad_feats = (cot_out.astype(jnp.float32) + back_rows).astype(jnp.bfloat16)
    return (out_feats, grad_feats)


def solution(mesh):
    nblk = mesh.shape["blk"]
    nrep = mesh.shape["rep"]
    fine = Mesh(mesh.devices.reshape(nblk // 16, 2, 8, nrep // 2, 2), NAMES)
    rows = P(BLK + REP, None)
    placed = (
        rows,
        P(BLK, REP, None, None, None),
        P(BLK, REP, None),
        P(),
        P(),
        P(),
        P(),
        rows,
    )
    return jax.shard_map(
        local,
        mesh=fine,
        in_specs=placed,
        out_specs=(rows, rows),
        check_vma=False,
    )
```

```python
import functools

import jax
import jax.numpy as jnp
from jax import lax
from jax.experimental import pallas as pl
from jax.experimental.pallas import tpu as pltpu
from jax.sharding import Mesh
from jax.sharding import PartitionSpec as P

BLOCK = 128
NAMES = ("x", "ylo", "z", "yhi", "core")
BLK = ("x", "ylo", "z")
REP = ("yhi", "core")


def group_place(axes):
    sizes = [lax.axis_size(a) for a in axes]
    me = 0
    for a, n in zip(axes, sizes):
        me = me * n + lax.axis_index(a)
    return me, sizes


def peer_id(axes, sizes, p):
    coords = {}
    for a, n in reversed(list(zip(axes, sizes))):
        coords[a] = p % n
        p = p // n
    return coords


def neighbours():
    nx, ny, nz = lax.axis_size("x"), lax.axis_size("ylo"), lax.axis_size("z")
    x, y, z = lax.axis_index("x"), lax.axis_index("ylo"), lax.axis_index("z")
    right, left, other = lax.rem(x + 1, nx), lax.rem(x + nx - 1, nx), ny - 1 - y
    return {"x": right}, {"x": left}, {"ylo": other}, {"z": lax.rem(z + 1, nz)}, {"z": lax.rem(z + nz - 1, nz)}


def gather_phase(phase, ring_src, tree_src, ring_out, tree_out, send_sem, recv_sem, local_sem, ready):
    nx, ny, nz = lax.axis_size("x"), lax.axis_size("ylo"), lax.axis_size("z")
    x, y, z = lax.axis_index("x"), lax.axis_index("ylo"), lax.axis_index("z")
    right, left, other = lax.rem(x + 1, nx), lax.rem(x + nx - 1, nx), ny - 1 - y
    to_right, to_left, to_other, up, down = neighbours()

    def send(kind, src, dst, peer):
        copy = pltpu.make_async_remote_copy(
            src_ref=src,
            dst_ref=dst,
            send_sem=send_sem.at[phase, kind],
            recv_sem=recv_sem.at[phase, kind],
            device_id=peer,
        )
        copy.start()
        return copy

    me = x * ny + y
    own_ring = pltpu.make_async_copy(ring_src, ring_out.at[z], local_sem.at[phase, 1])
    own_ring.start()
    steps = nz // 2
    half = ring_src.shape[0] // 2
    chunks = (pl.ds(0, half), pl.ds(half, half))
    ups = [[send(9 + c, ring_src.at[part], ring_out.at[z, part], up)] for c, part in enumerate(chunks)]
    downs = [
        [send(9 + 4 * steps + c, ring_src.at[part], ring_out.at[z, part], down)]
        for c, part in enumerate(chunks)
    ]

    ready()
    own_tree = pltpu.make_async_copy(tree_src, tree_out.at[me], local_sem.at[phase, 0])
    own_tree.start()
    first_right = send(0, tree_src, tree_out.at[me], to_right)
    first_left = send(1, tree_src, tree_out.at[me], to_left)
    first_other = send(2, tree_src, tree_out.at[me], to_other)

    def ring_step(s):
        below = lax.rem(z + nz - (s - 1), nz)
        above = lax.rem(z + s - 1, nz)
        for c, part in enumerate(chunks):
            ups[c][-1].wait_recv()
            if s < steps or c == 0:
                ups[c].append(send(9 + 2 * (s - 1) + c, ring_out.at[below, part], ring_out.at[below, part], up))
            downs[c][-1].wait_recv()
            if s < steps or c == 1:
                downs[c].append(
                    send(9 + 4 * steps + 2 * (s - 1) + c, ring_out.at[above, part], ring_out.at[above, part], down)
                )

    tree_split = tree_src.shape[0] // 2
    ring_step(2)
    first_right.wait_recv()
    from_left = left * ny + y
    second_right = send(3, tree_out.at[from_left, :tree_split], tree_out.at[from_left, :tree_split], to_right)
    first_left.wait_recv()
    from_right = right * ny + y
    second_left = send(7, tree_out.at[from_right, tree_split:], tree_out.at[from_right, tree_split:], to_left)
    ring_step(3)
    first_other.wait_recv()
    from_other = x * ny + other
    other_right = send(4, tree_out.at[from_other], tree_out.at[from_other], to_right)
    other_left = send(5, tree_out.at[from_other], tree_out.at[from_other], to_left)
    other_right.wait_recv()
    from_left_other = left * ny + other
    third_right = send(
        6, tree_out.at[from_left_other, :tree_split], tree_out.at[from_left_other, :tree_split], to_right
    )
    other_left.wait_recv()
    from_right_other = right * ny + other
    third_left = send(
        8, tree_out.at[from_right_other, tree_split:], tree_out.at[from_right_other, tree_split:], to_left
    )
    for s in range(4, steps + 1):
        ring_step(s)
    for copy in (second_right, second_left, third_right, third_left, ups[0][-1], downs[1][-1]):
        copy.wait_recv()
    tree = [first_right, first_left, first_other, second_right, second_left]
    tree += [other_right, other_left, third_right, third_left]
    return tree + ups[0] + ups[1] + downs[0] + downs[1], [own_tree, own_ring]


def phase_one(ring_src, tree_src, ring_out, tree_out, send_sem, recv_sem, local_sem):
    nx, ny, nz = lax.axis_size("x"), lax.axis_size("ylo"), lax.axis_size("z")
    x, y, z = lax.axis_index("x"), lax.axis_index("ylo"), lax.axis_index("z")

    def send(kind, src, dst, peer):
        copy = pltpu.make_async_remote_copy(
            src_ref=src, dst_ref=dst, send_sem=send_sem.at[0, kind], recv_sem=recv_sem.at[0, kind], device_id=peer
        )
        copy.start()
        return copy

    def on_z(step):
        return {"z": lax.rem(z + nz + step, nz)}

    me = x * ny + y
    own_tree = pltpu.make_async_copy(tree_src, tree_out.at[me], local_sem.at[0, 0])
    own_tree.start()
    own_ring = pltpu.make_async_copy(ring_src, ring_out.at[z], local_sem.at[0, 1])
    own_ring.start()
    n = nx * ny
    kind = n - 1
    up_two = send(kind + 2, ring_src, ring_out.at[z], on_z(2))
    down_two = send(kind + 3, ring_src, ring_out.at[z], on_z(-2))
    up_one = send(kind, ring_src, ring_out.at[z], on_z(1))
    down_one = send(kind + 1, ring_src, ring_out.at[z], on_z(-1))
    sends = []
    for d in range(1, n):
        p = lax.rem(me + d, n)
        sends.append(send(d - 1, tree_src, tree_out.at[me], {"x": p // ny, "ylo": p % ny}))
    split = ring_src.shape[0] // 2
    up_two.wait_recv()
    below = lax.rem(z + nz - 2, nz)
    fwd_up_one = send(kind + 4, ring_out.at[below], ring_out.at[below], on_z(1))
    fwd_up_two = send(kind + 5, ring_out.at[below, :split], ring_out.at[below, :split], on_z(2))
    down_two.wait_recv()
    above = lax.rem(z + 2, nz)
    fwd_down_one = send(kind + 6, ring_out.at[above], ring_out.at[above], on_z(-1))
    fwd_down_two = send(kind + 7, ring_out.at[above, split:], ring_out.at[above, split:], on_z(-2))
    ring = [up_one, down_one, up_two, down_two, fwd_up_one, fwd_up_two, fwd_down_one, fwd_down_two]
    for copy in sends:
        copy.wait_recv()
    own_tree.wait()

    def ring_landed():
        for copy in (up_one, down_one, fwd_up_one, fwd_up_two, fwd_down_one, fwd_down_two):
            copy.wait_recv()
        own_ring.wait()

    return sends + ring, ring_landed


def gather_kernel(rows_ref, mid_ring, mid_tree, ring_out, tree_out, send_sem, recv_sem, local_sem):
    nx, ny, nz = lax.axis_size("x"), lax.axis_size("ylo"), lax.axis_size("z")
    x, y, z = lax.axis_index("x"), lax.axis_index("ylo"), lax.axis_index("z")
    me = x * ny + y
    peers = [{"x": lax.rem(me + d, nx * ny) // ny, "ylo": lax.rem(me + d, nx * ny) % ny} for d in range(1, nx * ny)]
    peers += [{"z": lax.rem(z + nz + step, nz)} for step in (1, -1, 2, -2)]
    barrier = pltpu.get_barrier_semaphore()
    for peer in peers:
        pl.semaphore_signal(barrier, 1, device_id=peer)
    pl.semaphore_wait(barrier, len(peers))
    half = rows_ref.shape[0] // 2
    ring_src, tree_src = rows_ref.at[pl.ds(half, half)], rows_ref.at[pl.ds(0, half)]
    sends, ring_landed = phase_one(ring_src, tree_src, mid_ring, mid_tree, send_sem, recv_sem, local_sem)
    more, local = gather_phase(
        1, mid_tree, mid_ring, ring_out, tree_out, send_sem, recv_sem, local_sem, ring_landed
    )
    for copy in sends + more:
        copy.wait_send()
    for copy in local:
        copy.wait()


def gather_blk(rows, cid):
    nz = lax.axis_size("z")
    nxy = lax.axis_size("x") * lax.axis_size("ylo")
    half = rows.shape[0] // 2
    width = rows.shape[1]
    piece = (half, width)
    any_space = pl.BlockSpec(memory_space=pl.ANY)
    _, _, first, second = pl.pallas_call(
        gather_kernel,
        out_shape=(
            jax.ShapeDtypeStruct((nz, *piece), rows.dtype),
            jax.ShapeDtypeStruct((nxy, *piece), rows.dtype),
            jax.ShapeDtypeStruct((nz, nxy, *piece), rows.dtype),
            jax.ShapeDtypeStruct((nxy, nz, *piece), rows.dtype),
        ),
        in_specs=[any_space],
        out_specs=(any_space,) * 4,
        scratch_shapes=[
            pltpu.SemaphoreType.DMA((2, 9 + 4 * nz)),
            pltpu.SemaphoreType.DMA((2, 9 + 4 * nz)),
            pltpu.SemaphoreType.DMA((2, 2)),
        ],
        compiler_params=pltpu.CompilerParams(collective_id=cid, has_side_effects=True),
    )(rows)
    return first.reshape(-1, BLOCK, width), second.reshape(-1, BLOCK, width)


def reduce_kernel(src_ref, out_ref, own, landed, mid, last, send_sem, recv_sem, local_sem):
    nyhi, ncore = lax.axis_size("yhi"), lax.axis_size("core")
    yhi, core = lax.axis_index("yhi"), lax.axis_index("core")
    other_core, other_yhi = ncore - 1 - core, nyhi - 1 - yhi
    to_core, to_yhi = {"core": other_core}, {"yhi": other_yhi}
    barrier = pltpu.get_barrier_semaphore()
    for peer in (to_core, to_yhi):
        pl.semaphore_signal(barrier, 1, device_id=peer)
    pl.semaphore_wait(barrier, 2)
    rows = last.shape[0] // 2
    parts = (pl.ds(0, rows), pl.ds(rows, rows))
    copies, locals_ = [], []
    for k, part in enumerate(parts):
        for h in range(nyhi):
            copy = pltpu.make_async_remote_copy(
                src_ref=src_ref.at[h * ncore + other_core, part],
                dst_ref=landed.at[h, part],
                send_sem=send_sem.at[k, h],
                recv_sem=recv_sem.at[k, h],
                device_id=to_core,
            )
            copy.start()
            copies.append(copy)
            keep = pltpu.make_async_copy(src_ref.at[h * ncore + core, part], own.at[h, part], local_sem.at[k, h])
            keep.start()
            locals_.append(keep)
    crosses = []
    for k, part in enumerate(parts):
        for h in range(nyhi):
            copies[k * nyhi + h].wait_recv()
            locals_[k * nyhi + h].wait()
        mid[other_yhi, part] = own[other_yhi, part] + landed[other_yhi, part]
        mid[yhi, part] = own[yhi, part] + landed[yhi, part]
        cross = pltpu.make_async_remote_copy(
            src_ref=mid.at[other_yhi, part],
            dst_ref=last.at[part],
            send_sem=send_sem.at[k, nyhi],
            recv_sem=recv_sem.at[k, nyhi],
            device_id=to_yhi,
        )
        cross.start()
        crosses.append(cross)
    for k, part in enumerate(parts):
        crosses[k].wait_recv()
        out_ref[part] = mid[yhi, part] + last[part]
    for copy in copies + crosses:
        copy.wait_send()


def reduce_rep(partial, cid):
    nyhi, ncore = lax.axis_size("yhi"), lax.axis_size("core")
    pieces = partial.reshape(nyhi * ncore, -1, partial.shape[1])
    piece = pieces.shape[1:]
    return pl.pallas_call(
        reduce_kernel,
        out_shape=jax.ShapeDtypeStruct(piece, pieces.dtype),
        in_specs=[pl.BlockSpec(memory_space=pl.ANY)],
        out_specs=pl.BlockSpec(memory_space=pltpu.VMEM),
        scratch_shapes=[
            pltpu.VMEM((nyhi, *piece), pieces.dtype),
            pltpu.VMEM((nyhi, *piece), pieces.dtype),
            pltpu.VMEM((nyhi, *piece), pieces.dtype),
            pltpu.VMEM(piece, pieces.dtype),
            pltpu.SemaphoreType.DMA((2, nyhi + 1)),
            pltpu.SemaphoreType.DMA((2, nyhi + 1)),
            pltpu.SemaphoreType.DMA((2, nyhi)),
        ],
        compiler_params=pltpu.CompilerParams(collective_id=cid, has_side_effects=True),
    )(pieces)


def staged_index(col, per_owner):
    nz = lax.axis_size("z")
    nxy = lax.axis_size("x") * lax.axis_size("ylo")
    half = per_owner // 2
    owner = col // per_owner
    sub = col % per_owner
    z = owner % nz
    xy = owner // nz
    in_first = sub < half
    first = (z * nxy + xy) * half + jnp.where(in_first, sub, 0)
    second = (xy * nz + z) * half + jnp.where(in_first, 0, sub - half)
    return in_first.astype(jnp.int32), first, second


def products_kernel(flag_ref, first_ref, second_ref, *refs):
    adj_ref, out_ref = refs[-2:]
    rows, kq = adj_ref.shape[0], adj_ref.shape[1]
    firsts, seconds = refs[: rows * kq], refs[rows * kq : 2 * rows * kq]
    base = pl.program_id(0) * rows
    for r in range(rows):
        acc = jnp.zeros(out_ref.shape[1:], jnp.float32)
        for k in range(kq):
            at = r * kq + k
            block = jnp.where(flag_ref[base + r, k] != 0, firsts[at][0], seconds[at][0])
            acc = acc + jnp.dot(adj_ref[r, k], block, preferred_element_type=jnp.float32)
        out_ref[r] = acc


def tile_products(panels, adj_tiles, index, per_piece):
    flag, first, second = index
    rows, kq = flag.shape
    width = panels[0].shape[2]
    tile = (1, BLOCK, width)

    def pick(table, r, k):
        return pl.BlockSpec(tile, lambda g, f, a, b: (table(f, a, b)[g * per_piece + r, k], 0, 0))

    specs = [pick(lambda f, a, b: a, r, k) for r in range(per_piece) for k in range(kq)]
    specs += [pick(lambda f, a, b: b, r, k) for r in range(per_piece) for k in range(kq)]
    specs.append(pl.BlockSpec((per_piece, kq, BLOCK, BLOCK), lambda g, f, a, b: (g, 0, 0, 0)))
    out_spec = pl.BlockSpec((per_piece, BLOCK, width), lambda g, f, a, b: (g, 0, 0))
    summed = pl.pallas_call(
        products_kernel,
        out_shape=jax.ShapeDtypeStruct((rows, BLOCK, width), jnp.float32),
        grid_spec=pltpu.PrefetchScalarGridSpec(
            num_scalar_prefetch=3,
            grid=(rows // per_piece,),
            in_specs=specs,
            out_specs=out_spec,
        ),
    )(flag, first, second, *([panels[0]] * (per_piece * kq)), *([panels[1]] * (per_piece * kq)), adj_tiles[:, 0])
    return summed.reshape(-1, width)


def local(node_feats, adj_tiles, col_index, w_in, b_in, w_out, b_out, cot_out):
    per_piece = node_feats.shape[0] // BLOCK
    index = staged_index(col_index[:, 0, :], per_piece)
    panels = gather_blk(node_feats, 0)
    partial_sum = tile_products(panels, adj_tiles, index, 2 * per_piece)
    agg = reduce_rep(partial_sum, 8)
    agg_b = agg.astype(jnp.bfloat16)
    pre = jnp.dot(agg_b, w_in, preferred_element_type=jnp.float32) + b_in
    hidden = jax.nn.silu(pre).astype(jnp.bfloat16)
    projected = jnp.dot(hidden, w_out, preferred_element_type=jnp.float32) + b_out
    out_feats = (node_feats.astype(jnp.float32) + projected).astype(jnp.bfloat16)
    g_hidden = jnp.einsum("nh,fh->nf", cot_out, w_out, preferred_element_type=jnp.float32)
    sigma = jax.nn.sigmoid(pre)
    g_pre = (g_hidden * sigma * (1.0 + pre * (1.0 - sigma))).astype(jnp.bfloat16)
    g_agg = jnp.einsum("nf,hf->nh", g_pre, w_in, preferred_element_type=jnp.float32).astype(
        jnp.bfloat16
    )
    g_panels = gather_blk(g_agg, 1)
    back_partial = tile_products(g_panels, adj_tiles, index, 2 * per_piece)
    back_rows = reduce_rep(back_partial, 9)
    grad_feats = (cot_out.astype(jnp.float32) + back_rows).astype(jnp.bfloat16)
    return (out_feats, grad_feats)


def solution(mesh):
    nblk = mesh.shape["blk"]
    nrep = mesh.shape["rep"]
    fine = Mesh(mesh.devices.reshape(nblk // 16, 2, 8, nrep // 2, 2), NAMES)
    rows = P(BLK + REP, None)
    placed = (
        rows,
        P(BLK, REP, None, None, None),
        P(BLK, REP, None),
        P(),
        P(),
        P(),
        P(),
        rows,
    )
    return jax.shard_map(
        local,
        mesh=fine,
        in_specs=placed,
        out_specs=(rows, rows),
        check_vma=False,
    )
```
